32 devices in a mesh: blk: 4 (over z), batch: 8 (over y, x, core).
Axes of the slice: x: 2, y: 2, z: 4, core: 2. Of those that a mesh axis runs over, the one named last changes fastest.
Arguments:
- tokens: bfloat16 [24, 512, 768], P('batch', 'blk'), may hold values from -6 to 6
- segment_ids: int32 [24, 512], P('batch', 'blk'), may hold values from 0 to 3, never falling along the last dimension, each value on 1 to 384 neighbouring positions
- w_query: bfloat16 [768, 768], replicated, may hold values from -0.21875 to 0.21875
- b_query: float32 [768], replicated, may hold values from -3 to 3
- w_key: bfloat16 [768, 768], replicated, may hold values from -0.21875 to 0.21875
- w_value: bfloat16 [768, 768], replicated, may hold values from -0.21875 to 0.21875
- b_value: float32 [768], replicated, may hold values from -3 to 3
- w_out: bfloat16 [768, 768], replicated, may hold values from -1.25 to 1.25
- b_out: float32 [768], replicated, may hold values from -2 to 2
- gain_first: float32 [768], replicated, may hold values from 0.5 to 1.5
- shift_first: float32 [768], replicated, may hold values from -2 to 2
- w_inner: bfloat16 [768, 3072], replicated, may hold values from -0.21875 to 0.21875
- b_inner: float32 [3072], replicated, may hold values from -3 to 3
- w_outer: bfloat16 [3072, 768], replicated, may hold values from -0.109375 to 0.109375
- b_outer: float32 [768], replicated, may hold values from -2 to 2
- gain_second: float32 [768], replicated, may hold values from 0.5 to 1.5
- shift_second: float32 [768], replicated, may hold values from -2 to 2
- cotangent: bfloat16 [24, 512, 768], P('batch', 'blk'), may hold values from -6 to 6
Outputs:
- layer_out: bfloat16 [24, 512, 768], P('batch', 'blk')
- input_grad: bfloat16 [24, 512, 768], P('batch', 'blk')
- grad_w_query: float32 [768, 768], P('batch')
- grad_b_query: float32 [768], P('batch')
- grad_w_key: float32 [768, 768], P('batch')
- grad_w_value: float32 [768, 768], P('batch')
- grad_b_value: float32 [768], P('batch')
- grad_w_out: float32 [768, 768], P('batch')
- grad_b_out: float32 [768], P('batch')
- grad_gain_first: float32 [768], P('batch')
- grad_shift_first: float32 [768], P('batch')
- grad_w_inner: float32 [768, 3072], P('batch')
- grad_b_inner: float32 [3072], P('batch')
- grad_w_outer: float32 [3072, 768], P('batch')
- grad_b_outer: float32 [768], P('batch')
- grad_gain_second: float32 [768], P('batch')
- grad_shift_second: float32 [768], P('batch')
The draws below stay inside these ranges and needn't reach their ends.
Inputs may be any that keep to these rules, and one draw needn't show every extreme that they name: `segment_ids`: within each row the numbers never fall, and no fragment has more than 384 tokens; some fragment has exactly that many.
All inputs are finite; a program needn't handle non-finite values.
Results may differ from the reference program's by a relative error of at most 0.019.
Values may be sent and summed in bfloat16 or wider, within the bound.
A program may use at most 128 MiB of HBM per device.

```python
import math
import jax
import jax.numpy as jnp
import numpy as np
from jax import lax

D = 768
HEADS = 12
HEAD_DIM = 64
FF = 3072
SEQ_LEN = 512
SEQS = 24


def levels(stream_key, shape, split, low, largest):
    def one(axis_at, shards_of):
        steps = jax.random.uniform(jax.random.fold_in(jax.random.fold_in(stream_key, 6), axis_at), (shards_of,), jnp.float32, low / len(split), largest / len(split))
        return jnp.repeat(jnp.exp(steps), shape[axis_at] // shards_of).reshape((-1,) + (1,) * (len(shape) - axis_at - 1))

    loudness = one(*split[0])
    for cut in split[1:]:
        loudness = loudness * one(*cut)
    return loudness


def profile(count, total, most, skew):
    weights = [(1 << 20) // math.isqrt(standing ** skew) + 1 for standing in range(2, count + 1)]
    spare, counts = total - most - (count - 1), [1] * (count - 1)
    while spare > 0:
        candidates = [i for i in range(count - 1) if counts[i] < most]
        mass, remaining = sum([weights[i] for i in candidates]), spare
        for i in candidates:
            extra = min(most - counts[i], max(1, remaining * weights[i] // mass), spare)
            counts[i] = counts[i] + extra
            spare = spare - extra
    return np.array([most] + counts)


def uneven(stream_key, count, total, bound, skew):
    if count == 2:
        one = jax.random.randint(stream_key, (), max(1, total - bound), min(bound, total - 1) + 1)
        return jnp.stack([one, total - one])
    sizes = jnp.asarray(profile(count, total, bound, skew), jnp.int32)
    couples = (count - 1) // 2
    donor, sink = sizes[1:1 + 2 * couples:2], sizes[2:2 + 2 * couples:2]
    room = jnp.minimum(donor - 1, bound - sink)
    passed = jax.random.randint(jax.random.fold_in(stream_key, 1), (couples,), 0, 1 << 20) % (room + 1)
    sizes = sizes.at[1:1 + 2 * couples:2].set(donor - passed).at[2:2 + 2 * couples:2].set(sink + passed)
    return sizes[jax.random.permutation(jax.random.fold_in(stream_key, 2), count)]


def bell_draw(own_key, dims, scale, bound, split=(), kind=jnp.bfloat16):
    entries = jax.random.normal(own_key, dims, jnp.float32) * scale
    if len(split) > 0:
        entries = levels(own_key, dims, split, -0.22, 0.18) * entries
    return jnp.clip(entries, min=-bound, max=bound).astype(kind)


def setup_inputs(seed: int = 0) -> dict:
    arg_keys = jax.random.split(jax.random.key(seed), 19)
    return {
        "tokens": bell_draw(arg_keys[0], (SEQS, SEQ_LEN, D), 1.0, 6.0, ((0, 8), (1, 4))),
        "segment_ids": jax.vmap(lambda own: jnp.searchsorted(jnp.cumsum(uneven(own, 4, SEQ_LEN, 3 * SEQ_LEN // 4, 0)), jnp.arange(SEQ_LEN), side="right"))(jax.random.split(arg_keys[1], SEQS)).reshape((SEQS, SEQ_LEN)).astype(jnp.int32),
        "w_query": bell_draw(arg_keys[2], (D, D), D ** -0.5, 0.21875),
        "b_query": bell_draw(arg_keys[3], (D,), 0.5, 3.0, (), jnp.float32),
        "w_key": bell_draw(arg_keys[4], (D, D), D ** -0.5, 0.21875),
        "w_value": bell_draw(arg_keys[5], (D, D), D ** -0.5, 0.21875),
        "b_value": bell_draw(arg_keys[6], (D,), 0.5, 3.0, (), jnp.float32),
        "w_out": bell_draw(arg_keys[7], (D, D), (D // 32) ** -0.5, 1.25),
        "b_out": bell_draw(arg_keys[8], (D,), 0.3, 2.0, (), jnp.float32),
        "gain_first": jnp.clip(1.0 + 0.1 * jax.random.normal(arg_keys[9], (D,), jnp.float32), 0.5, 1.5),
        "shift_first": bell_draw(arg_keys[10], (D,), 0.3, 2.0, (), jnp.float32),
        "w_inner": bell_draw(arg_keys[11], (D, FF), D ** -0.5, 0.21875),
        "b_inner": bell_draw(arg_keys[12], (FF,), 0.5, 3.0, (), jnp.float32),
        "w_outer": bell_draw(arg_keys[13], (FF, D), FF ** -0.5, 0.109375),
        "b_outer": bell_draw(arg_keys[14], (D,), 0.3, 2.0, (), jnp.float32),
        "gain_second": jnp.clip(1.0 + 0.1 * jax.random.normal(arg_keys[15], (D,), jnp.float32), 0.5, 1.5),
        "shift_second": bell_draw(arg_keys[16], (D,), 0.3, 2.0, (), jnp.float32),
        "cotangent": bell_draw(arg_keys[17], (SEQS, SEQ_LEN, D), 1.0, 6.0, ((0, 8), (1, 4))),
    }


@jax.custom_vjp
def low(v):
    return lax.optimization_barrier(v.astype(jnp.bfloat16)).astype(jnp.float32)

@jax.custom_vjp
def low_back(v):
    return v

def low_keep(v):
    return (low(v), None)

def low_pass(kept, grad):
    return (grad,)

def back_keep(v):
    return (v, None)

def back_low(kept, grad):
    return (low(grad),)
low.defvjp(low_keep, low_pass)
low_back.defvjp(back_keep, back_low)
epsilon = 1e-05

def matmul(left, right):
    return jnp.einsum('gld,de->gle', left, right, precision=lax.Precision.HIGHEST)

def layer_norm(resid, gain, shift):
    center = resid - lax.optimization_barrier(jnp.mean(resid, axis=-1, keepdims=True))
    scale = lax.rsqrt(lax.optimization_barrier(jnp.mean(center * center, axis=-1, keepdims=True)) + epsilon)
    return center * scale * gain + shift

def block_forward(params, inputs, segments):
    w_query, b_query, w_key, w_value, b_value, w_out, b_out, gain_first, shift_first, w_inner, b_inner, w_outer, b_outer, gain_second, shift_second = params
    group, length, width = inputs.shape
    query = low(low_back(matmul(inputs, w_query) + b_query)).reshape(group, length, HEADS, HEAD_DIM)
    keyed = low(low_back(matmul(inputs, w_key))).reshape(group, length, HEADS, HEAD_DIM)
    valued = low(low_back(matmul(inputs, w_value) + b_value)).reshape(group, length, HEADS, HEAD_DIM)
    score = jnp.einsum('gqhd,gkhd->ghqk', query, keyed, precision=lax.Precision.HIGHEST) * 0.125
    score = low_back(score)
    same = segments[:, None, :, None] == segments[:, None, None, :]
    score = jnp.where(same, score, -1e+30)
    top = lax.optimization_barrier(jnp.max(score, axis=-1, keepdims=True))
    expo = jnp.exp(score - top)
    prob = low(expo / lax.optimization_barrier(jnp.sum(expo, axis=-1, keepdims=True)))
    attended = jnp.einsum('ghqk,gkhd->gqhd', prob, valued, precision=lax.Precision.HIGHEST)
    attended = low(low_back(attended.reshape(group, length, width)))
    branch = low_back(matmul(attended, w_out) + b_out)
    normed = layer_norm(inputs + branch, gain_first, shift_first)
    pre = low_back(matmul(low(normed), w_inner) + b_inner)
    act = low(jax.nn.gelu(pre, approximate=False))
    outer = low_back(matmul(act, w_outer) + b_outer)
    return layer_norm(normed + outer, gain_second, shift_second)

def reference(tokens, segment_ids, w_query, b_query, w_key, w_value, b_value, w_out, b_out, gain_first, shift_first, w_inner, b_inner, w_outer, b_outer, gain_second, shift_second, cotangent):
    params = tuple((p.astype(jnp.float32) for p in (w_query, b_query, w_key, w_value, b_value, w_out, b_out, gain_first, shift_first, w_inner, b_inner, w_outer, b_outer, gain_second, shift_second)))
    group = math.gcd(SEQS, 4)
    count = SEQS // group
    xs = (tokens.astype(jnp.float32).reshape(count, group, SEQ_LEN, D), segment_ids.reshape(count, group, SEQ_LEN), cotangent.astype(jnp.float32).reshape(count, group, SEQ_LEN, D))

    def step(carry, item):
        inputs, segments, cotan = item
        forward = jax.checkpoint(lambda prm, xin: block_forward(prm, xin, segments))
        result, pull = jax.vjp(forward, params, inputs)
        grad_params, grad_inputs = pull(cotan)
        carry = jax.tree.map(lambda a, b: a + b, carry, grad_params)
        return (carry, (result.astype(jnp.bfloat16), grad_inputs.astype(jnp.bfloat16)))
    start = tuple((jnp.zeros_like(p) for p in params))
    totals, (result, grad_inputs) = lax.scan(step, start, xs)
    layer_out = result.reshape(SEQS, SEQ_LEN, D)
    input_grad = grad_inputs.reshape(SEQS, SEQ_LEN, D)
    return (layer_out, input_grad, totals[0], totals[1], totals[2], totals[3], totals[4], totals[5], totals[6], totals[7], totals[8], totals[9], totals[10], totals[11], totals[12], totals[13], totals[14])
```

```python
import functools
import math

import jax
import jax.numpy as jnp
from jax import lax
from jax.experimental import pallas as pl
from jax.experimental.pallas import tpu as pltpu
from jax.sharding import PartitionSpec as P

BF = jnp.bfloat16
F32 = jnp.float32
EPS = 1e-05
D = 768
PAIRS = 6
LANES = 128
BLOCK = 128
ROW = 512
FFT = 768
FFN = 4
EARLY = 9
CHUNKS = 12
MIB = 1 << 20


def dot(a, b):
    return jnp.dot(a, b, preferred_element_type=F32)


def dot_nt(a, b):
    return lax.dot_general(a, b, (((1,), (1,)), ((), ())), preferred_element_type=F32)


def dot_tn(a, b):
    return lax.dot_general(a, b, (((0,), (0,)), ((), ())), preferred_element_type=F32)


def place():
    z = lax.axis_index("blk")
    beta = lax.axis_index("batch")
    c = lax.rem(beta, 2)
    return z, beta, c, beta - c


def at(z, beta):
    return {"blk": z, "batch": beta}


def greet(devices):
    barrier = pltpu.get_barrier_semaphore()
    for device in devices:
        pl.semaphore_signal(barrier, inc=1, device_id=device, device_id_type=pl.DeviceIdType.MESH)
    pl.semaphore_wait(barrier, len(devices))


def column_mates(z, c, base):
    mates = [at(lax.rem(z + step, 4), base + core) for step in range(1, 4) for core in range(2)]
    return mates + [at(z, base + 1 - c)]


def remote(src, dst, send_sem, recv_sem, device):
    return pltpu.make_async_remote_copy(
        src_ref=src,
        dst_ref=dst,
        send_sem=send_sem,
        recv_sem=recv_sem,
        device_id=device,
        device_id_type=pl.DeviceIdType.MESH,
    )


class Mover:
    def __init__(self, z, c, base):
        self.z, self.c, self.base, self.sent = z, c, base, []

    def send(self, src, dst, send_sem, recv_sem, to_z, to_c, when=None):
        self_target = jnp.logical_and(to_z == self.z, to_c == self.c)
        other = jnp.logical_not(self_target)
        if when is not None:
            self_target = jnp.logical_and(self_target, when)
            other = jnp.logical_and(other, when)
        out = remote(src, dst, send_sem, recv_sem, at(to_z, self.base + to_c))

        @pl.when(self_target)
        def _():
            pltpu.make_async_copy(src, dst, recv_sem).start()

        @pl.when(other)
        def _():
            out.start()

        self.sent.append((other, out))

    def finish(self):
        for other, out in self.sent:

            @pl.when(other)
            def _(out=out):
                out.wait_send()

        self.sent = []


def landed(dst, sem):
    pltpu.make_async_copy(dst, dst, sem).wait()


def exchange_body(tok, seg, cot, x, segs, cotq, d_send, d_recv, f_send, g_send, g_recv, c_send, c_recv):
    z, beta, c, base = place()
    greet(column_mates(z, c, base))
    move = Mover(z, c, base)
    first, second = c == 0, c == 1
    routes = [(s, 0, s, first) for s in range(3)] + [
        (0, 0, 3, second),
        (1, 1, 0, second),
        (1, 1, 1, second),
        (2, 1, 2, second),
        (2, 1, 3, second),
    ]
    count = 0
    for slot, ab, chip, when in routes:
        for half in range(2):
            move.send(
                tok.at[slot, half], x.at[ab, z, half], d_send.at[count], d_recv.at[ab, z, half], chip, half, when
            )
            move.send(seg.at[slot], segs.at[ab, z], g_send.at[count], g_recv.at[ab, z], chip, half, when)
            count += 1
    deep, low = z // 2, lax.rem(z, 2)
    for slot in range(3):
        move.send(cot.at[slot], cotq.at[low], c_send.at[slot], c_recv.at[low], slot, deep, first)
    move.send(cot.at[0], cotq.at[low], c_send.at[3], c_recv.at[low], 3, deep, second)
    move.send(cot.at[1], cotq.at[2], c_send.at[4], c_recv.at[2], deep, low, second)
    move.send(cot.at[2], cotq.at[2], c_send.at[5], c_recv.at[2], 2 + deep, low, second)
    forwards = []
    for ab in range(2):
        for b in range(4):
            landed(x.at[ab, b, c], d_recv.at[ab, b, c])
            copy = remote(
                x.at[ab, b, c], x.at[ab, b, c], f_send.at[ab, b], d_recv.at[ab, b, c], at(z, base + 1 - c)
            )
            copy.start()
            forwards.append(copy)
    for ab in range(2):
        for b in range(4):
            landed(x.at[ab, b, 1 - c], d_recv.at[ab, b, 1 - c])
            landed(segs.at[ab, b], g_recv.at[ab, b])
    for slot in range(3):
        landed(cotq.at[slot], c_recv.at[slot])
    for copy in forwards:
        copy.wait_send()
    move.finish()


def exchange(tokens, segments, cotangent):
    vmem = pl.BlockSpec(memory_space=pltpu.VMEM)
    dma = pltpu.SemaphoreType.DMA
    return pl.pallas_call(
        exchange_body,
        out_shape=(
            jax.ShapeDtypeStruct((2, 4, 2, 64, D), BF),
            jax.ShapeDtypeStruct((2, 4, 8, BLOCK), jnp.int32),
            jax.ShapeDtypeStruct((3, BLOCK, D), BF),
        ),
        in_specs=[vmem] * 3,
        out_specs=[vmem] * 3,
        scratch_shapes=[dma((16,)), dma((2, 4, 2)), dma((2, 4)), dma((16,)), dma((2, 4)), dma((6,)), dma((3,))],
        compiler_params=pltpu.CompilerParams(
            collective_id=0, has_side_effects=True, vmem_limit_bytes=16 * MIB
        ),
    )(tokens, segments, cotangent)


def lane_low():
    return lax.broadcasted_iota(jnp.int32, (BLOCK, LANES), 1) < 64


def stack_heads(pair, low):
    zero = jnp.zeros_like(pair)
    return jnp.concatenate([jnp.where(low, pair, zero), jnp.where(low, zero, pair)], axis=0)


def merge_heads(both, low):
    return jnp.where(low, both[:BLOCK], both[BLOCK:])


def moments(resid):
    center = resid - jnp.mean(resid, axis=-1, keepdims=True)
    inverse = lax.rsqrt(jnp.mean(center * center, axis=-1, keepdims=True) + EPS)
    return center * inverse, inverse


def norm_back(upstream, unit, inverse, gain):
    scaled = upstream * gain
    return inverse * (
        scaled
        - jnp.mean(scaled, axis=-1, keepdims=True)
        - unit * jnp.mean(scaled * unit, axis=-1, keepdims=True)
    )


def column_sum(value):
    return jnp.sum(value, axis=0, keepdims=True)


def forward_body(
    x,
    segs,
    cot,
    w_query,
    b_query,
    w_key,
    w_value,
    b_value,
    w_out,
    b_out,
    gain_first,
    shift_first,
    w_inner,
    b_inner,
    w_outer,
    b_outer,
    gain_second,
    shift_second,
    q,
    k,
    v,
    prob,
    att,
    d_att,
    d_first,
    xq,
    layer,
    early,
    vec,
    bias,
    unit1,
    inv1,
    low1,
    act,
    slope,
    acc,
    d_out,
):
    z, beta, c, base = place()
    low = lane_low()
    tokens = 3 * BLOCK
    vec[...] = jnp.zeros_like(vec)
    own = [(0, 2 * c), (0, 2 * c + 1), (1, 2 * lax.rem(z, 2) + c)]
    for u, (ab, b) in enumerate(own):
        xq[u] = x[ab, b].reshape(BLOCK, D)

    def one_hot(row):
        return (lax.broadcasted_iota(jnp.int32, (8, BLOCK), 0) == row).astype(F32)

    for u, (ab, b) in enumerate(own):
        mine = one_hot(segs[ab, b])
        for kb in range(4):
            same = dot_tn(mine, one_hot(segs[ab, kb]))
            bias[u, :, kb * BLOCK : (kb + 1) * BLOCK] = jnp.where(same > 0.5, 0.0, -1e30)

    xq_all = xq[...].reshape(tokens, D)
    q[...] = ((dot(xq_all, w_query[...]) + b_query[...]).astype(BF) * 0.125).astype(BF).reshape(3, BLOCK, D)
    for ab in range(2):
        xk = x[ab].reshape(ROW, D)
        k[ab] = dot(xk, w_key[...]).astype(BF)
        v[ab] = (dot(xk, w_value[...]) + b_value[...]).astype(BF)

    def attend(n, carry):
        u, j = n // PAIRS, lax.rem(n, PAIRS)
        ab = u // 2
        cols = pl.ds(pl.multiple_of(j * LANES, LANES), LANES)
        score = dot_nt(stack_heads(q[u, :, cols], low), k[ab, :, cols])
        score = (score.reshape(2, BLOCK, ROW) + bias[u][None]).reshape(2 * BLOCK, ROW)
        expo = jnp.exp(score - jnp.max(score, axis=-1, keepdims=True))
        p = (expo * (1.0 / jnp.sum(expo, axis=-1, keepdims=True))).astype(BF)
        prob[n] = p
        att[u, :, cols] = merge_heads(dot(p, v[ab, :, cols]), low).astype(BF)
        return carry

    lax.fori_loop(0, 3 * PAIRS, attend, 0)

    acc[...] = dot(att[...].reshape(tokens, D), w_out[...]).reshape(3, BLOCK, D)

    def norm_one(u, carry):
        first = xq[u].astype(F32) + acc[u] + b_out[...]
        unit, inverse = moments(first)
        unit1[u] = unit
        inv1[u] = jnp.broadcast_to(inverse, (BLOCK, LANES))
        low1[u] = (unit * gain_first[...] + shift_first[...]).astype(BF)
        return carry

    lax.fori_loop(0, 3, norm_one, 0)
    acc[...] = jnp.zeros_like(acc)

    def feed(f, carry):
        cols = pl.ds(pl.multiple_of(f * FFT, FFT), FFT)
        pre = dot(low1[...].reshape(tokens, D), w_inner[:, cols]) + b_inner[:, cols]
        half = 0.5 * (1.0 + lax.erf(pre * (1.0 / math.sqrt(2.0))))
        slope[f] = (half + pre * jnp.exp(-0.5 * pre * pre) * (1.0 / math.sqrt(2.0 * math.pi))).astype(BF)
        act_low = (pre * half).astype(BF)
        act[f] = act_low
        acc[...] += dot(act_low, w_outer[cols, :]).reshape(3, BLOCK, D)
        return carry

    lax.fori_loop(0, FFN, feed, 0)

    def norm_two(u, carry):
        second = unit1[u] * gain_first[...] + shift_first[...] + acc[u] + b_outer[...]
        unit, inverse = moments(second)
        layer[u] = (unit * gain_second[...] + shift_second[...]).astype(BF)
        up = cot[u].astype(F32)
        d_second = norm_back(up, unit, inverse, gain_second[...])
        d_low = d_second.astype(BF)
        acc[u] = d_second
        d_out[u] = d_low
        vec[5:6] += column_sum(d_low.astype(F32))
        vec[6:7] += column_sum(up * unit)
        vec[7:8] += column_sum(up)
        return carry

    lax.fori_loop(0, 3, norm_two, 0)

    def feed_back(f, carry):
        cols = pl.ds(pl.multiple_of(f * FFT, FFT), FFT)
        up = d_out[...].reshape(tokens, D)
        d_pre = (dot_nt(up, w_outer[cols, :]) * slope[f].astype(F32)).astype(BF)
        vec[pl.ds(8 + f, 1)] = column_sum(d_pre.astype(F32))
        g_outer = dot_tn(act[f], up).astype(BF)
        for piece in range(2):
            for part in range(4):
                row = 384 * piece + 96 * part
                early[part, piece, f] = g_outer[row : row + 96].reshape(2, 48, D)
        g_inner = dot_tn(low1[...].reshape(tokens, D), d_pre).astype(BF)
        for p in range(8):
            early[4 + f, p % 2, p // 2] = g_inner[96 * p : 96 * p + 96].reshape(2, 48, D)
        acc[...] += dot_nt(d_pre, w_inner[:, cols]).reshape(3, BLOCK, D)
        return carry

    lax.fori_loop(0, FFN, feed_back, 0)

    def norm_one_back(u, carry):
        up = acc[u]
        inner = norm_back(up, unit1[u], inv1[u][:, 0:1], gain_first[...])
        d_first[u] = inner
        d_low = inner.astype(BF)
        d_out[u] = d_low
        vec[2:3] += column_sum(d_low.astype(F32))
        vec[3:4] += column_sum(up * unit1[u])
        vec[4:5] += column_sum(up)
        return carry

    lax.fori_loop(0, 3, norm_one_back, 0)
    up = d_out[...].reshape(tokens, D)
    d_att[...] = dot_nt(up, w_out[...]).astype(BF).reshape(3, BLOCK, D)
    g_out = dot_tn(att[...].reshape(tokens, D), up).astype(BF)
    for p in range(8):
        early[8, p % 2, p // 2] = g_out[96 * p : 96 * p + 96].reshape(2, 48, D)


def forward(x, segs, cot, weights):
    vmem = pl.BlockSpec(memory_space=pltpu.VMEM)
    tok = (3, BLOCK, D)
    shapes = [
        (tok, BF),
        ((2, ROW, D), BF),
        ((2, ROW, D), BF),
        ((3 * PAIRS, 2 * BLOCK, ROW), BF),
        (tok, BF),
        (tok, BF),
        (tok, F32),
        (tok, BF),
        (tok, BF),
        ((EARLY, 2, 4, 2, 48, D), BF),
        ((16, D), F32),
    ]
    args = (x, segs, cot) + weights
    return pl.pallas_call(
        forward_body,
        out_shape=tuple(jax.ShapeDtypeStruct(s, t) for s, t in shapes),
        in_specs=[vmem] * len(args),
        out_specs=[vmem] * len(shapes),
        scratch_shapes=[
            pltpu.VMEM((3, BLOCK, ROW), F32),
            pltpu.VMEM(tok, F32),
            pltpu.VMEM((3, BLOCK, LANES), F32),
            pltpu.VMEM(tok, BF),
            pltpu.VMEM((FFN, 3 * BLOCK, FFT), BF),
            pltpu.VMEM((FFN, 3 * BLOCK, FFT), BF),
            pltpu.VMEM(tok, F32),
            pltpu.VMEM(tok, BF),
        ],
        compiler_params=pltpu.CompilerParams(vmem_limit_bytes=62 * MIB),
    )(*args)


def backward_body(
    x,
    xq,
    q,
    k,
    v,
    prob,
    att,
    d_att,
    d_first,
    layer,
    early,
    vec_in,
    w_query,
    w_key,
    w_value,
    sums,
    vec_out,
    lay_out,
    grad_parts,
    own,
    late,
    r1,
    r2,
    r3,
    ro,
    rj,
    dq,
    dkt,
    dvt,
    dk,
    dv,
    dx,
    dxs,
    rxa,
    rxb,
    sv,
    rv,
    own_sem,
    s1,
    t1,
    s2,
    t2,
    s3,
    t3,
    so,
    to,
    sj,
    tj,
    sf,
    tf,
    lay_s,
    lay_r,
    xs,
    xr,
    gs,
    gr,
    vs,
    vr,
):
    z, beta, c, base = place()
    low = lane_low()
    bx, by = lax.rem(beta // 2, 2), lax.rem(beta // 4, 2)
    sibling = at(z, base + 1 - c)
    to_x, to_y = at(z, beta + 2 - 4 * bx), at(z, beta + 4 - 8 * by)
    greet(column_mates(z, c, base) + [to_x, to_y])
    inner = jnp.logical_and(z > 0, z < 3)
    outer = jnp.logical_not(inner)
    half = lax.rem(z + 1, 2)
    mine = jnp.where(z == 2, 1, 0)
    neighbour = jnp.where(z < 2, 1 - z, 5 - z)
    partner = jnp.where(z == 1, 2, 1)
    near, across = at(neighbour, beta), at(partner, beta)
    tokens = 3 * BLOCK

    def fetch_own(i):
        return pltpu.make_async_copy(early.at[i, c], own.at[i], own_sem.at[i])

    def first_send(i, src):
        return remote(src, r1.at[i], s1.at[i], t1.at[i], sibling)

    for i in range(EARLY):
        first_send(i, early.at[i, 1 - c]).start()
        fetch_own(i).start()

    move = Mover(z, c, base)
    row_core = jnp.where(z == 3, 1, 0)
    row_slot = lax.rem(z, 3)
    deep, lowz = z // 2, lax.rem(z, 2)
    move.send(layer.at[0], lay_out.at[row_slot], lay_s.at[0], lay_r.at[row_slot], 2 * c, row_core)
    move.send(layer.at[1], lay_out.at[row_slot], lay_s.at[1], lay_r.at[row_slot], 2 * c + 1, row_core)
    move.send(layer.at[2], lay_out.at[1 + deep], lay_s.at[2], lay_r.at[1 + deep], 2 * lowz + c, 1)

    def split(i):
        t = lax.rem(i, 2)
        return t, 1 - t

    def sent_piece(i, e):
        t, s = split(i)
        return t * (2 * (1 - by) + e) + s * (2 * e + 1 - bx)

    def kept_piece(i, e):
        t, s = split(i)
        return t * (2 * by + e) + s * (2 * e + bx)

    def second_to(i):
        t, s = split(i)
        return at(z, beta + s * (2 - 4 * bx) + t * (4 - 8 * by))

    def third_to(i):
        t, s = split(i)
        return at(z, beta + t * (2 - 4 * bx) + s * (4 - 8 * by))

    def kept_half(i):
        t, s = split(i)
        return t * bx + s * by

    def second_send(i, e):
        return remote(r1.at[i, sent_piece(i, e)], r2.at[i, e], s2.at[i, e], t2.at[i, e], second_to(i))

    def third_send(i):
        return remote(r2.at[i, 1 - kept_half(i)], r3.at[i], s3.at[i], t3.at[i], third_to(i))

    def outer_send(i):
        return remote(r3.at[i], ro.at[i], so.at[i], to.at[i], near)

    def cross_send(i):
        return remote(r3.at[i, 1 - mine], rj.at[i], sj.at[i], tj.at[i], across)

    def final_near(i):
        return remote(sums.at[i, mine], sums.at[i, mine], sf.at[i, 0], tf.at[i, mine], near)

    def final_across(i):
        return remote(sums.at[i, mine], sums.at[i, mine], sf.at[i, 1], tf.at[i, mine], across)

    def final_forward(i):
        return remote(sums.at[i, 1 - mine], sums.at[i, 1 - mine], sf.at[i, 2], tf.at[i, 1 - mine], near)

    def wide(value):
        return value.astype(F32)

    def stage2(i):
        @pl.when(i < EARLY)
        def _():
            fetch_own(i).wait()

        landed(r1.at[i], t1.at[i])
        for e in range(2):
            p = sent_piece(i, e)
            r1[i, p] = (wide(r1[i, p]) + wide(own[i, p])).astype(BF)
            second_send(i, e).start()

    def stage3(i):
        for e in range(2):
            landed(r2.at[i, e], t2.at[i, e])
        e = 1 - kept_half(i)
        p = kept_piece(i, e)
        r2[i, e] = (wide(r2[i, e]) + wide(r1[i, p]) + wide(own[i, p])).astype(BF)
        third_send(i).start()

    def stage4(i):
        landed(r3.at[i], t3.at[i])
        e = kept_half(i)
        p = kept_piece(i, e)
        total = wide(r2[i, e]) + wide(r1[i, p]) + wide(own[i, p]) + wide(r3[i])
        r3[i] = total.astype(BF)

        @pl.when(outer)
        def _():
            outer_send(i).start()

    def stage5(i):
        @pl.when(inner)
        def _():
            landed(ro.at[i], to.at[i])
            r3[i, 1 - mine] = (wide(r3[i, 1 - mine]) + wide(ro[i, 1 - mine])).astype(BF)
            cross_send(i).start()

    def stage6(i):
        @pl.when(inner)
        def _():
            landed(rj.at[i], tj.at[i])
            sums[i, mine] = (wide(r3[i, mine]) + wide(ro[i, mine]) + wide(rj[i])).astype(BF)
            final_near(i).start()
            final_across(i).start()

    def stage7(i):
        @pl.when(inner)
        def _():
            landed(sums.at[i, 1 - mine], tf.at[i, 1 - mine])
            final_forward(i).start()

    stages = [stage2, stage3, stage4, stage5, stage6, stage7]

    def tick(n):
        for lag, stage in enumerate(stages):
            i = n - lag

            @pl.when(jnp.logical_and(i >= 0, i < CHUNKS))
            def _(i=i, stage=stage):
                stage(i)

    def attend_back(n):
        u, j = n // PAIRS, lax.rem(n, PAIRS)
        ab = u // 2
        cols = pl.ds(pl.multiple_of(j * LANES, LANES), LANES)
        d_pair = d_att[u, :, cols]
        d_both = stack_heads(d_pair, low)
        product = wide(d_pair) * wide(att[u, :, cols])
        even = jnp.sum(jnp.where(low, product, 0.0), axis=-1, keepdims=True)
        odd = jnp.sum(jnp.where(low, 0.0, product), axis=-1, keepdims=True)
        centre = jnp.concatenate([even, odd], axis=0)
        p = prob[n]
        d_prob = dot_nt(d_both, v[ab, :, cols])
        d_score = (wide(p) * (d_prob - centre)).astype(BF)
        dq[u, :, cols] = (merge_heads(dot(d_score, k[ab, :, cols]), low) * 0.125).astype(BF)
        q_both = stack_heads(q[u, :, cols], low)
        g_key = dot(q_both.T, d_score)
        g_value = dot(d_both.T, p)

        @pl.when(u == 1)
        def _():
            dkt[ab, cols, :] += g_key
            dvt[ab, cols, :] += g_value

        @pl.when(u != 1)
        def _():
            dkt[ab, cols, :] = g_key
            dvt[ab, cols, :] = g_value

    def step(n, carry):
        attend_back(n)

        @pl.when(lax.rem(n, 3) == 2)
        def _():
            tick(n // 3)

        return carry

    lax.fori_loop(0, 3 * PAIRS, step, 0)
    done = PAIRS

    for ab in range(2):
        dk[ab] = dkt[ab].astype(BF).T
        dv[ab] = dvt[ab].astype(BF).T

    def keep_late(i, grad):
        low_grad = grad.astype(BF)
        for p in range(8):
            late[i, p % 2, p // 2] = low_grad[96 * p : 96 * p + 96].reshape(2, 48, D)
        first_send(EARLY + i, late.at[i, 1 - c]).start()
        own[EARLY + i] = late[i, c]

    keep_late(0, dot_tn(xq[...].reshape(tokens, D), dq[...].reshape(tokens, D)))
    tick(done)
    keep_late(1, dot_tn(x[...].reshape(2 * ROW, D), dk[...].reshape(2 * ROW, D)))
    keep_late(2, dot_tn(x[...].reshape(2 * ROW, D), dv[...].reshape(2 * ROW, D)))
    tick(done + 1)
    sv[0] = vec_in[...]
    sv[0, 0:1] = column_sum(wide(dq[...].reshape(tokens, D)))
    sv[0, 1:2] = column_sum(wide(dv[...].reshape(2 * ROW, D)))

    vec_to = [sibling, to_x, to_y, at(z + 1 - 2 * lowz, beta), at(z + 2 - 4 * deep, beta)]

    def vec_send(i):
        return remote(sv.at[i], rv.at[i], vs.at[i], vr.at[i], vec_to[i])

    vec_send(0).start()

    for ab in range(2):
        part = dot_nt(dk[ab], w_key[...]) + dot_nt(dv[ab], w_value[...])
        dx[ab] = part.reshape(4, BLOCK, D)
    query_part = dot_nt(dq[...].reshape(tokens, D), w_query[...]).reshape(3, BLOCK, D)
    blocks = [(0, 2 * c), (0, 2 * c + 1), (1, 2 * lowz + c)]
    for u, (ab, b) in enumerate(blocks):
        dx[ab, b] += query_part[u] + d_first[u]
    dxs[...] = dx[...].astype(BF)
    swap = [
        remote(dxs.at[0, 2 * (1 - c) + e], rxa.at[e], xs.at[0, e], xr.at[0, e], sibling) for e in range(2)
    ] + [remote(dxs.at[1, 1 - c + 2 * e], rxb.at[e], xs.at[1, e], xr.at[1, e], sibling) for e in range(2)]
    for copy in swap:
        copy.start()
    tick(done + 2)
    for e in range(2):
        landed(rxa.at[e], xr.at[0, e])
        rxa[e] = (dx[0, 2 * c + e] + wide(rxa[e])).astype(BF)
        move.send(rxa.at[e], grad_parts.at[row_slot, 0], gs.at[e], gr.at[row_slot, 0], 2 * c + e, row_core)
    for e in range(2):
        landed(rxb.at[e], xr.at[1, e])
        rxb[e] = (dx[1, c + 2 * e] + wide(rxb[e])).astype(BF)
        move.send(rxb.at[e], grad_parts.at[1 + deep, lowz], gs.at[2 + e], gr.at[1 + deep, lowz], c + 2 * e, 1)
    done += 3

    def vec_stage(i):
        landed(rv.at[i], vr.at[i])
        total = sv[i] + rv[i]
        if i < 4:
            sv[i + 1] = total
            vec_send(i + 1).start()
        else:
            vec_out[...] = total

    for i in range(5):
        tick(done + i)
        vec_stage(i)
    done += 5

    def rest(n, carry):
        tick(n)
        return carry

    lax.fori_loop(done, CHUNKS + len(stages) - 1, rest, 0)

    def close(i, carry):
        first_send(i, own.at[i]).wait_send()
        for e in range(2):
            second_send(i, e).wait_send()
        third_send(i).wait_send()

        @pl.when(outer)
        def _():
            outer_send(i).wait_send()
            landed(sums.at[i, 0], tf.at[i, 0])
            landed(sums.at[i, 1], tf.at[i, 1])

        @pl.when(inner)
        def _():
            cross_send(i).wait_send()
            final_near(i).wait_send()
            final_across(i).wait_send()
            final_forward(i).wait_send()

        return carry

    lax.fori_loop(0, CHUNKS, close, 0)
    for i in range(5):
        vec_send(i).wait_send()
    for copy in swap:
        copy.wait_send()
    for slot in range(3):
        landed(lay_out.at[slot], lay_r.at[slot])
        landed(grad_parts.at[slot, 0], gr.at[slot, 0])

    @pl.when(c == 1)
    def _():
        for slot in range(1, 3):
            landed(grad_parts.at[slot, 1], gr.at[slot, 1])

    move.finish()


def backward(x, xq, q, k, v, prob, att, d_att, d_first, layer, early, vec, w_query, w_key, w_value):
    vmem = pl.BlockSpec(memory_space=pltpu.VMEM)
    dma = pltpu.SemaphoreType.DMA
    args = (x, xq, q, k, v, prob, att, d_att, d_first, layer, early, vec, w_query, w_key, w_value)
    specs = [vmem] * len(args)
    specs[10] = pl.BlockSpec(memory_space=pl.ANY)
    n = CHUNKS
    return pl.pallas_call(
        backward_body,
        out_shape=(
            jax.ShapeDtypeStruct((n, 2, 48, D), BF),
            jax.ShapeDtypeStruct((16, D), F32),
            jax.ShapeDtypeStruct((3, BLOCK, D), BF),
            jax.ShapeDtypeStruct((3, 2, BLOCK, D), BF),
        ),
        in_specs=specs,
        out_specs=[vmem] * 4,
        scratch_shapes=[
            pltpu.VMEM((n, 4, 2, 48, D), BF),
            pltpu.VMEM((3, 2, 4, 2, 48, D), BF),
            pltpu.VMEM((n, 4, 2, 48, D), BF),
            pltpu.VMEM((n, 2, 2, 48, D), BF),
            pltpu.VMEM((n, 2, 48, D), BF),
            pltpu.VMEM((n, 2, 48, D), BF),
            pltpu.VMEM((n, 48, D), BF),
            pltpu.VMEM((3, BLOCK, D), BF),
            pltpu.VMEM((2, D, ROW), F32),
            pltpu.VMEM((2, D, ROW), F32),
            pltpu.VMEM((2, ROW, D), BF),
            pltpu.VMEM((2, ROW, D), BF),
            pltpu.VMEM((2, 4, BLOCK, D), F32),
            pltpu.VMEM((2, 4, BLOCK, D), BF),
            pltpu.VMEM((2, BLOCK, D), BF),
            pltpu.VMEM((2, BLOCK, D), BF),
            pltpu.VMEM((5, 16, D), F32),
            pltpu.VMEM((5, 16, D), F32),
            dma((n,)),
            dma((n,)),
            dma((n,)),
            dma((n, 2)),
            dma((n, 2)),
            dma((n,)),
            dma((n,)),
            dma((n,)),
            dma((n,)),
            dma((n,)),
            dma((n,)),
            dma((n, 3)),
            dma((n, 2)),
            dma((3,)),
            dma((3,)),
            dma((2, 2)),
            dma((2, 2)),
            dma((4,)),
            dma((3, 2)),
            dma((5,)),
            dma((5,)),
        ],
        compiler_params=pltpu.CompilerParams(
            collective_id=1, has_side_effects=True, vmem_limit_bytes=63 * MIB
        ),
    )(*args)


def finish_body(sums, vec, lay, parts, *outs):
    p = lax.rem(lax.axis_index("batch"), 8)
    c = lax.rem(p, 2)
    layer_out, input_grad, g_q, g_k, g_v, g_o, g_inner, g_outer, vecs, b_inner = outs
    layer_out[...] = lay[...]
    input_grad[...] = parts[:, 0]

    @pl.when(c == 1)
    def _():
        for slot in range(1, 3):
            input_grad[slot] = (parts[slot, 0].astype(F32) + parts[slot, 1].astype(F32)).astype(BF)

    def piece(i):
        return sums[i].reshape(96, D).astype(F32)

    for part in range(4):
        g_outer[96 * part : 96 * part + 96] = piece(part)
    for f in range(FFN):
        g_inner[:, f * FFT : (f + 1) * FFT] = piece(4 + f)
    g_o[...] = piece(8)
    g_q[...] = piece(9)
    g_k[...] = piece(10)
    g_v[...] = piece(11)
    pick = lax.broadcasted_iota(jnp.int32, (D, LANES), 0) == lax.broadcasted_iota(jnp.int32, (D, LANES), 1) + 96 * p
    vecs[...] = jnp.dot(
        vec[0:8], pick.astype(F32), preferred_element_type=F32, precision=lax.Precision.HIGHEST
    )
    b_inner[...] = vec[pl.ds(8 + p // 2, 1), pl.ds(pl.multiple_of(384 * lax.rem(p, 2), LANES), 384)]


def finish(sums, vec, lay, parts):
    vmem = pl.BlockSpec(memory_space=pltpu.VMEM)
    tok = (3, BLOCK, D)
    shapes = [
        (tok, BF),
        (tok, BF),
        ((96, D), F32),
        ((96, D), F32),
        ((96, D), F32),
        ((96, D), F32),
        ((96, 4 * D), F32),
        ((384, D), F32),
        ((8, LANES), F32),
        ((1, 384), F32),
    ]
    return pl.pallas_call(
        finish_body,
        out_shape=tuple(jax.ShapeDtypeStruct(s, t) for s, t in shapes),
        in_specs=[vmem] * 4,
        out_specs=[vmem] * len(shapes),
        compiler_params=pltpu.CompilerParams(vmem_limit_bytes=32 * MIB),
    )(sums, vec, lay, parts)


def per_device(
    groups,
    tokens,
    segment_ids,
    w_query,
    b_query,
    w_key,
    w_value,
    b_value,
    w_out,
    b_out,
    gain_first,
    shift_first,
    w_inner,
    b_inner,
    w_outer,
    b_outer,
    gain_second,
    shift_second,
    cotangent,
):
    def row(value):
        return value.reshape(1, -1)

    seg = jnp.broadcast_to(segment_ids[:, None, :], (3, 8, BLOCK))
    x, segs, cot = exchange(tokens.reshape(3, 2, 64, D), seg, cotangent)
    weights = (
        w_query,
        row(b_query),
        w_key,
        w_value,
        row(b_value),
        w_out,
        row(b_out),
        row(gain_first),
        row(shift_first),
        w_inner,
        row(b_inner),
        w_outer,
        row(b_outer),
        row(gain_second),
        row(shift_second),
    )
    q, k, v, prob, att, d_att, d_first, xq, layer, early, vec = forward(x, segs, cot, weights)
    sums, vec, lay, parts = backward(
        x, xq, q, k, v, prob, att, d_att, d_first, layer, early, vec, w_query, w_key, w_value
    )
    layer_out, input_grad, g_q, g_k, g_v, g_o, g_inner, g_outer, vecs, g_b_inner = finish(sums, vec, lay, parts)
    vecs = [vecs[i, :96] for i in range(8)]
    g_b_query, g_b_value, g_b_out, g_gain_first, g_shift_first, g_b_outer, g_gain_second, g_shift_second = vecs
    grads = (
        g_q,
        g_b_query,
        g_k,
        g_v,
        g_b_value,
        g_o,
        g_b_out,
        g_gain_first,
        g_shift_first,
        g_inner,
        g_b_inner.reshape(384),
        g_outer,
        g_b_outer,
        g_gain_second,
        g_shift_second,
    )
    if groups > 1:
        place_at = lax.rem(lax.axis_index("batch"), 8)

        def spread(grad):
            whole = jnp.zeros((8 * grad.shape[0],) + grad.shape[1:], grad.dtype)
            whole = lax.dynamic_update_slice_in_dim(whole, grad, place_at * grad.shape[0], 0)
            return lax.psum_scatter(whole, "batch", scatter_dimension=0, tiled=True)

        grads = tuple(spread(grad) for grad in grads)
    return (layer_out, input_grad) + grads


def solution(mesh):
    tokens = P("batch", "blk", None)
    weight, vector = P("batch", None), P("batch")
    return jax.shard_map(
        functools.partial(per_device, mesh.shape["batch"] // 8),
        mesh=mesh,
        in_specs=(tokens, P("batch", "blk")) + (P(),) * 15 + (tokens,),
        out_specs=(tokens, tokens)
        + (
            weight,
            vector,
            weight,
            weight,
            vector,
            weight,
            vector,
            vector,
            vector,
            weight,
            vector,
            weight,
            vector,
            vector,
            vector,
        ),
        check_vma=False,
    )
```

```python
import functools
import math

import jax
import jax.numpy as jnp
from jax import lax
from jax.experimental import pallas as pl
from jax.experimental.pallas import tpu as pltpu
from jax.sharding import PartitionSpec as P

BF = jnp.bfloat16
F32 = jnp.float32
EPS = 1e-05
D = 768
PAIRS = 6
LANES = 128
BLOCK = 128
ROW = 512
FFT = 768
FFN = 4
EARLY = 9
CHUNKS = 12
LAGS = (0, 2, 4, 5, 6, 7)
MIB = 1 << 20


def dot(a, b):
    return jnp.dot(a, b, preferred_element_type=F32)


def dot_nt(a, b):
    return lax.dot_general(a, b, (((1,), (1,)), ((), ())), preferred_element_type=F32)


def dot_tn(a, b):
    return lax.dot_general(a, b, (((0,), (0,)), ((), ())), preferred_element_type=F32)


def place():
    z = lax.axis_index("blk")
    beta = lax.axis_index("batch")
    c = lax.rem(beta, 2)
    return z, beta, c, beta - c


def at(z, beta):
    return {"blk": z, "batch": beta}


def greet(devices):
    barrier = pltpu.get_barrier_semaphore()
    for device in devices:
        pl.semaphore_signal(barrier, inc=1, device_id=device, device_id_type=pl.DeviceIdType.MESH)
    pl.semaphore_wait(barrier, len(devices))


def column_mates(z, c, base):
    mates = [at(lax.rem(z + step, 4), base + core) for step in range(1, 4) for core in range(2)]
    return mates + [at(z, base + 1 - c)]


def remote(src, dst, send_sem, recv_sem, device):
    return pltpu.make_async_remote_copy(
        src_ref=src,
        dst_ref=dst,
        send_sem=send_sem,
        recv_sem=recv_sem,
        device_id=device,
        device_id_type=pl.DeviceIdType.MESH,
    )


class Mover:
    def __init__(self, z, c, base):
        self.z, self.c, self.base, self.sent = z, c, base, []

    def send(self, src, dst, send_sem, recv_sem, to_z, to_c, when=None):
        self_target = jnp.logical_and(to_z == self.z, to_c == self.c)
        other = jnp.logical_not(self_target)
        if when is not None:
            self_target = jnp.logical_and(self_target, when)
            other = jnp.logical_and(other, when)
        out = remote(src, dst, send_sem, recv_sem, at(to_z, self.base + to_c))

        @pl.when(self_target)
        def _():
            pltpu.make_async_copy(src, dst, recv_sem).start()

        @pl.when(other)
        def _():
            out.start()

        self.sent.append((other, out))

    def finish(self):
        for other, out in self.sent:

            @pl.when(other)
            def _(out=out):
                out.wait_send()

        self.sent = []


def landed(dst, sem):
    pltpu.make_async_copy(dst, dst, sem).wait()


def lane_low():
    return lax.broadcasted_iota(jnp.int32, (BLOCK, LANES), 1) < 64


def stack_heads(pair, low):
    zero = jnp.zeros_like(pair)
    return jnp.concatenate([jnp.where(low, pair, zero), jnp.where(low, zero, pair)], axis=0)


def merge_heads(both, low):
    return jnp.where(low, both[:BLOCK], both[BLOCK:])


def moments(resid):
    center = resid - jnp.mean(resid, axis=-1, keepdims=True)
    inverse = lax.rsqrt(jnp.mean(center * center, axis=-1, keepdims=True) + EPS)
    return center * inverse, inverse


def norm_back(upstream, unit, inverse, gain):
    scaled = upstream * gain
    return inverse * (
        scaled
        - jnp.mean(scaled, axis=-1, keepdims=True)
        - unit * jnp.mean(scaled * unit, axis=-1, keepdims=True)
    )


def column_sum(value):
    return jnp.sum(value, axis=0, keepdims=True)


def layer_body(
    tok,
    seg,
    cot,
    w_query_in,
    w_key_in,
    w_value_in,
    w_out_in,
    w_inner_in,
    w_outer_in,
    b_query_in,
    b_value_in,
    b_out_in,
    gain_first_in,
    shift_first_in,
    b_outer_in,
    gain_second_in,
    shift_second_in,
    b_inner_in,
    sums,
    vec_out,
    lay_out,
    grad_parts,
    pool,
    w_outer,
    w_query,
    w_key,
    w_value,
    w_out,
    rows,
    b_inner,
    x,
    segs,
    cotq,
    q,
    k,
    v,
    att,
    low1,
    act,
    slope,
    acc,
    unit1,
    d_out,
    bias,
    lse,
    inv1,
    vec,
    r1,
    r2,
    r3,
    ro,
    rj,
    rxa,
    rxb,
    sv,
    rv,
    w_sem,
    d_send,
    d_recv,
    f_send,
    g_send,
    g_recv,
    c_send,
    c_recv,
    s1,
    t1,
    s2,
    t2,
    s3,
    t3,
    so,
    to,
    sj,
    tj,
    sf,
    tf,
    lay_s,
    lay_r,
    xs,
    xr,
    gs,
    gr,
    vs,
    vr,
):
    z, beta, c, base = place()
    low = lane_low()
    tokens = 3 * BLOCK
    bx, by = lax.rem(beta // 2, 2), lax.rem(beta // 4, 2)
    sibling = at(z, base + 1 - c)
    to_x, to_y = at(z, beta + 2 - 4 * bx), at(z, beta + 4 - 8 * by)
    inner = jnp.logical_and(z > 0, z < 3)
    outer = jnp.logical_not(inner)
    mine = jnp.where(z == 2, 1, 0)
    near = at(jnp.where(z < 2, 1 - z, 5 - z), beta)
    across = at(jnp.where(z == 1, 2, 1), beta)
    deep, lowz = z // 2, lax.rem(z, 2)

    loads = []

    def load(src, dst):
        copy = pltpu.make_async_copy(src, dst, w_sem.at[len(loads)])
        copy.start()
        loads.append(copy)
        return copy

    greet(column_mates(z, c, base) + [to_x, to_y])
    move = Mover(z, c, base)
    first, second = c == 0, c == 1
    routes = [(s, 0, s, first) for s in range(3)] + [
        (0, 0, 3, second),
        (1, 1, 0, second),
        (1, 1, 1, second),
        (2, 1, 2, second),
        (2, 1, 3, second),
    ]
    count = 0
    for slot, ab, chip, when in routes:
        for half in range(2):
            move.send(
                tok.at[slot, half], x.at[ab, z, half], d_send.at[count], d_recv.at[ab, z, half], chip, half, when
            )
            move.send(seg.at[slot], segs.at[ab, z, 0], g_send.at[count], g_recv.at[ab, z], chip, half, when)
            count += 1

    got_key = load(w_key_in, w_key)
    got_value = load(w_value_in, w_value)
    got_query = load(w_query_in, w_query)
    vectors = [b_query_in, b_value_in, b_out_in, gain_first_in, shift_first_in, b_outer_in, gain_second_in]
    got_rows = [load(ref, rows.at[i]) for i, ref in enumerate(vectors + [shift_second_in])]
    got_rows.append(load(b_inner_in, b_inner.at[0]))
    got_out = load(w_out_in, w_out)
    got_inner = [load(w_inner_in.at[:, :, f * FFT : (f + 1) * FFT], pool.at[EARLY + f]) for f in range(FFN)]
    got_outer = [load(w_outer_in.at[f], w_outer.at[f]) for f in range(FFN)]

    b_query, b_value, b_out, gain_first, shift_first, b_outer, gain_second, shift_second = (
        rows.at[i : i + 1] for i in range(8)
    )
    vec[...] = jnp.zeros_like(vec)
    forwards = []
    for ab in range(2):
        for b in range(4):
            landed(x.at[ab, b, c], d_recv.at[ab, b, c])
            copy = remote(x.at[ab, b, c], x.at[ab, b, c], f_send.at[ab, b], d_recv.at[ab, b, c], sibling)
            copy.start()
            forwards.append(copy)

    for slot in range(3):
        move.send(cot.at[slot], cotq.at[lowz], c_send.at[slot], c_recv.at[lowz], slot, deep, first)
    move.send(cot.at[0], cotq.at[lowz], c_send.at[3], c_recv.at[lowz], 3, deep, second)
    move.send(cot.at[1], cotq.at[2], c_send.at[4], c_recv.at[2], deep, lowz, second)
    move.send(cot.at[2], cotq.at[2], c_send.at[5], c_recv.at[2], 2 + deep, lowz, second)

    own_blocks = [(0, 2 * c), (0, 2 * c + 1), (1, 2 * lowz + c)]

    def own_tokens(u):
        ab, b = own_blocks[u]
        return x[ab, b].reshape(BLOCK, D)

    def one_hot(row):
        return (lax.broadcasted_iota(jnp.int32, (8, BLOCK), 0) == row).astype(F32)

    got_key.wait()
    got_value.wait()
    got_query.wait()
    for copy in got_rows:
        copy.wait()
    for ab in range(2):
        for b in range(4):
            landed(x.at[ab, b, 1 - c], d_recv.at[ab, b, 1 - c])
            landed(segs.at[ab, b, 0], g_recv.at[ab, b])
        xk = x[ab].reshape(ROW, D)
        k[ab] = dot(xk, w_key[...]).astype(BF)
        v[ab] = (dot(xk, w_value[...]) + b_value[...]).astype(BF)
        for u, (row, b) in enumerate(own_blocks):
            if row == ab:
                q[u] = ((dot(own_tokens(u), w_query[...]) + b_query[...]).astype(BF) * 0.125).astype(BF)
                own_hot = one_hot(segs[ab, b, 0:1])
                for kb in range(4):
                    same = dot_tn(own_hot, one_hot(segs[ab, kb, 0:1]))
                    bias[u, :, kb * BLOCK : (kb + 1) * BLOCK] = jnp.where(same > 0.5, 0.0, -1e30)

    def lanes(j):
        return pl.ds(pl.multiple_of(j * LANES, LANES), LANES)

    lane = lax.broadcasted_iota(jnp.int32, (BLOCK, LANES), 1)

    def scores(u, cols, keys):
        score = dot_nt(stack_heads(q[u, :, cols], low), keys)
        return (score.reshape(2, BLOCK, ROW) + bias[u][None]).reshape(2 * BLOCK, ROW)

    def attend(n, carry):
        u, j = n // PAIRS, lax.rem(n, PAIRS)
        ab, cols = u // 2, lanes(j)
        score = scores(u, cols, k[ab, :, cols])
        top = jnp.max(score, axis=-1, keepdims=True)
        expo = jnp.exp(score - top)
        total = jnp.sum(expo, axis=-1, keepdims=True)
        p = (expo * (1.0 / total)).astype(BF)
        stat = top + jnp.log(total)
        lse[u] = jnp.where(lane == 2 * j, stat[:BLOCK], jnp.where(lane == 2 * j + 1, stat[BLOCK:], lse[u]))
        att[u, :, cols] = merge_heads(dot(p, v[ab, :, cols]), low).astype(BF)
        return carry

    for copy in forwards:
        copy.wait_send()
    lse[...] = jnp.zeros_like(lse)
    lax.fori_loop(0, 3 * PAIRS, attend, 0)

    got_out.wait()
    acc[...] = dot(att[...].reshape(tokens, D), w_out[...]).reshape(3, BLOCK, D)
    for u in range(3):
        resid = own_tokens(u).astype(F32) + acc[u] + b_out[...]
        unit, inverse = moments(resid)
        unit1[u] = unit
        inv1[u] = jnp.broadcast_to(inverse, (BLOCK, LANES))
        low1[u] = (unit * gain_first[...] + shift_first[...]).astype(BF)
    acc[...] = jnp.zeros_like(acc)
    for copy in got_inner + got_outer:
        copy.wait()

    def inner_weight(f):
        return pool[EARLY + f].reshape(D, FFT)

    def outer_weight(f):
        return w_outer[f].reshape(FFT, D)

    def feed(f, carry):
        cols = pl.ds(pl.multiple_of(f * FFT, FFT), FFT)
        pre = dot(low1[...].reshape(tokens, D), inner_weight(f)) + b_inner[0:1, cols]
        half = 0.5 * (1.0 + lax.erf(pre * (1.0 / math.sqrt(2.0))))
        slope[f] = (half + pre * jnp.exp(-0.5 * pre * pre) * (1.0 / math.sqrt(2.0 * math.pi))).astype(BF)
        act_low = (pre * half).astype(BF)
        act[f] = act_low
        acc[...] += dot(act_low, outer_weight(f)).reshape(3, BLOCK, D)
        return carry

    lax.fori_loop(0, FFN, feed, 0)

    for slot in range(3):
        landed(cotq.at[slot], c_recv.at[slot])
    for u in range(3):
        resid = unit1[u] * gain_first[...] + shift_first[...] + acc[u] + b_outer[...]
        unit, inverse = moments(resid)
        up = cotq[u].astype(F32)
        cotq[u] = (unit * gain_second[...] + shift_second[...]).astype(BF)
        d_second = norm_back(up, unit, inverse, gain_second[...])
        d_low = d_second.astype(BF)
        acc[u] = d_second
        d_out[u] = d_low
        vec[5:6] += column_sum(d_low.astype(F32))
        vec[6:7] += column_sum(up * unit)
        vec[7:8] += column_sum(up)

    row_core = jnp.where(z == 3, 1, 0)
    row_slot = lax.rem(z, 3)
    move.send(cotq.at[0], lay_out.at[row_slot], lay_s.at[0], lay_r.at[row_slot], 2 * c, row_core)
    move.send(cotq.at[1], lay_out.at[row_slot], lay_s.at[1], lay_r.at[row_slot], 2 * c + 1, row_core)
    move.send(cotq.at[2], lay_out.at[1 + deep], lay_s.at[2], lay_r.at[1 + deep], 2 * lowz + c, 1)

    def split(i):
        t = lax.rem(i, 2)
        return t, 1 - t

    def sent_piece(i, e):
        t, s = split(i)
        return 2 * (t * (2 * (1 - by) + e) + s * (2 * e + 1 - bx))

    def kept_piece(i, e):
        t, s = split(i)
        return 2 * (t * (2 * by + e) + s * (2 * e + bx))

    def second_to(i):
        t, s = split(i)
        return at(z, beta + s * (2 - 4 * bx) + t * (4 - 8 * by))

    def third_to(i):
        t, s = split(i)
        return at(z, beta + t * (2 - 4 * bx) + s * (4 - 8 * by))

    def kept_half(i):
        t, s = split(i)
        return t * bx + s * by

    def first_send(i):
        return remote(pool.at[i, pl.ds(8 * (1 - c), 8)], r1.at[i], s1.at[i], t1.at[i], sibling)

    def second_send(i, e):
        return remote(r1.at[i, pl.ds(sent_piece(i, e), 2)], r2.at[i, e], s2.at[i, e], t2.at[i, e], second_to(i))

    def third_send(i):
        return remote(r2.at[i, 1 - kept_half(i)], r3.at[i], s3.at[i], t3.at[i], third_to(i))

    def outer_send(i):
        return remote(r3.at[i], ro.at[i], so.at[i], to.at[i], near)

    def cross_send(i):
        return remote(r3.at[i, 1 - mine], rj.at[i], sj.at[i], tj.at[i], across)

    def final_near(i):
        return remote(sums.at[i, mine], sums.at[i, mine], sf.at[i, 0], tf.at[i, mine], near)

    def final_across(i):
        return remote(sums.at[i, mine], sums.at[i, mine], sf.at[i, 1], tf.at[i, mine], across)

    def final_forward(i):
        return remote(sums.at[i, 1 - mine], sums.at[i, 1 - mine], sf.at[i, 2], tf.at[i, 1 - mine], near)

    def wide(value):
        return value.astype(F32)

    def pair_sum(i, p):
        return wide(r1[i, pl.ds(p, 2)]) + wide(pool[i, pl.ds(8 * c + p, 2)])

    def stage2(i):
        landed(r1.at[i], t1.at[i])
        for order in range(2):
            e = lax.rem(1 - kept_half(i) + order, 2)
            p = sent_piece(i, e)
            r1[i, pl.ds(p, 2)] = pair_sum(i, p).astype(BF)
            second_send(i, e).start()

    def stage3(i):
        e = 1 - kept_half(i)
        landed(r2.at[i, e], t2.at[i, e])
        r2[i, e] = (wide(r2[i, e]) + pair_sum(i, kept_piece(i, e))).astype(BF)
        third_send(i).start()

    def stage4(i):
        e = kept_half(i)
        landed(r2.at[i, e], t2.at[i, e])
        landed(r3.at[i], t3.at[i])
        r3[i] = (wide(r2[i, e]) + pair_sum(i, kept_piece(i, e)) + wide(r3[i])).astype(BF)

        @pl.when(outer)
        def _():
            outer_send(i).start()

    def stage5(i):
        @pl.when(inner)
        def _():
            landed(ro.at[i], to.at[i])
            r3[i, 1 - mine] = (wide(r3[i, 1 - mine]) + wide(ro[i, 1 - mine])).astype(BF)
            cross_send(i).start()

    def stage6(i):
        @pl.when(inner)
        def _():
            landed(rj.at[i], tj.at[i])
            sums[i, mine] = (wide(r3[i, mine]) + wide(ro[i, mine]) + wide(rj[i])).astype(BF)
            final_near(i).start()
            final_across(i).start()

    def stage7(i):
        @pl.when(inner)
        def _():
            landed(sums.at[i, 1 - mine], tf.at[i, 1 - mine])
            final_forward(i).start()

    stages = list(zip((stage2, stage3, stage4, stage5, stage6, stage7), LAGS))

    def tick(n):
        for stage, lag in stages:
            i = n - lag

            @pl.when(jnp.logical_and(i >= 0, i < CHUNKS))
            def _(i=i, stage=stage):
                stage(i)

    up_all = d_out[...].reshape(tokens, D)
    for f in range(FFN):
        g_outer = dot_tn(act[f], up_all).astype(BF)
        for piece in range(2):
            for part in range(4):
                row = 384 * piece + 96 * part
                at_row = 8 * piece + 2 * f
                pool[part, at_row : at_row + 2] = g_outer[row : row + 96].reshape(2, 48, D)
    for i in range(4):
        first_send(i).start()

    def keep_rows(i, grad):
        low_grad = grad.astype(BF)
        for p in range(8):
            at_row = 8 * (p % 2) + 2 * (p // 2)
            pool[i, at_row : at_row + 2] = low_grad[96 * p : 96 * p + 96].reshape(2, 48, D)

    def feed_back(f, carry):
        up = d_out[...].reshape(tokens, D)
        d_pre = (dot_nt(up, outer_weight(f)) * slope[f].astype(F32)).astype(BF)
        vec[pl.ds(8 + f, 1)] = column_sum(d_pre.astype(F32))
        keep_rows(4 + f, dot_tn(low1[...].reshape(tokens, D), d_pre))
        first_send(4 + f).start()
        acc[...] += dot_nt(d_pre, inner_weight(f)).reshape(3, BLOCK, D)
        tick(f)
        return carry

    lax.fori_loop(0, FFN, feed_back, 0)

    for u in range(3):
        up = acc[u]
        d_first = norm_back(up, unit1[u], inv1[u][:, 0:1], gain_first[...])
        acc[u] = d_first
        d_low = d_first.astype(BF)
        d_out[u] = d_low
        vec[2:3] += column_sum(d_low.astype(F32))
        vec[3:4] += column_sum(up * unit1[u])
        vec[4:5] += column_sum(up)
    up_all = d_out[...].reshape(tokens, D)
    keep_rows(8, dot_tn(att[...].reshape(tokens, D), up_all))
    first_send(8).start()
    d_out[...] = dot_nt(up_all, w_out[...]).astype(BF).reshape(3, BLOCK, D)
    tick(FFN)

    def attend_back(j):
        cols = lanes(j)
        for ab in range(2):
            keys, values = k[ab, :, cols], v[ab, :, cols]
            g_key = g_value = None
            for u in (0, 1) if ab == 0 else (2,):
                q_both = stack_heads(q[u, :, cols], low)
                score = dot_nt(q_both, keys)
                score = (score.reshape(2, BLOCK, ROW) + bias[u][None]).reshape(2 * BLOCK, ROW)
                even = jnp.sum(jnp.where(lane == 2 * j, lse[u], 0.0), axis=-1, keepdims=True)
                odd = jnp.sum(jnp.where(lane == 2 * j + 1, lse[u], 0.0), axis=-1, keepdims=True)
                p = jnp.exp(score - jnp.concatenate([even, odd], axis=0))
                d_pair = d_out[u, :, cols]
                d_both = stack_heads(d_pair, low)
                product = wide(d_pair) * wide(att[u, :, cols])
                even = jnp.sum(jnp.where(low, product, 0.0), axis=-1, keepdims=True)
                odd = jnp.sum(jnp.where(low, 0.0, product), axis=-1, keepdims=True)
                d_prob = dot_nt(d_both, values)
                d_score = (p * (d_prob - jnp.concatenate([even, odd], axis=0))).astype(BF)
                one_key = dot(q_both.T, d_score)
                one_value = dot(d_both.T, p.astype(BF))
                g_key = one_key if g_key is None else g_key + one_key
                g_value = one_value if g_value is None else g_value + one_value
                q[u, :, cols] = (merge_heads(dot(d_score, keys), low) * 0.125).astype(BF)
            k[ab, :, cols] = g_key.astype(BF).T
            v[ab, :, cols] = g_value.astype(BF).T

    def step(j, carry):
        attend_back(j)

        @pl.when(lax.rem(j, 2) == 1)
        def _():
            tick(FFN + 1 + j // 2)

        return carry

    lax.fori_loop(0, PAIRS, step, 0)
    done = FFN + 1 + PAIRS // 2

    keep_rows(9, sum(dot_tn(own_tokens(u), q[u]) for u in range(3)))
    first_send(9).start()
    for i, grads in ((10, k), (11, v)):
        keep_rows(i, sum(dot_tn(x[ab].reshape(ROW, D), grads[ab]) for ab in range(2)))
        first_send(i).start()
    tick(done)
    sv[0] = vec[...]
    sv[0, 0:1] = sum(column_sum(wide(q[u])) for u in range(3))
    sv[0, 1:2] = sum(column_sum(wide(v[ab])) for ab in range(2))
    vec_to = [sibling, to_x, to_y, at(z + 1 - 2 * lowz, beta), at(z + 2 - 4 * deep, beta)]

    def vec_send(i):
        return remote(sv.at[i], rv.at[i], vs.at[i], vr.at[i], vec_to[i])

    vec_send(0).start()

    def share(ab, b):
        rows_b = pl.ds(pl.multiple_of(b * BLOCK, BLOCK), BLOCK)
        return dot_nt(k[ab, rows_b, :], w_key[...]) + dot_nt(v[ab, rows_b, :], w_value[...])

    def query_share(u):
        return dot_nt(q[u], w_query[...]) + acc[u]

    def put(ab, b, value):
        x[ab, b] = value.astype(BF).reshape(2, 64, D)

    swap = []
    for e in range(2):
        b = 2 * (1 - c) + e
        put(0, b, share(0, b))
        swap.append(remote(x.at[0, b], rxa.at[e], xs.at[0, e], xr.at[0, e], sibling))
        swap[-1].start()
    for e in range(2):
        b = 1 - c + 2 * e
        put(1, b, share(1, b))
        swap.append(remote(x.at[1, b], rxb.at[e], xs.at[1, e], xr.at[1, e], sibling))
        swap[-1].start()
    tick(done + 1)
    for e in range(2):
        total = share(0, 2 * c + e) + query_share(e)
        landed(rxa.at[e], xr.at[0, e])
        rxa[e] = (total + wide(rxa[e]).reshape(BLOCK, D)).astype(BF).reshape(2, 64, D)
        move.send(rxa.at[e], grad_parts.at[row_slot, 0], gs.at[e], gr.at[row_slot, 0], 2 * c + e, row_core)
    unit1[0] = query_share(2)
    for e in range(2):
        total = share(1, c + 2 * e) + jnp.where(lowz == e, unit1[0], 0.0)
        landed(rxb.at[e], xr.at[1, e])
        rxb[e] = (total + wide(rxb[e]).reshape(BLOCK, D)).astype(BF).reshape(2, 64, D)
        move.send(rxb.at[e], grad_parts.at[1 + deep, lowz], gs.at[2 + e], gr.at[1 + deep, lowz], c + 2 * e, 1)
    done += 2

    def vec_stage(i):
        landed(rv.at[i], vr.at[i])
        total = sv[i] + rv[i]
        if i < 4:
            sv[i + 1] = total
            vec_send(i + 1).start()
        else:
            vec_out[...] = total

    for i in range(5):
        tick(done + i)
        vec_stage(i)
    done += 5

    def rest(n, carry):
        tick(n)
        return carry

    lax.fori_loop(done, CHUNKS + LAGS[-1], rest, 0)

    def close(i, carry):
        first_send(i).wait_send()
        for e in range(2):
            second_send(i, e).wait_send()
        third_send(i).wait_send()

        @pl.when(outer)
        def _():
            outer_send(i).wait_send()
            landed(sums.at[i, 0], tf.at[i, 0])
            landed(sums.at[i, 1], tf.at[i, 1])

        @pl.when(inner)
        def _():
            cross_send(i).wait_send()
            final_near(i).wait_send()
            final_across(i).wait_send()
            final_forward(i).wait_send()

        return carry

    lax.fori_loop(0, CHUNKS, close, 0)
    for i in range(5):
        vec_send(i).wait_send()
    for copy in swap:
        copy.wait_send()
    for slot in range(3):
        landed(lay_out.at[slot], lay_r.at[slot])
        landed(grad_parts.at[slot, 0], gr.at[slot, 0])

    @pl.when(c == 1)
    def _():
        for slot in range(1, 3):
            landed(grad_parts.at[slot, 1], gr.at[slot, 1])

    move.finish()


def whole_layer(tokens, segments, cotangent, weights, vectors):
    vmem, anywhere = pl.BlockSpec(memory_space=pltpu.VMEM), pl.BlockSpec(memory_space=pl.ANY)
    dma = pltpu.SemaphoreType.DMA
    args = (tokens, segments, cotangent) + weights + vectors
    n = CHUNKS
    tok = (3, BLOCK, D)
    square = (16, 48, D)
    buffers = [
        ((EARLY + FFN,) + square, BF),
        ((FFN,) + square, BF),
        ((D, D), BF),
        ((D, D), BF),
        ((D, D), BF),
        ((D, D), BF),
        ((8, D), F32),
        ((8, FFN * FFT), F32),
        ((2, 4, 2, 64, D), BF),
        ((2, 4, 8, BLOCK), jnp.int32),
        (tok, BF),
        (tok, BF),
        ((2, ROW, D), BF),
        ((2, ROW, D), BF),
        (tok, BF),
        (tok, BF),
        ((FFN, 3 * BLOCK, FFT), BF),
        ((FFN, 3 * BLOCK, FFT), BF),
        (tok, F32),
        (tok, F32),
        (tok, BF),
        ((3, BLOCK, ROW), F32),
        ((3, BLOCK, LANES), F32),
        ((3, BLOCK, LANES), F32),
        ((16, D), F32),
        ((n, 8, 48, D), BF),
        ((n, 2, 2, 48, D), BF),
        ((n, 2, 48, D), BF),
        ((n, 2, 48, D), BF),
        ((n, 48, D), BF),
        ((2, 2, 64, D), BF),
        ((2, 2, 64, D), BF),
        ((5, 16, D), F32),
        ((5, 16, D), F32),
    ]
    semaphores = [(21,), (16,), (2, 4, 2), (2, 4), (16,), (2, 4), (6,), (3,)]
    semaphores += [(n,), (n,), (n, 2), (n, 2)] + [(n,)] * 6 + [(n, 3), (n, 2)]
    semaphores += [(3,), (3,), (2, 2), (2, 2), (4,), (3, 2), (5,), (5,)]
    return pl.pallas_call(
        layer_body,
        out_shape=(
            jax.ShapeDtypeStruct((n, 2, 48, D), BF),
            jax.ShapeDtypeStruct((16, D), F32),
            jax.ShapeDtypeStruct(tok, BF),
            jax.ShapeDtypeStruct((3, 2, 2, 64, D), BF),
        ),
        in_specs=[anywhere] * len(args),
        out_specs=[vmem] * 4,
        scratch_shapes=[pltpu.VMEM(s, t) for s, t in buffers] + [dma(s) for s in semaphores],
        compiler_params=pltpu.CompilerParams(
            collective_id=0, has_side_effects=True, vmem_limit_bytes=int(63.9 * MIB)
        ),
    )(*args)


def finish_body(sums, vec, lay, parts, *outs):
    p = lax.rem(lax.axis_index("batch"), 8)
    c = lax.rem(p, 2)
    layer_out, input_grad, g_q, g_k, g_v, g_o, g_inner, g_outer, b_inner = outs[:9]
    layer_out[...] = lay[...]
    input_grad[...] = parts[:, 0].reshape(3, BLOCK, D)

    @pl.when(c == 1)
    def _():
        for slot in range(1, 3):
            both = parts[slot, 0].astype(F32) + parts[slot, 1].astype(F32)
            input_grad[slot] = both.astype(BF).reshape(BLOCK, D)

    def piece(i):
        return sums[i].reshape(96, D).astype(F32)

    for part in range(4):
        g_outer[96 * part : 96 * part + 96] = piece(part)
    for f in range(FFN):
        g_inner[:, f * FFT : (f + 1) * FFT] = piece(4 + f)
    g_o[...] = piece(8)
    g_q[...] = piece(9)
    g_k[...] = piece(10)
    g_v[...] = piece(11)
    pick = lax.broadcasted_iota(jnp.int32, (D, LANES), 0) == lax.broadcasted_iota(jnp.int32, (D, LANES), 1) + 96 * p
    vecs = jnp.dot(
        vec[0:8], pick.astype(F32), preferred_element_type=F32, precision=lax.Precision.HIGHEST
    )
    for i in range(8):
        outs[9 + i][...] = vecs[i, 0:96]
    quarter = vec[pl.ds(8 + p // 2, 1), :]
    b_inner[...] = jnp.where(lax.rem(p, 2) == 0, quarter[:, :384], quarter[:, 384:]).reshape(384)


def finish(sums, vec, lay, parts):
    vmem = pl.BlockSpec(memory_space=pltpu.VMEM)
    tok = (3, BLOCK, D)
    shapes = [
        (tok, BF),
        (tok, BF),
        ((96, D), F32),
        ((96, D), F32),
        ((96, D), F32),
        ((96, D), F32),
        ((96, 4 * D), F32),
        ((384, D), F32),
        ((384,), F32),
    ] + [((96,), F32)] * 8
    return pl.pallas_call(
        finish_body,
        out_shape=tuple(jax.ShapeDtypeStruct(s, t) for s, t in shapes),
        in_specs=[vmem] * 4,
        out_specs=[vmem] * len(shapes),
        compiler_params=pltpu.CompilerParams(vmem_limit_bytes=60 * MIB),
    )(sums, vec, lay, parts)


def per_device(
    groups,
    tokens,
    segment_ids,
    w_query,
    b_query,
    w_key,
    w_value,
    b_value,
    w_out,
    b_out,
    gain_first,
    shift_first,
    w_inner,
    b_inner,
    w_outer,
    b_outer,
    gain_second,
    shift_second,
    cotangent,
):
    weights = (w_query, w_key, w_value, w_out, w_inner.reshape(16, 48, FFN * FFT), w_outer.reshape(FFN, 16, 48, D))
    vectors = (b_query, b_value, b_out, gain_first, shift_first, b_outer, gain_second, shift_second, b_inner)
    reduced = whole_layer(tokens.reshape(3, 2, 64, D), segment_ids, cotangent, weights, vectors)
    layer_out, input_grad, g_q, g_k, g_v, g_o, g_inner, g_outer, g_b_inner, *vecs = finish(*reduced)
    g_b_query, g_b_value, g_b_out, g_gain_first, g_shift_first, g_b_outer, g_gain_second, g_shift_second = vecs
    grads = (
        g_q,
        g_b_query,
        g_k,
        g_v,
        g_b_value,
        g_o,
        g_b_out,
        g_gain_first,
        g_shift_first,
        g_inner,
        g_b_inner,
        g_outer,
        g_b_outer,
        g_gain_second,
        g_shift_second,
    )
    if groups > 1:
        place_at = lax.rem(lax.axis_index("batch"), 8)

        def spread(grad):
            whole = jnp.zeros((8 * grad.shape[0],) + grad.shape[1:], grad.dtype)
            whole = lax.dynamic_update_slice_in_dim(whole, grad, place_at * grad.shape[0], 0)
            return lax.psum_scatter(whole, "batch", scatter_dimension=0, tiled=True)

        grads = tuple(spread(grad) for grad in grads)
    return (layer_out, input_grad) + grads


def solution(mesh):
    tokens = P("batch", "blk", None)
    weight, vector = P("batch", None), P("batch")
    return jax.shard_map(
        functools.partial(per_device, mesh.shape["batch"] // 8),
        mesh=mesh,
        in_specs=(tokens, P("batch", "blk")) + (P(),) * 15 + (tokens,),
        out_specs=(tokens, tokens)
        + (
            weight,
            vector,
            weight,
            weight,
            vector,
            weight,
            vector,
            vector,
            vector,
            weight,
            vector,
            weight,
            vector,
            vector,
            vector,
        ),
        check_vma=False,
    )
```

```python
import functools
import math

import jax
import jax.numpy as jnp
from jax import lax
from jax.experimental import pallas as pl
from jax.experimental.pallas import tpu as pltpu
from jax.sharding import PartitionSpec as P

BF = jnp.bfloat16
F32 = jnp.float32
EPS = 1e-05
D = 768
PAIRS = 6
LANES = 128
BLOCK = 128
ROW = 512
FFT = 768
FFN = 4
EARLY = 9
CHUNKS = 24
LAGS = (0, 2, 4, 7, 10, 13)
MIB = 1 << 20


def dot(a, b):
    return jnp.dot(a, b, preferred_element_type=F32)


def dot_nt(a, b):
    return lax.dot_general(a, b, (((1,), (1,)), ((), ())), preferred_element_type=F32)


def dot_tn(a, b):
    return lax.dot_general(a, b, (((0,), (0,)), ((), ())), preferred_element_type=F32)


def place():
    z = lax.axis_index("blk")
    beta = lax.axis_index("batch")
    c = lax.rem(beta, 2)
    return z, beta, c, beta - c


def at(z, beta):
    return {"blk": z, "batch": beta}


def greet(devices):
    barrier = pltpu.get_barrier_semaphore()
    for device in devices:
        pl.semaphore_signal(barrier, inc=1, device_id=device, device_id_type=pl.DeviceIdType.MESH)
    pl.semaphore_wait(barrier, len(devices))


def column_mates(z, c, base):
    mates = [at(lax.rem(z + step, 4), base + core) for step in range(1, 4) for core in range(2)]
    return mates + [at(z, base + 1 - c)]


def remote(src, dst, send_sem, recv_sem, device):
    return pltpu.make_async_remote_copy(
        src_ref=src,
        dst_ref=dst,
        send_sem=send_sem,
        recv_sem=recv_sem,
        device_id=device,
        device_id_type=pl.DeviceIdType.MESH,
    )


class Mover:
    def __init__(self, z, c, base):
        self.z, self.c, self.base, self.sent = z, c, base, []

    def send(self, src, dst, send_sem, recv_sem, to_z, to_c, when=None):
        self_target = jnp.logical_and(to_z == self.z, to_c == self.c)
        other = jnp.logical_not(self_target)
        if when is not None:
            self_target = jnp.logical_and(self_target, when)
            other = jnp.logical_and(other, when)
        out = remote(src, dst, send_sem, recv_sem, at(to_z, self.base + to_c))

        @pl.when(self_target)
        def _():
            pltpu.make_async_copy(src, dst, recv_sem).start()

        @pl.when(other)
        def _():
            out.start()

        self.sent.append((other, out))

    def finish(self):
        for other, out in self.sent:

            @pl.when(other)
            def _(out=out):
                out.wait_send()

        self.sent = []


def landed(dst, sem):
    pltpu.make_async_copy(dst, dst, sem).wait()


def lane_low():
    return lax.broadcasted_iota(jnp.int32, (BLOCK, LANES), 1) < 64


def stack_heads(pair, low):
    zero = jnp.zeros_like(pair)
    return jnp.concatenate([jnp.where(low, pair, zero), jnp.where(low, zero, pair)], axis=0)


def merge_heads(both, low):
    return jnp.where(low, both[:BLOCK], both[BLOCK:])


def moments(resid):
    center = resid - jnp.mean(resid, axis=-1, keepdims=True)
    inverse = lax.rsqrt(jnp.mean(center * center, axis=-1, keepdims=True) + EPS)
    return center * inverse, inverse


def norm_back(upstream, unit, inverse, gain):
    scaled = upstream * gain
    return inverse * (
        scaled
        - jnp.mean(scaled, axis=-1, keepdims=True)
        - unit * jnp.mean(scaled * unit, axis=-1, keepdims=True)
    )


def column_sum(value):
    return jnp.sum(value, axis=0, keepdims=True)


def layer_body(
    tok,
    seg,
    cot,
    w_query_in,
    w_key_in,
    w_value_in,
    w_out_in,
    w_inner_in,
    w_outer_in,
    b_query_in,
    b_value_in,
    b_out_in,
    gain_first_in,
    shift_first_in,
    b_outer_in,
    gain_second_in,
    shift_second_in,
    b_inner_in,
    sums,
    vec_out,
    lay_out,
    grad_parts,
    pool,
    w_outer,
    w_query,
    w_key,
    w_value,
    w_out,
    rows,
    b_inner,
    x,
    segs,
    cotq,
    q,
    k,
    v,
    att,
    low1,
    act,
    slope,
    acc,
    unit1,
    d_out,
    bias,
    lse,
    inv1,
    vec,
    r1,
    r2,
    r3,
    ro,
    rj,
    rxa,
    rxb,
    sv,
    rv,
    w_sem,
    d_send,
    d_recv,
    f_send,
    g_send,
    g_recv,
    c_send,
    c_recv,
    s1,
    t1,
    s2,
    t2,
    s3,
    t3,
    so,
    to,
    tj,
    sf,
    tf,
    lay_s,
    lay_r,
    xs,
    xr,
    gs,
    gr,
    vs,
    vr,
):
    z, beta, c, base = place()
    low = lane_low()
    tokens = 3 * BLOCK
    bx, by = lax.rem(beta // 2, 2), lax.rem(beta // 4, 2)
    sibling = at(z, base + 1 - c)
    to_x, to_y = at(z, beta + 2 - 4 * bx), at(z, beta + 4 - 8 * by)
    inner = jnp.logical_and(z > 0, z < 3)
    outer = jnp.logical_not(inner)
    near = at(jnp.where(z < 2, 1 - z, 5 - z), beta)
    across = at(jnp.where(z == 1, 2, 1), beta)
    deep, lowz = z // 2, lax.rem(z, 2)

    loads = []

    def load(src, dst):
        copy = pltpu.make_async_copy(src, dst, w_sem.at[len(loads)])
        copy.start()
        loads.append(copy)
        return copy

    greet(column_mates(z, c, base) + [to_x, to_y])
    move = Mover(z, c, base)
    first, second = c == 0, c == 1
    routes = [(s, 0, s, first) for s in range(3)] + [
        (0, 0, 3, second),
        (1, 1, 0, second),
        (1, 1, 1, second),
        (2, 1, 2, second),
        (2, 1, 3, second),
    ]
    counts = iter(range(16))

    def send_rows(which):
        for slot, ab, chip, when in routes:
            if ab == which:
                for half in range(2):
                    n = next(counts)
                    move.send(
                        tok.at[slot, half], x.at[ab, z, half], d_send.at[n], d_recv.at[ab, z, half], chip, half, when
                    )
                    move.send(seg.at[slot], segs.at[ab, z, 0], g_send.at[n], g_recv.at[ab, z], chip, half, when)

    send_rows(0)
    got_key = load(w_key_in, w_key)
    got_value = load(w_value_in, w_value)
    got_query = load(w_query_in, w_query)
    vectors = [b_query_in, b_value_in, b_out_in, gain_first_in, shift_first_in, b_outer_in, gain_second_in]
    got_rows = [load(ref, rows.at[i]) for i, ref in enumerate(vectors + [shift_second_in])]
    got_rows.append(load(b_inner_in, b_inner.at[0]))
    got_out = load(w_out_in, w_out)
    got_inner = [load(w_inner_in.at[:, :, f * FFT : (f + 1) * FFT], pool.at[EARLY + f]) for f in range(FFN)]
    got_outer = [load(w_outer_in.at[f], w_outer.at[f]) for f in range(FFN)]

    b_query, b_value, b_out, gain_first, shift_first, b_outer, gain_second, shift_second = (
        rows.at[i : i + 1] for i in range(8)
    )
    vec[...] = jnp.zeros_like(vec)
    forwards = []

    def forward_rows(ab):
        for b in range(4):
            landed(x.at[ab, b, c], d_recv.at[ab, b, c])
            copy = remote(x.at[ab, b, c], x.at[ab, b, c], f_send.at[ab, b], d_recv.at[ab, b, c], sibling)
            copy.start()
            forwards.append(copy)

    def send_cotangents():
        for slot in range(3):
            move.send(cot.at[slot], cotq.at[lowz], c_send.at[slot], c_recv.at[lowz], slot, deep, first)
        move.send(cot.at[0], cotq.at[lowz], c_send.at[3], c_recv.at[lowz], 3, deep, second)
        move.send(cot.at[1], cotq.at[2], c_send.at[4], c_recv.at[2], deep, lowz, second)
        move.send(cot.at[2], cotq.at[2], c_send.at[5], c_recv.at[2], 2 + deep, lowz, second)

    forward_rows(0)
    send_rows(1)
    own_blocks = [(0, 2 * c), (0, 2 * c + 1), (1, 2 * lowz + c)]

    def own_tokens(u):
        ab, b = own_blocks[u]
        return x[ab, b].reshape(BLOCK, D)

    def one_hot(row):
        return (lax.broadcasted_iota(jnp.int32, (8, BLOCK), 0) == row).astype(F32)

    got_key.wait()
    got_value.wait()
    got_query.wait()
    for copy in got_rows:
        copy.wait()
    def project(ab):
        for b in range(4):
            landed(x.at[ab, b, 1 - c], d_recv.at[ab, b, 1 - c])
            landed(segs.at[ab, b, 0], g_recv.at[ab, b])
        xk = x[ab].reshape(ROW, D)
        k[ab] = dot(xk, w_key[...]).astype(BF)
        v[ab] = (dot(xk, w_value[...]) + b_value[...]).astype(BF)
        for u, (row, b) in enumerate(own_blocks):
            if row == ab:
                q[u] = ((dot(own_tokens(u), w_query[...]) + b_query[...]).astype(BF) * 0.125).astype(BF)
                own_hot = one_hot(segs[ab, b, 0:1])
                for kb in range(4):
                    same = dot_tn(own_hot, one_hot(segs[ab, kb, 0:1]))
                    bias[u, :, kb * BLOCK : (kb + 1) * BLOCK] = jnp.where(same > 0.5, 0.0, -1e30)

    def lanes(j):
        return pl.ds(pl.multiple_of(j * LANES, LANES), LANES)

    lane = lax.broadcasted_iota(jnp.int32, (BLOCK, LANES), 1)

    def scores(u, cols, keys):
        score = dot_nt(stack_heads(q[u, :, cols], low), keys)
        return (score.reshape(2, BLOCK, ROW) + bias[u][None]).reshape(2 * BLOCK, ROW)

    def attend(n, carry):
        u, j = n // PAIRS, lax.rem(n, PAIRS)
        ab, cols = u // 2, lanes(j)
        score = scores(u, cols, k[ab, :, cols])
        top = jnp.max(score, axis=-1, keepdims=True)
        expo = jnp.exp(score - top)
        total = jnp.sum(expo, axis=-1, keepdims=True)
        p = (expo * (1.0 / total)).astype(BF)
        stat = top + jnp.log(total)
        lse[u] = jnp.where(lane == 2 * j, stat[:BLOCK], jnp.where(lane == 2 * j + 1, stat[BLOCK:], lse[u]))
        att[u, :, cols] = merge_heads(dot(p, v[ab, :, cols]), low).astype(BF)
        return carry

    lse[...] = jnp.zeros_like(lse)
    project(0)
    lax.fori_loop(0, 2 * PAIRS, attend, 0)
    forward_rows(1)
    send_cotangents()
    project(1)
    for copy in forwards:
        copy.wait_send()
    lax.fori_loop(2 * PAIRS, 3 * PAIRS, attend, 0)

    got_out.wait()
    acc[...] = dot(att[...].reshape(tokens, D), w_out[...]).reshape(3, BLOCK, D)
    for u in range(3):
        resid = own_tokens(u).astype(F32) + acc[u] + b_out[...]
        unit, inverse = moments(resid)
        unit1[u] = unit
        inv1[u] = jnp.broadcast_to(inverse, (BLOCK, LANES))
        low1[u] = (unit * gain_first[...] + shift_first[...]).astype(BF)
    acc[...] = jnp.zeros_like(acc)
    for copy in got_inner + got_outer:
        copy.wait()

    def inner_weight(f):
        return pool[EARLY + f].reshape(D, FFT)

    def outer_weight(f):
        return w_outer[f].reshape(FFT, D)

    def feed(f, carry):
        cols = pl.ds(pl.multiple_of(f * FFT, FFT), FFT)
        pre = dot(low1[...].reshape(tokens, D), inner_weight(f)) + b_inner[0:1, cols]
        half = 0.5 * (1.0 + lax.erf(pre * (1.0 / math.sqrt(2.0))))
        slope[f] = (half + pre * jnp.exp(-0.5 * pre * pre) * (1.0 / math.sqrt(2.0 * math.pi))).astype(BF)
        act_low = (pre * half).astype(BF)
        act[f] = act_low
        acc[...] += dot(act_low, outer_weight(f)).reshape(3, BLOCK, D)
        return carry

    lax.fori_loop(0, FFN, feed, 0)

    for slot in range(3):
        landed(cotq.at[slot], c_recv.at[slot])
    for u in range(3):
        resid = unit1[u] * gain_first[...] + shift_first[...] + acc[u] + b_outer[...]
        unit, inverse = moments(resid)
        up = cotq[u].astype(F32)
        cotq[u] = (unit * gain_second[...] + shift_second[...]).astype(BF)
        d_second = norm_back(up, unit, inverse, gain_second[...])
        d_low = d_second.astype(BF)
        acc[u] = d_second
        d_out[u] = d_low
        vec[5:6] += column_sum(d_low.astype(F32))
        vec[6:7] += column_sum(up * unit)
        vec[7:8] += column_sum(up)

    row_core = jnp.where(z == 3, 1, 0)
    row_slot = lax.rem(z, 3)
    move.send(cotq.at[0], lay_out.at[row_slot], lay_s.at[0], lay_r.at[row_slot], 2 * c, row_core)
    move.send(cotq.at[1], lay_out.at[row_slot], lay_s.at[1], lay_r.at[row_slot], 2 * c + 1, row_core)
    move.send(cotq.at[2], lay_out.at[1 + deep], lay_s.at[2], lay_r.at[1 + deep], 2 * lowz + c, 1)

    def split(i):
        t = lax.rem(i, 2)
        return t, 1 - t

    def sent_piece(i, e):
        t, s = split(i)
        return t * (2 * (1 - by) + e) + s * (2 * e + 1 - bx)

    def kept_piece(i, e):
        t, s = split(i)
        return t * (2 * by + e) + s * (2 * e + bx)

    def second_to(i):
        t, s = split(i)
        return at(z, beta + s * (2 - 4 * bx) + t * (4 - 8 * by))

    def third_to(i):
        t, s = split(i)
        return at(z, beta + t * (2 - 4 * bx) + s * (4 - 8 * by))

    def kept_half(i):
        t, s = split(i)
        return t * bx + s * by

    def finisher(i):
        return z == 1 + lax.rem(i // 2, 2)

    def helper(i):
        return z == 2 - lax.rem(i // 2, 2)

    def place_in(i):
        return i // 2, 8 * lax.rem(i, 2)

    def first_send(i):
        chunk, row = place_in(i)
        return remote(pool.at[chunk, pl.ds(row + 4 * (1 - c), 4)], r1.at[i], s1.at[i], t1.at[i], sibling)

    def second_send(i, e):
        return remote(r1.at[i, sent_piece(i, e)], r2.at[i, e], s2.at[i, e], t2.at[i, e], second_to(i))

    def third_send(i):
        return remote(r2.at[i, 1 - kept_half(i)], r3.at[i], s3.at[i], t3.at[i], third_to(i))

    def outer_send(i):
        return remote(r3.at[i], ro.at[i], so.at[i], to.at[i], near)

    def crossed(i):
        return 2 * (i // 4) + lax.rem(i, 2)

    def cross_send(i):
        return remote(r3.at[i], rj.at[crossed(i)], so.at[i], tj.at[crossed(i)], across)

    def final_near(i):
        return remote(sums.at[i], sums.at[i], sf.at[i, 0], tf.at[i], near)

    def final_across(i):
        return remote(sums.at[i], sums.at[i], sf.at[i, 1], tf.at[i], across)

    def wide(value):
        return value.astype(F32)

    def pair_sum(i, p):
        chunk, row = place_in(i)
        return wide(r1[i, p]) + wide(pool[chunk, row + 4 * c + p])

    def stage2(i):
        landed(r1.at[i], t1.at[i])
        for order in range(2):
            e = lax.rem(1 - kept_half(i) + order, 2)
            p = sent_piece(i, e)
            r1[i, p] = pair_sum(i, p).astype(BF)
            second_send(i, e).start()

    def stage3(i):
        e = 1 - kept_half(i)
        landed(r2.at[i, e], t2.at[i, e])
        r2[i, e] = (wide(r2[i, e]) + pair_sum(i, kept_piece(i, e))).astype(BF)
        third_send(i).start()

    def stage4(i):
        e = kept_half(i)
        landed(r2.at[i, e], t2.at[i, e])
        landed(r3.at[i], t3.at[i])
        r3[i] = (wide(r2[i, e]) + pair_sum(i, kept_piece(i, e)) + wide(r3[i])).astype(BF)

        @pl.when(outer)
        def _():
            outer_send(i).start()

    def stage5(i):
        @pl.when(helper(i))
        def _():
            landed(ro.at[i], to.at[i])
            r3[i] = (wide(r3[i]) + wide(ro[i])).astype(BF)
            cross_send(i).start()

    def stage6(i):
        @pl.when(finisher(i))
        def _():
            landed(ro.at[i], to.at[i])
            landed(rj.at[crossed(i)], tj.at[crossed(i)])
            sums[i] = (wide(r3[i]) + wide(ro[i]) + wide(rj[crossed(i)])).astype(BF)
            final_near(i).start()
            final_across(i).start()

    def stage7(i):
        @pl.when(helper(i))
        def _():
            landed(sums.at[i], tf.at[i])
            final_near(i).start()

    stages = list(zip((stage2, stage3, stage4, stage5, stage6, stage7), LAGS))

    def tick(n):
        for stage, lag in stages:
            i = n - lag

            @pl.when(jnp.logical_and(i >= 0, i < CHUNKS))
            def _(i=i, stage=stage):
                stage(i)

    up_all = d_out[...].reshape(tokens, D)
    for f in range(FFN):
        g_outer = dot_tn(act[f], up_all).astype(BF)
        for piece in range(2):
            for part in range(4):
                for half in range(2):
                    row = 384 * piece + 96 * part + 48 * half
                    pool[part, 8 * half + 4 * piece + f] = g_outer[row : row + 48]
    for i in range(8):
        first_send(i).start()

    def keep_rows(i, grad):
        low_grad = grad.astype(BF)
        for p in range(8):
            for half in range(2):
                row = 96 * p + 48 * half
                pool[i, 8 * half + 4 * (p % 2) + p // 2] = low_grad[row : row + 48]
        for half in range(2):
            first_send(2 * i + half).start()

    def feed_back(f, carry):
        up = d_out[...].reshape(tokens, D)
        d_pre = (dot_nt(up, outer_weight(f)) * slope[f].astype(F32)).astype(BF)
        vec[pl.ds(8 + f, 1)] = column_sum(d_pre.astype(F32))
        keep_rows(4 + f, dot_tn(low1[...].reshape(tokens, D), d_pre))
        acc[...] += dot_nt(d_pre, inner_weight(f)).reshape(3, BLOCK, D)
        tick(f)
        return carry

    lax.fori_loop(0, FFN, feed_back, 0)

    for u in range(3):
        up = acc[u]
        d_first = norm_back(up, unit1[u], inv1[u][:, 0:1], gain_first[...])
        acc[u] = d_first
        d_low = d_first.astype(BF)
        d_out[u] = d_low
        vec[2:3] += column_sum(d_low.astype(F32))
        vec[3:4] += column_sum(up * unit1[u])
        vec[4:5] += column_sum(up)
    up_all = d_out[...].reshape(tokens, D)
    keep_rows(8, dot_tn(att[...].reshape(tokens, D), up_all))
    d_out[...] = dot_nt(up_all, w_out[...]).astype(BF).reshape(3, BLOCK, D)
    tick(FFN)

    def attend_back(j):
        cols = lanes(j)
        for ab in range(2):
            keys, values = k[ab, :, cols], v[ab, :, cols]
            g_key = g_value = None
            for u in (0, 1) if ab == 0 else (2,):
                q_both = stack_heads(q[u, :, cols], low)
                score = dot_nt(q_both, keys)
                score = (score.reshape(2, BLOCK, ROW) + bias[u][None]).reshape(2 * BLOCK, ROW)
                even = jnp.sum(jnp.where(lane == 2 * j, lse[u], 0.0), axis=-1, keepdims=True)
                odd = jnp.sum(jnp.where(lane == 2 * j + 1, lse[u], 0.0), axis=-1, keepdims=True)
                p = jnp.exp(score - jnp.concatenate([even, odd], axis=0))
                d_pair = d_out[u, :, cols]
                d_both = stack_heads(d_pair, low)
                product = wide(d_pair) * wide(att[u, :, cols])
                even = jnp.sum(jnp.where(low, product, 0.0), axis=-1, keepdims=True)
                odd = jnp.sum(jnp.where(low, 0.0, product), axis=-1, keepdims=True)
                d_prob = dot_nt(d_both, values)
                d_score = (p * (d_prob - jnp.concatenate([even, odd], axis=0))).astype(BF)
                one_key = dot(q_both.T, d_score)
                one_value = dot(d_both.T, p.astype(BF))
                g_key = one_key if g_key is None else g_key + one_key
                g_value = one_value if g_value is None else g_value + one_value
                q[u, :, cols] = (merge_heads(dot(d_score, keys), low) * 0.125).astype(BF)
            k[ab, :, cols] = g_key.astype(BF).T
            v[ab, :, cols] = g_value.astype(BF).T

    def step(j, carry):
        attend_back(j)

        tick(FFN + 1 + j)
        return carry

    lax.fori_loop(0, PAIRS, step, 0)
    done = FFN + 1 + PAIRS

    keep_rows(9, sum(dot_tn(own_tokens(u), q[u]) for u in range(3)))
    tick(done)
    for i, grads in ((10, k), (11, v)):
        keep_rows(i, sum(dot_tn(x[ab].reshape(ROW, D), grads[ab]) for ab in range(2)))
        tick(done + i - 9)
    done += 2
    sv[0] = vec[...]
    sv[0, 0:1] = sum(column_sum(wide(q[u])) for u in range(3))
    sv[0, 1:2] = sum(column_sum(wide(v[ab])) for ab in range(2))
    vec_to = [sibling, to_x, to_y, at(z + 1 - 2 * lowz, beta), at(z + 2 - 4 * deep, beta)]

    def vec_send(i):
        return remote(sv.at[i], rv.at[i], vs.at[i], vr.at[i], vec_to[i])

    vec_send(0).start()

    def share(ab, b):
        rows_b = pl.ds(pl.multiple_of(b * BLOCK, BLOCK), BLOCK)
        return dot_nt(k[ab, rows_b, :], w_key[...]) + dot_nt(v[ab, rows_b, :], w_value[...])

    def query_share(u):
        return dot_nt(q[u], w_query[...]) + acc[u]

    def put(ab, b, value):
        x[ab, b] = value.astype(BF).reshape(2, 64, D)

    swap = []
    for e in range(2):
        b = 2 * (1 - c) + e
        put(0, b, share(0, b))
        swap.append(remote(x.at[0, b], rxa.at[e], xs.at[0, e], xr.at[0, e], sibling))
        swap[-1].start()
    for e in range(2):
        b = 1 - c + 2 * e
        put(1, b, share(1, b))
        swap.append(remote(x.at[1, b], rxb.at[e], xs.at[1, e], xr.at[1, e], sibling))
        swap[-1].start()
    tick(done + 1)
    for e in range(2):
        total = share(0, 2 * c + e) + query_share(e)
        landed(rxa.at[e], xr.at[0, e])
        rxa[e] = (total + wide(rxa[e]).reshape(BLOCK, D)).astype(BF).reshape(2, 64, D)
        move.send(rxa.at[e], grad_parts.at[row_slot, 0], gs.at[e], gr.at[row_slot, 0], 2 * c + e, row_core)
    unit1[0] = query_share(2)
    for e in range(2):
        total = share(1, c + 2 * e) + jnp.where(lowz == e, unit1[0], 0.0)
        landed(rxb.at[e], xr.at[1, e])
        rxb[e] = (total + wide(rxb[e]).reshape(BLOCK, D)).astype(BF).reshape(2, 64, D)
        move.send(rxb.at[e], grad_parts.at[1 + deep, lowz], gs.at[2 + e], gr.at[1 + deep, lowz], c + 2 * e, 1)
    done += 2

    def vec_stage(i):
        landed(rv.at[i], vr.at[i])
        total = sv[i] + rv[i]
        if i < 4:
            sv[i + 1] = total
            vec_send(i + 1).start()
        else:
            vec_out[...] = total

    for i in range(5):
        tick(done + i)
        vec_stage(i)
    done += 5

    def rest(n, carry):
        tick(n)
        return carry

    lax.fori_loop(done, CHUNKS + LAGS[-1], rest, 0)

    def close(i, carry):
        first_send(i).wait_send()
        for e in range(2):
            second_send(i, e).wait_send()
        third_send(i).wait_send()

        @pl.when(outer)
        def _():
            outer_send(i).wait_send()
            landed(sums.at[i], tf.at[i])

        @pl.when(inner)
        def _():
            final_near(i).wait_send()

        @pl.when(finisher(i))
        def _():
            final_across(i).wait_send()

        @pl.when(helper(i))
        def _():
            cross_send(i).wait_send()

        return carry

    lax.fori_loop(0, CHUNKS, close, 0)
    for i in range(5):
        vec_send(i).wait_send()
    for copy in swap:
        copy.wait_send()
    for slot in range(3):
        landed(lay_out.at[slot], lay_r.at[slot])
        landed(grad_parts.at[slot, 0], gr.at[slot, 0])

    @pl.when(c == 1)
    def _():
        for slot in range(1, 3):
            landed(grad_parts.at[slot, 1], gr.at[slot, 1])

    move.finish()


def whole_layer(tokens, segments, cotangent, weights, vectors):
    vmem, anywhere = pl.BlockSpec(memory_space=pltpu.VMEM), pl.BlockSpec(memory_space=pl.ANY)
    dma = pltpu.SemaphoreType.DMA
    args = (tokens, segments, cotangent) + weights + vectors
    n = CHUNKS
    tok = (3, BLOCK, D)
    square = (16, 48, D)
    buffers = [
        ((EARLY + FFN,) + square, BF),
        ((FFN,) + square, BF),
        ((D, D), BF),
        ((D, D), BF),
        ((D, D), BF),
        ((D, D), BF),
        ((8, D), F32),
        ((8, FFN * FFT), F32),
        ((2, 4, 2, 64, D), BF),
        ((2, 4, 8, BLOCK), jnp.int32),
        (tok, BF),
        (tok, BF),
        ((2, ROW, D), BF),
        ((2, ROW, D), BF),
        (tok, BF),
        (tok, BF),
        ((FFN, 3 * BLOCK, FFT), BF),
        ((FFN, 3 * BLOCK, FFT), BF),
        (tok, F32),
        (tok, F32),
        (tok, BF),
        ((3, BLOCK, ROW), F32),
        ((3, BLOCK, LANES), F32),
        ((3, BLOCK, LANES), F32),
        ((16, D), F32),
        ((n, 4, 48, D), BF),
        ((n, 2, 48, D), BF),
        ((n, 48, D), BF),
        ((n, 48, D), BF),
        ((n // 2, 48, D), BF),
        ((2, 2, 64, D), BF),
        ((2, 2, 64, D), BF),
        ((5, 16, D), F32),
        ((5, 16, D), F32),
    ]
    semaphores = [(21,), (16,), (2, 4, 2), (2, 4), (16,), (2, 4), (6,), (3,)]
    semaphores += [(n,), (n,), (n, 2), (n, 2)] + [(n,)] * 4 + [(n // 2,), (n, 2), (n,)]
    semaphores += [(3,), (3,), (2, 2), (2, 2), (4,), (3, 2), (5,), (5,)]
    return pl.pallas_call(
        layer_body,
        out_shape=(
            jax.ShapeDtypeStruct((n, 48, D), BF),
            jax.ShapeDtypeStruct((16, D), F32),
            jax.ShapeDtypeStruct(tok, BF),
            jax.ShapeDtypeStruct((3, 2, 2, 64, D), BF),
        ),
        in_specs=[anywhere] * len(args),
        out_specs=[vmem] * 4,
        scratch_shapes=[pltpu.VMEM(s, t) for s, t in buffers] + [dma(s) for s in semaphores],
        compiler_params=pltpu.CompilerParams(
            collective_id=0, has_side_effects=True, vmem_limit_bytes=int(63.9 * MIB)
        ),
    )(*args)


def finish_body(sums, vec, lay, parts, *outs):
    p = lax.rem(lax.axis_index("batch"), 8)
    c = lax.rem(p, 2)
    layer_out, input_grad, g_q, g_k, g_v, g_o, g_inner, g_outer, b_inner = outs[:9]
    layer_out[...] = lay[...]
    input_grad[...] = parts[:, 0].reshape(3, BLOCK, D)

    @pl.when(c == 1)
    def _():
        for slot in range(1, 3):
            both = parts[slot, 0].astype(F32) + parts[slot, 1].astype(F32)
            input_grad[slot] = both.astype(BF).reshape(BLOCK, D)

    def piece(i):
        return sums[2 * i : 2 * i + 2].reshape(96, D).astype(F32)

    for part in range(4):
        g_outer[96 * part : 96 * part + 96] = piece(part)
    for f in range(FFN):
        g_inner[:, f * FFT : (f + 1) * FFT] = piece(4 + f)
    g_o[...] = piece(8)
    g_q[...] = piece(9)
    g_k[...] = piece(10)
    g_v[...] = piece(11)
    pick = lax.broadcasted_iota(jnp.int32, (D, LANES), 0) == lax.broadcasted_iota(jnp.int32, (D, LANES), 1) + 96 * p
    vecs = jnp.dot(
        vec[0:8], pick.astype(F32), preferred_element_type=F32, precision=lax.Precision.HIGHEST
    )
    for i in range(8):
        outs[9 + i][...] = vecs[i, 0:96]
    quarter = vec[pl.ds(8 + p // 2, 1), :]
    b_inner[...] = jnp.where(lax.rem(p, 2) == 0, quarter[:, :384], quarter[:, 384:]).reshape(384)


def finish(sums, vec, lay, parts):
    vmem = pl.BlockSpec(memory_space=pltpu.VMEM)
    tok = (3, BLOCK, D)
    shapes = [
        (tok, BF),
        (tok, BF),
        ((96, D), F32),
        ((96, D), F32),
        ((96, D), F32),
        ((96, D), F32),
        ((96, 4 * D), F32),
        ((384, D), F32),
        ((384,), F32),
    ] + [((96,), F32)] * 8
    return pl.pallas_call(
        finish_body,
        out_shape=tuple(jax.ShapeDtypeStruct(s, t) for s, t in shapes),
        in_specs=[vmem] * 4,
        out_specs=[vmem] * len(shapes),
        compiler_params=pltpu.CompilerParams(vmem_limit_bytes=60 * MIB),
    )(sums, vec, lay, parts)


def per_device(
    groups,
    tokens,
    segment_ids,
    w_query,
    b_query,
    w_key,
    w_value,
    b_value,
    w_out,
    b_out,
    gain_first,
    shift_first,
    w_inner,
    b_inner,
    w_outer,
    b_outer,
    gain_second,
    shift_second,
    cotangent,
):
    weights = (w_query, w_key, w_value, w_out, w_inner.reshape(16, 48, FFN * FFT), w_outer.reshape(FFN, 16, 48, D))
    vectors = (b_query, b_value, b_out, gain_first, shift_first, b_outer, gain_second, shift_second, b_inner)
    reduced = whole_layer(tokens.reshape(3, 2, 64, D), segment_ids, cotangent, weights, vectors)
    layer_out, input_grad, g_q, g_k, g_v, g_o, g_inner, g_outer, g_b_inner, *vecs = finish(*reduced)
    g_b_query, g_b_value, g_b_out, g_gain_first, g_shift_first, g_b_outer, g_gain_second, g_shift_second = vecs
    grads = (
        g_q,
        g_b_query,
        g_k,
        g_v,
        g_b_value,
        g_o,
        g_b_out,
        g_gain_first,
        g_shift_first,
        g_inner,
        g_b_inner,
        g_outer,
        g_b_outer,
        g_gain_second,
        g_shift_second,
    )
    if groups > 1:
        place_at = lax.rem(lax.axis_index("batch"), 8)

        def spread(grad):
            whole = jnp.zeros((8 * grad.shape[0],) + grad.shape[1:], grad.dtype)
            whole = lax.dynamic_update_slice_in_dim(whole, grad, place_at * grad.shape[0], 0)
            return lax.psum_scatter(whole, "batch", scatter_dimension=0, tiled=True)

        grads = tuple(spread(grad) for grad in grads)
    return (layer_out, input_grad) + grads


def solution(mesh):
    tokens = P("batch", "blk", None)
    weight, vector = P("batch", None), P("batch")
    return jax.shard_map(
        functools.partial(per_device, mesh.shape["batch"] // 8),
        mesh=mesh,
        in_specs=(tokens, P("batch", "blk")) + (P(),) * 15 + (tokens,),
        out_specs=(tokens, tokens)
        + (
            weight,
            vector,
            weight,
            weight,
            vector,
            weight,
            vector,
            vector,
            vector,
            weight,
            vector,
            weight,
            vector,
            vector,
            vector,
        ),
        check_vma=False,
    )
```

```python
import functools
import math

import jax
import jax.numpy as jnp
from jax import lax
from jax.experimental import pallas as pl
from jax.experimental.pallas import tpu as pltpu
from jax.sharding import PartitionSpec as P

BF = jnp.bfloat16
F32 = jnp.float32
EPS = 1e-05
D = 768
PAIRS = 6
LANES = 128
BLOCK = 128
ROW = 512
FFT = 768
FFN = 4
EARLY = 9
CHUNKS = 24
ORDER = "".join(
    (
        "BF2Y2Y2FW32F3F2Y43L3224A34A3452A34552A643A53645A56W5646X7262",
        "7264WT33T7277752WO4352T72T52q323k3244vV536246344V56363527573",
        "6V5274247554643V67562546677336746V37755745764455667667777",
    )
)
KINDS = "234567BFLAXTWOqkvYV"
LOOPED = "FAT"
MIB = 1 << 20


def dot(a, b):
    return jnp.dot(a, b, preferred_element_type=F32)


def dot_nt(a, b):
    return lax.dot_general(a, b, (((1,), (1,)), ((), ())), preferred_element_type=F32)


def dot_tn(a, b):
    return lax.dot_general(a, b, (((0,), (0,)), ((), ())), preferred_element_type=F32)


def place():
    z = lax.axis_index("blk")
    beta = lax.axis_index("batch")
    c = lax.rem(beta, 2)
    return z, beta, c, beta - c


def at(z, beta):
    return {"blk": z, "batch": beta}


def greet(devices):
    barrier = pltpu.get_barrier_semaphore()
    for device in devices:
        pl.semaphore_signal(barrier, inc=1, device_id=device, device_id_type=pl.DeviceIdType.MESH)
    pl.semaphore_wait(barrier, len(devices))


def column_mates(z, c, base):
    mates = [at(lax.rem(z + step, 4), base + core) for step in range(1, 4) for core in range(2)]
    return mates + [at(z, base + 1 - c)]


def remote(src, dst, send_sem, recv_sem, device):
    return pltpu.make_async_remote_copy(
        src_ref=src,
        dst_ref=dst,
        send_sem=send_sem,
        recv_sem=recv_sem,
        device_id=device,
        device_id_type=pl.DeviceIdType.MESH,
    )


class Mover:
    def __init__(self, z, c, base):
        self.z, self.c, self.base, self.sent = z, c, base, []

    def send(self, src, dst, send_sem, recv_sem, to_z, to_c, when=None):
        self_target = jnp.logical_and(to_z == self.z, to_c == self.c)
        other = jnp.logical_not(self_target)
        if when is not None:
            self_target = jnp.logical_and(self_target, when)
            other = jnp.logical_and(other, when)
        out = remote(src, dst, send_sem, recv_sem, at(to_z, self.base + to_c))

        @pl.when(self_target)
        def _():
            pltpu.make_async_copy(src, dst, recv_sem).start()

        @pl.when(other)
        def _():
            out.start()

        self.sent.append((other, out))

    def finish(self):
        for other, out in self.sent:

            @pl.when(other)
            def _(out=out):
                out.wait_send()

        self.sent = []


def landed(dst, sem):
    pltpu.make_async_copy(dst, dst, sem).wait()


def lane_low():
    return lax.broadcasted_iota(jnp.int32, (BLOCK, LANES), 1) < 64


def stack_heads(pair, low):
    zero = jnp.zeros_like(pair)
    return jnp.concatenate([jnp.where(low, pair, zero), jnp.where(low, zero, pair)], axis=0)


def merge_heads(both, low):
    return jnp.where(low, both[:BLOCK], both[BLOCK:])


def moments(resid):
    center = resid - jnp.mean(resid, axis=-1, keepdims=True)
    inverse = lax.rsqrt(jnp.mean(center * center, axis=-1, keepdims=True) + EPS)
    return center * inverse, inverse


def norm_back(upstream, unit, inverse, gain):
    scaled = upstream * gain
    return inverse * (
        scaled
        - jnp.mean(scaled, axis=-1, keepdims=True)
        - unit * jnp.mean(scaled * unit, axis=-1, keepdims=True)
    )


def column_sum(value):
    return jnp.sum(value, axis=0, keepdims=True)


def layer_body(
    tok,
    seg,
    cot,
    w_query_in,
    w_key_in,
    w_value_in,
    w_out_in,
    w_inner_in,
    w_outer_in,
    b_query_in,
    b_value_in,
    b_out_in,
    gain_first_in,
    shift_first_in,
    b_outer_in,
    gain_second_in,
    shift_second_in,
    b_inner_in,
    sums,
    vec_out,
    lay_out,
    grad_parts,
    pool,
    w_outer,
    w_query,
    w_key,
    w_value,
    w_out,
    rows,
    b_inner,
    x,
    segs,
    cotq,
    q,
    k,
    v,
    att,
    low1,
    act,
    slope,
    acc,
    unit1,
    d_out,
    bias,
    lse,
    inv1,
    vec,
    r1,
    r2,
    r3,
    ro,
    rj,
    rxa,
    sv,
    rv,
    w_sem,
    d_send,
    d_recv,
    f_send,
    g_send,
    g_recv,
    c_send,
    c_recv,
    s1,
    t1,
    s2,
    t2,
    s3,
    t3,
    so,
    to,
    tj,
    sf,
    tf,
    lay_s,
    lay_r,
    xs,
    xr,
    gs,
    gr,
    vs,
    vr,
):
    z, beta, c, base = place()
    low = lane_low()
    tokens = 3 * BLOCK
    bx, by = lax.rem(beta // 2, 2), lax.rem(beta // 4, 2)
    sibling = at(z, base + 1 - c)
    to_x, to_y = at(z, beta + 2 - 4 * bx), at(z, beta + 4 - 8 * by)
    inner = jnp.logical_and(z > 0, z < 3)
    outer = jnp.logical_not(inner)
    near = at(jnp.where(z < 2, 1 - z, 5 - z), beta)
    across = at(jnp.where(z == 1, 2, 1), beta)
    deep, lowz = z // 2, lax.rem(z, 2)

    loads = []

    def load(src, dst):
        copy = pltpu.make_async_copy(src, dst, w_sem.at[len(loads)])
        copy.start()
        loads.append(copy)
        return copy

    greet(column_mates(z, c, base) + [to_x, to_y])
    move = Mover(z, c, base)
    first, second = c == 0, c == 1
    routes = [(s, 0, s, first) for s in range(3)] + [
        (0, 0, 3, second),
        (1, 1, 0, second),
        (1, 1, 1, second),
        (2, 1, 2, second),
        (2, 1, 3, second),
    ]
    counts = iter(range(16))

    def send_rows(which):
        for slot, ab, chip, when in routes:
            if ab == which:
                for half in range(2):
                    n = next(counts)
                    move.send(
                        tok.at[slot, half], x.at[ab, z, half], d_send.at[n], d_recv.at[ab, z, half], chip, half, when
                    )
                    move.send(seg.at[slot], segs.at[ab, z, 0], g_send.at[n], g_recv.at[ab, z], chip, half, when)

    send_rows(0)
    got_key = load(w_key_in, w_key)
    got_value = load(w_value_in, w_value)
    got_query = load(w_query_in, w_query)
    vectors = [b_query_in, b_value_in, b_out_in, gain_first_in, shift_first_in, b_outer_in, gain_second_in]
    got_rows = [load(ref, rows.at[i]) for i, ref in enumerate(vectors + [shift_second_in])]
    got_rows.append(load(b_inner_in, b_inner.at[0]))
    got_out = load(w_out_in, w_out)
    got_inner = [load(w_inner_in.at[:, :, f * FFT : (f + 1) * FFT], pool.at[EARLY + f]) for f in range(FFN)]
    got_outer = [load(w_outer_in.at[f], w_outer.at[f]) for f in range(FFN)]

    b_query, b_value, b_out, gain_first, shift_first, b_outer, gain_second, shift_second = (
        rows.at[i : i + 1] for i in range(8)
    )
    vec[...] = jnp.zeros_like(vec)
    forwards = []

    def forward_rows(ab):
        for b in range(4):
            landed(x.at[ab, b, c], d_recv.at[ab, b, c])
            copy = remote(x.at[ab, b, c], x.at[ab, b, c], f_send.at[ab, b], d_recv.at[ab, b, c], sibling)
            copy.start()
            forwards.append(copy)

    def send_cotangents():
        for slot in range(3):
            move.send(cot.at[slot], cotq.at[lowz], c_send.at[slot], c_recv.at[lowz], slot, deep, first)
        move.send(cot.at[0], cotq.at[lowz], c_send.at[3], c_recv.at[lowz], 3, deep, second)
        move.send(cot.at[1], cotq.at[2], c_send.at[4], c_recv.at[2], deep, lowz, second)
        move.send(cot.at[2], cotq.at[2], c_send.at[5], c_recv.at[2], 2 + deep, lowz, second)

    forward_rows(0)
    send_rows(1)
    own_blocks = [(0, 2 * c), (0, 2 * c + 1), (1, 2 * lowz + c)]

    def own_tokens(u):
        ab, b = own_blocks[u]
        return x[ab, b].reshape(BLOCK, D)

    def one_hot(row):
        return (lax.broadcasted_iota(jnp.int32, (8, BLOCK), 0) == row).astype(F32)

    got_key.wait()
    got_value.wait()
    got_query.wait()
    for copy in got_rows:
        copy.wait()
    def project(ab):
        for b in range(4):
            landed(x.at[ab, b, 1 - c], d_recv.at[ab, b, 1 - c])
            landed(segs.at[ab, b, 0], g_recv.at[ab, b])
        xk = x[ab].reshape(ROW, D)
        k[ab] = dot(xk, w_key[...]).astype(BF)
        v[ab] = (dot(xk, w_value[...]) + b_value[...]).astype(BF)
        for u, (row, b) in enumerate(own_blocks):
            if row == ab:
                q[u] = ((dot(own_tokens(u), w_query[...]) + b_query[...]).astype(BF) * 0.125).astype(BF)
                own_hot = one_hot(segs[ab, b, 0:1])
                for kb in range(4):
                    same = dot_tn(own_hot, one_hot(segs[ab, kb, 0:1]))
                    bias[u, :, kb * BLOCK : (kb + 1) * BLOCK] = jnp.where(same > 0.5, 0.0, -1e30)

    def lanes(j):
        return pl.ds(pl.multiple_of(j * LANES, LANES), LANES)

    lane = lax.broadcasted_iota(jnp.int32, (BLOCK, LANES), 1)

    def scores(u, cols, keys):
        score = dot_nt(stack_heads(q[u, :, cols], low), keys)
        return (score.reshape(2, BLOCK, ROW) + bias[u][None]).reshape(2 * BLOCK, ROW)

    def attend(n, carry):
        u, j = n // PAIRS, lax.rem(n, PAIRS)
        ab, cols = u // 2, lanes(j)
        score = scores(u, cols, k[ab, :, cols])
        top = jnp.max(score, axis=-1, keepdims=True)
        expo = jnp.exp(score - top)
        total = jnp.sum(expo, axis=-1, keepdims=True)
        p = (expo * (1.0 / total)).astype(BF)
        stat = top + jnp.log(total)
        lse[u] = jnp.where(lane == 2 * j, stat[:BLOCK], jnp.where(lane == 2 * j + 1, stat[BLOCK:], lse[u]))
        att[u, :, cols] = merge_heads(dot(p, v[ab, :, cols]), low).astype(BF)
        return carry

    lse[...] = jnp.zeros_like(lse)
    project(0)
    lax.fori_loop(0, 2 * PAIRS, attend, 0)
    forward_rows(1)
    send_cotangents()
    project(1)
    for copy in forwards:
        copy.wait_send()
    lax.fori_loop(2 * PAIRS, 3 * PAIRS, attend, 0)

    got_out.wait()
    acc[...] = dot(att[...].reshape(tokens, D), w_out[...]).reshape(3, BLOCK, D)
    for u in range(3):
        resid = own_tokens(u).astype(F32) + acc[u] + b_out[...]
        unit, inverse = moments(resid)
        unit1[u] = unit
        inv1[u] = jnp.broadcast_to(inverse, (BLOCK, LANES))
        low1[u] = (unit * gain_first[...] + shift_first[...]).astype(BF)
    acc[...] = jnp.zeros_like(acc)
    for copy in got_inner + got_outer:
        copy.wait()

    def inner_weight(f):
        return pool[EARLY + f].reshape(D, FFT)

    def outer_weight(f):
        return w_outer[f].reshape(FFT, D)

    def feed(f, carry):
        cols = pl.ds(pl.multiple_of(f * FFT, FFT), FFT)
        pre = dot(low1[...].reshape(tokens, D), inner_weight(f)) + b_inner[0:1, cols]
        half = 0.5 * (1.0 + lax.erf(pre * (1.0 / math.sqrt(2.0))))
        slope[f] = (half + pre * jnp.exp(-0.5 * pre * pre) * (1.0 / math.sqrt(2.0 * math.pi))).astype(BF)
        act_low = (pre * half).astype(BF)
        act[f] = act_low
        acc[...] += dot(act_low, outer_weight(f)).reshape(3, BLOCK, D)
        return carry

    lax.fori_loop(0, FFN, feed, 0)

    for slot in range(3):
        landed(cotq.at[slot], c_recv.at[slot])
    for u in range(3):
        resid = unit1[u] * gain_first[...] + shift_first[...] + acc[u] + b_outer[...]
        unit, inverse = moments(resid)
        up = cotq[u].astype(F32)
        cotq[u] = (unit * gain_second[...] + shift_second[...]).astype(BF)
        d_second = norm_back(up, unit, inverse, gain_second[...])
        d_low = d_second.astype(BF)
        acc[u] = d_second
        d_out[u] = d_low
        vec[5:6] += column_sum(d_low.astype(F32))
        vec[6:7] += column_sum(up * unit)
        vec[7:8] += column_sum(up)

    row_core = jnp.where(z == 3, 1, 0)
    row_slot = lax.rem(z, 3)
    def sent_piece(i, e):
        return 2 * (1 - by) + e if i % 2 else 2 * e + 1 - bx

    def kept_piece(i, e):
        return 2 * by + e if i % 2 else 2 * e + bx

    def second_to(i):
        return to_y if i % 2 else to_x

    def third_to(i):
        return to_x if i % 2 else to_y

    def kept_half(i):
        return bx if i % 2 else by

    def finisher(i):
        return z == 1 + (i // 2) % 2

    def helper(i):
        return z == 2 - (i // 2) % 2

    def place_in(i):
        return i // 2, 8 * (i % 2)

    def first_send(i):
        chunk, row = place_in(i)
        return remote(pool.at[chunk, pl.ds(row + 4 * (1 - c), 4)], r1.at[i], s1.at[i], t1.at[i], sibling)

    def second_send(i, e):
        return remote(r1.at[i, sent_piece(i, e)], r2.at[i, e], s2.at[i, e], t2.at[i, e], second_to(i))

    def third_send(i):
        return remote(r2.at[i, 1 - kept_half(i)], r3.at[i], s3.at[i], t3.at[i], third_to(i))

    def outer_send(i):
        return remote(r3.at[i], ro.at[i], so.at[i], to.at[i], near)

    def crossed(i):
        return 2 * (i // 4) + i % 2

    def cross_send(i):
        return remote(r3.at[i], rj.at[crossed(i)], so.at[i], tj.at[crossed(i)], across)

    def final_near(i):
        return remote(sums.at[i], sums.at[i], sf.at[i, 0], tf.at[i], near)

    def final_across(i):
        return remote(sums.at[i], sums.at[i], sf.at[i, 1], tf.at[i], across)

    def wide(value):
        return value.astype(F32)

    def pair_sum(i, p):
        chunk, row = place_in(i)
        return wide(r1[i, p]) + wide(pool[chunk, row + 4 * c + p])

    def stage2(i):
        landed(r1.at[i], t1.at[i])
        for order in range(2):
            e = lax.rem(1 - kept_half(i) + order, 2)
            p = sent_piece(i, e)
            r1[i, p] = pair_sum(i, p).astype(BF)
            second_send(i, e).start()

    def stage3(i):
        e = 1 - kept_half(i)
        landed(r2.at[i, e], t2.at[i, e])
        r2[i, e] = (wide(r2[i, e]) + pair_sum(i, kept_piece(i, e))).astype(BF)
        third_send(i).start()

    def stage4(i):
        e = kept_half(i)
        landed(r2.at[i, e], t2.at[i, e])
        landed(r3.at[i], t3.at[i])
        r3[i] = (wide(r2[i, e]) + pair_sum(i, kept_piece(i, e)) + wide(r3[i])).astype(BF)

        @pl.when(outer)
        def _():
            outer_send(i).start()

    def stage5(i):
        @pl.when(helper(i))
        def _():
            landed(ro.at[i], to.at[i])
            r3[i] = (wide(r3[i]) + wide(ro[i])).astype(BF)
            cross_send(i).start()

    def stage6(i):
        @pl.when(finisher(i))
        def _():
            landed(ro.at[i], to.at[i])
            landed(rj.at[crossed(i)], tj.at[crossed(i)])
            sums[i] = (wide(r3[i]) + wide(ro[i]) + wide(rj[crossed(i)])).astype(BF)
            final_near(i).start()
            final_across(i).start()

    def stage7(i):
        @pl.when(helper(i))
        def _():
            landed(sums.at[i], tf.at[i])
            final_near(i).start()

    def block_outer(i):
        up = d_out[...].reshape(tokens, D)
        for f in range(FFN):
            g_outer = dot_tn(act[f], up).astype(BF)
            for piece in range(2):
                for part in range(4):
                    for half in range(2):
                        row = 384 * piece + 96 * part + 48 * half
                        pool[part, 8 * half + 4 * piece + f] = g_outer[row : row + 48]
        for n in range(8):
            first_send(n).start()

    def keep_rows(i, grad):
        low_grad = grad.astype(BF)
        for p in range(8):
            for half in range(2):
                row = 96 * p + 48 * half
                pool[i, 8 * half + 4 * (p % 2) + p // 2] = low_grad[row : row + 48]
        for half in range(2):
            first_send(2 * i + half).start()

    def block_feed(f):
        up = d_out[...].reshape(tokens, D)
        d_pre = (dot_nt(up, outer_weight(f)) * slope[f].astype(F32)).astype(BF)
        slope[f] = d_pre
        vec[pl.ds(8 + f, 1)] = column_sum(d_pre.astype(F32))
        acc[...] += dot_nt(d_pre, inner_weight(f)).reshape(3, BLOCK, D)

    def block_inner(f):
        keep_rows(4 + f, dot_tn(low1[...].reshape(tokens, D), slope[f]))

    def block_norm(i):
        for u in range(3):
            up = acc[u]
            d_first = norm_back(up, unit1[u], inv1[u][:, 0:1], gain_first[...])
            acc[u] = d_first
            d_low = d_first.astype(BF)
            d_out[u] = d_low
            vec[2:3] += column_sum(d_low.astype(F32))
            vec[3:4] += column_sum(up * unit1[u])
            vec[4:5] += column_sum(up)
        act[0] = dot_nt(d_out[...].reshape(tokens, D), w_out[...]).astype(BF)

    def block_out(i):
        keep_rows(8, dot_tn(att[...].reshape(tokens, D), d_out[...].reshape(tokens, D)))

    def block_attend(j):
        cols = lanes(j)
        for ab in range(2):
            keys, values = k[ab, :, cols], v[ab, :, cols]
            g_key = g_value = None
            for u in (0, 1) if ab == 0 else (2,):
                q_both = stack_heads(q[u, :, cols], low)
                score = dot_nt(q_both, keys)
                score = (score.reshape(2, BLOCK, ROW) + bias[u][None]).reshape(2 * BLOCK, ROW)
                even = jnp.sum(jnp.where(lane == 2 * j, lse[u], 0.0), axis=-1, keepdims=True)
                odd = jnp.sum(jnp.where(lane == 2 * j + 1, lse[u], 0.0), axis=-1, keepdims=True)
                p = jnp.exp(score - jnp.concatenate([even, odd], axis=0))
                d_pair = act[0, u * BLOCK : (u + 1) * BLOCK, cols]
                d_both = stack_heads(d_pair, low)
                product = wide(d_pair) * wide(att[u, :, cols])
                even = jnp.sum(jnp.where(low, product, 0.0), axis=-1, keepdims=True)
                odd = jnp.sum(jnp.where(low, 0.0, product), axis=-1, keepdims=True)
                d_prob = dot_nt(d_both, values)
                d_score = (p * (d_prob - jnp.concatenate([even, odd], axis=0))).astype(BF)
                one_key = dot(q_both.T, d_score)
                one_value = dot(d_both.T, p.astype(BF))
                g_key = one_key if g_key is None else g_key + one_key
                g_value = one_value if g_value is None else g_value + one_value
                q[u, :, cols] = (merge_heads(dot(d_score, keys), low) * 0.125).astype(BF)
            k[ab, :, cols] = g_key.astype(BF).T
            v[ab, :, cols] = g_value.astype(BF).T

    def block_query(i):
        keep_rows(9, sum(dot_tn(own_tokens(u), q[u]) for u in range(3)))

    def block_key(i):
        keep_rows(10, sum(dot_tn(x[ab].reshape(ROW, D), k[ab]) for ab in range(2)))

    def block_value(i):
        keep_rows(11, sum(dot_tn(x[ab].reshape(ROW, D), v[ab]) for ab in range(2)))

    def share(ab, b):
        rows_b = pl.ds(pl.multiple_of(b * BLOCK, BLOCK), BLOCK)
        return dot_nt(k[ab, rows_b, :], w_key[...]) + dot_nt(v[ab, rows_b, :], w_value[...])

    def swap_send(e):
        src = act.at[1 + e // 2, (e % 2) * BLOCK : (e % 2 + 1) * BLOCK]
        return remote(src, rxa.at[e], xs.at[e], xr.at[e], sibling)

    def block_swap(i):
        for e in range(4):
            b = 2 * (1 - c) + e if e < 2 else 1 - c + 2 * (e - 2)
            act[1 + e // 2, (e % 2) * BLOCK : (e % 2 + 1) * BLOCK] = share(e // 2, b).astype(BF)
            swap_send(e).start()

    class Unit:
        def __init__(self, src, dst, send_sem, recv_sem, to_z, to_c):
            self.here = jnp.logical_and(to_z == z, to_c == c)
            self.away = jnp.logical_not(self.here)
            self.local = pltpu.make_async_copy(src, dst, recv_sem)
            self.out = remote(src, dst, send_sem, recv_sem, at(to_z, base + to_c))

        def start(self):
            @pl.when(self.here)
            def _():
                self.local.start()

            @pl.when(self.away)
            def _():
                self.out.start()

        def finish(self):
            @pl.when(self.away)
            def _():
                self.out.wait_send()

    def layer_unit(u):
        shared = u // 2
        slot = (1 - shared) * row_slot + shared * (1 + deep)
        to_z = (1 - shared) * (2 * c + u) + shared * (2 * lowz + c)
        to_c = (1 - shared) * row_core + shared
        return Unit(cotq.at[u], lay_out.at[slot], lay_s.at[u], lay_r.at[slot], to_z, to_c)

    def grad_unit(e):
        shared = e // 2
        slot = (1 - shared) * row_slot + shared * (1 + deep)
        part = shared * lowz
        to_z = (1 - shared) * (2 * c + e) + shared * (c + 2 * (e - 2))
        to_c = (1 - shared) * row_core + shared
        return Unit(rxa.at[e], grad_parts.at[slot, part], gs.at[e], gr.at[slot, part], to_z, to_c)

    def block_layer(u):
        layer_unit(u).start()

    def block_total(e):
        shared = e // 2
        b = (1 - shared) * (2 * c + e) + shared * (c + 2 * (e - 2))
        own = jnp.logical_or(e < 2, e - 2 == lowz)
        landed(rxa.at[e], xr.at[e])
        unit1[0] = share(shared, b) + wide(rxa[e])

        @pl.when(own)
        def _():
            u = (1 - shared) * e + shared * 2
            unit1[0] += dot_nt(q[u], w_query[...]) + acc[u]

        rxa[e] = unit1[0].astype(BF)
        grad_unit(e).start()

    def vec_send(i):
        hops = [sibling, to_x, to_y, at(z + 1 - 2 * lowz, beta), at(z + 2 - 4 * deep, beta)]
        return remote(sv.at[i], rv.at[i], vs.at[i], vr.at[i], hops[i])

    def block_vector(i):
        if i == 0:
            sv[0] = vec[...]
            sv[0, 0:1] = sum(column_sum(wide(q[u])) for u in range(3))
            sv[0, 1:2] = sum(column_sum(wide(v[ab])) for ab in range(2))
        else:
            landed(rv.at[i - 1], vr.at[i - 1])
            sv[i] = sv[i - 1] + rv[i - 1]
        vec_send(i).start()

    stages = [stage2, stage3, stage4, stage5, stage6, stage7]
    blocks = [
        block_outer,
        block_feed,
        block_norm,
        block_attend,
        block_swap,
        block_total,
        block_inner,
        block_out,
        block_query,
        block_key,
        block_value,
        block_layer,
        block_vector,
    ]
    OPS = stages + blocks
    counts = {kind: 0 for kind in KINDS}

    def emit(kinds):
        for kind in kinds:
            OPS[KINDS.index(kind)](counts[kind])
            counts[kind] += 1

    rest = ORDER
    for kind in LOOPED:
        emit(rest[: rest.index(kind)])
        first_turn, last_turn = rest.index(kind), rest.rindex(kind)
        between = rest[first_turn + 1 : last_turn].split(kind)

        def turn(n, carry, kind=kind, between=between):
            OPS[KINDS.index(kind)](n)
            for at_turn, kinds in enumerate(between):

                @pl.when(n == at_turn)
                def _(kinds=kinds):
                    emit(kinds)

            return carry

        lax.fori_loop(0, len(between) + 1, turn, 0)
        rest = rest[last_turn + 1 :]
    emit(rest)

    for i in range(CHUNKS):
        first_send(i).wait_send()
        for e in range(2):
            second_send(i, e).wait_send()
        third_send(i).wait_send()

        @pl.when(outer)
        def _(i=i):
            outer_send(i).wait_send()
            landed(sums.at[i], tf.at[i])

        @pl.when(inner)
        def _(i=i):
            final_near(i).wait_send()

        @pl.when(finisher(i))
        def _(i=i):
            final_across(i).wait_send()

        @pl.when(helper(i))
        def _(i=i):
            cross_send(i).wait_send()

    landed(rv.at[4], vr.at[4])
    vec_out[...] = sv[4] + rv[4]
    for i in range(5):
        vec_send(i).wait_send()
    for e in range(4):
        swap_send(e).wait_send()
        grad_unit(e).finish()
    for slot in range(3):
        layer_unit(slot).finish()
        landed(lay_out.at[slot], lay_r.at[slot])
        landed(grad_parts.at[slot, 0], gr.at[slot, 0])

    @pl.when(c == 1)
    def _():
        for slot in range(1, 3):
            landed(grad_parts.at[slot, 1], gr.at[slot, 1])

    move.finish()


def whole_layer(tokens, segments, cotangent, weights, vectors):
    vmem, anywhere = pl.BlockSpec(memory_space=pltpu.VMEM), pl.BlockSpec(memory_space=pl.ANY)
    dma = pltpu.SemaphoreType.DMA
    args = (tokens, segments, cotangent) + weights + vectors
    n = CHUNKS
    tok = (3, BLOCK, D)
    square = (16, 48, D)
    buffers = [
        ((EARLY + FFN,) + square, BF),
        ((FFN,) + square, BF),
        ((D, D), BF),
        ((D, D), BF),
        ((D, D), BF),
        ((D, D), BF),
        ((8, D), F32),
        ((8, FFN * FFT), F32),
        ((2, 4, 2, 64, D), BF),
        ((2, 4, 8, BLOCK), jnp.int32),
        (tok, BF),
        (tok, BF),
        ((2, ROW, D), BF),
        ((2, ROW, D), BF),
        (tok, BF),
        (tok, BF),
        ((FFN, 3 * BLOCK, FFT), BF),
        ((FFN, 3 * BLOCK, FFT), BF),
        (tok, F32),
        (tok, F32),
        (tok, BF),
        ((3, BLOCK, ROW), F32),
        ((3, BLOCK, LANES), F32),
        ((3, BLOCK, LANES), F32),
        ((16, D), F32),
        ((n, 4, 48, D), BF),
        ((n, 2, 48, D), BF),
        ((n, 48, D), BF),
        ((n, 48, D), BF),
        ((n // 2, 48, D), BF),
        ((4, BLOCK, D), BF),
        ((5, 16, D), F32),
        ((5, 16, D), F32),
    ]
    semaphores = [(21,), (16,), (2, 4, 2), (2, 4), (16,), (2, 4), (6,), (3,)]
    semaphores += [(n,), (n,), (n, 2), (n, 2)] + [(n,)] * 4 + [(n // 2,), (n, 2), (n,)]
    semaphores += [(3,), (3,), (4,), (4,), (4,), (3, 2), (5,), (5,)]
    return pl.pallas_call(
        layer_body,
        out_shape=(
            jax.ShapeDtypeStruct((n, 48, D), BF),
            jax.ShapeDtypeStruct((16, D), F32),
            jax.ShapeDtypeStruct(tok, BF),
            jax.ShapeDtypeStruct((3, 2, BLOCK, D), BF),
        ),
        in_specs=[anywhere] * len(args),
        out_specs=[vmem] * 4,
        scratch_shapes=[pltpu.VMEM(s, t) for s, t in buffers] + [dma(s) for s in semaphores],
        compiler_params=pltpu.CompilerParams(
            collective_id=0, has_side_effects=True, vmem_limit_bytes=int(63.9 * MIB)
        ),
    )(*args)


def finish_body(sums, vec, lay, parts, *outs):
    p = lax.rem(lax.axis_index("batch"), 8)
    c = lax.rem(p, 2)
    layer_out, input_grad, g_q, g_k, g_v, g_o, g_inner, g_outer, b_inner = outs[:9]
    layer_out[...] = lay[...]
    input_grad[...] = parts[:, 0]

    @pl.when(c == 1)
    def _():
        for slot in range(1, 3):
            both = parts[slot, 0].astype(F32) + parts[slot, 1].astype(F32)
            input_grad[slot] = both.astype(BF)

    def piece(i):
        return sums[2 * i : 2 * i + 2].reshape(96, D).astype(F32)

    for part in range(4):
        g_outer[96 * part : 96 * part + 96] = piece(part)
    for f in range(FFN):
        g_inner[:, f * FFT : (f + 1) * FFT] = piece(4 + f)
    g_o[...] = piece(8)
    g_q[...] = piece(9)
    g_k[...] = piece(10)
    g_v[...] = piece(11)
    pick = lax.broadcasted_iota(jnp.int32, (D, LANES), 0) == lax.broadcasted_iota(jnp.int32, (D, LANES), 1) + 96 * p
    vecs = jnp.dot(
        vec[0:8], pick.astype(F32), preferred_element_type=F32, precision=lax.Precision.HIGHEST
    )
    for i in range(8):
        outs[9 + i][...] = vecs[i, 0:96]
    quarter = vec[pl.ds(8 + p // 2, 1), :]
    b_inner[...] = jnp.where(lax.rem(p, 2) == 0, quarter[:, :384], quarter[:, 384:]).reshape(384)


def finish(sums, vec, lay, parts):
    vmem = pl.BlockSpec(memory_space=pltpu.VMEM)
    tok = (3, BLOCK, D)
    shapes = [
        (tok, BF),
        (tok, BF),
        ((96, D), F32),
        ((96, D), F32),
        ((96, D), F32),
        ((96, D), F32),
        ((96, 4 * D), F32),
        ((384, D), F32),
        ((384,), F32),
    ] + [((96,), F32)] * 8
    return pl.pallas_call(
        finish_body,
        out_shape=tuple(jax.ShapeDtypeStruct(s, t) for s, t in shapes),
        in_specs=[vmem] * 4,
        out_specs=[vmem] * len(shapes),
        compiler_params=pltpu.CompilerParams(vmem_limit_bytes=60 * MIB),
    )(sums, vec, lay, parts)


def per_device(
    groups,
    tokens,
    segment_ids,
    w_query,
    b_query,
    w_key,
    w_value,
    b_value,
    w_out,
    b_out,
    gain_first,
    shift_first,
    w_inner,
    b_inner,
    w_outer,
    b_outer,
    gain_second,
    shift_second,
    cotangent,
):
    weights = (w_query, w_key, w_value, w_out, w_inner.reshape(16, 48, FFN * FFT), w_outer.reshape(FFN, 16, 48, D))
    vectors = (b_query, b_value, b_out, gain_first, shift_first, b_outer, gain_second, shift_second, b_inner)
    reduced = whole_layer(tokens.reshape(3, 2, 64, D), segment_ids, cotangent, weights, vectors)
    layer_out, input_grad, g_q, g_k, g_v, g_o, g_inner, g_outer, g_b_inner, *vecs = finish(*reduced)
    g_b_query, g_b_value, g_b_out, g_gain_first, g_shift_first, g_b_outer, g_gain_second, g_shift_second = vecs
    grads = (
        g_q,
        g_b_query,
        g_k,
        g_v,
        g_b_value,
        g_o,
        g_b_out,
        g_gain_first,
        g_shift_first,
        g_inner,
        g_b_inner,
        g_outer,
        g_b_outer,
        g_gain_second,
        g_shift_second,
    )
    if groups > 1:
        place_at = lax.rem(lax.axis_index("batch"), 8)

        def spread(grad):
            whole = jnp.zeros((8 * grad.shape[0],) + grad.shape[1:], grad.dtype)
            whole = lax.dynamic_update_slice_in_dim(whole, grad, place_at * grad.shape[0], 0)
            return lax.psum_scatter(whole, "batch", scatter_dimension=0, tiled=True)

        grads = tuple(spread(grad) for grad in grads)
    return (layer_out, input_grad) + grads


def solution(mesh):
    tokens = P("batch", "blk", None)
    weight, vector = P("batch", None), P("batch")
    return jax.shard_map(
        functools.partial(per_device, mesh.shape["batch"] // 8),
        mesh=mesh,
        in_specs=(tokens, P("batch", "blk")) + (P(),) * 15 + (tokens,),
        out_specs=(tokens, tokens)
        + (
            weight,
            vector,
            weight,
            weight,
            vector,
            weight,
            vector,
            vector,
            vector,
            weight,
            vector,
            weight,
            vector,
            vector,
            vector,
        ),
        check_vma=False,
    )
```

```python
import functools
import math

import jax
import jax.numpy as jnp
from jax import lax
from jax.experimental import pallas as pl
from jax.experimental.pallas import tpu as pltpu
from jax.sharding import PartitionSpec as P

BF = jnp.bfloat16
F32 = jnp.float32
EPS = 1e-05
D = 768
PAIRS = 6
LANES = 128
BLOCK = 128
ROW = 512
FFT = 768
FFN = 4
EARLY = 9
CHUNKS = 24
ORDER = "".join(
    (
        "YBF2Y2F22YFF3233L23W342AA42534W24W325A43624535A42563A642565A",
        "6354X6465W425663T32T2O3q3245T32k25346vV324655436245642563534",
        "62465256345V64356364V546545V666VT",
    )
)
KINDS = "23456BFLAXTWOqkvYV"
LOOPED = "FAT"
MIB = 1 << 20


def dot(a, b):
    return jnp.dot(a, b, preferred_element_type=F32)


def dot_nt(a, b):
    return lax.dot_general(a, b, (((1,), (1,)), ((), ())), preferred_element_type=F32)


def dot_tn(a, b):
    return lax.dot_general(a, b, (((0,), (0,)), ((), ())), preferred_element_type=F32)


def place():
    z = lax.axis_index("blk")
    beta = lax.axis_index("batch")
    c = lax.rem(beta, 2)
    return z, beta, c, beta - c


def at(z, beta):
    return {"blk": z, "batch": beta}


def greet(devices):
    barrier = pltpu.get_barrier_semaphore()
    for device in devices:
        pl.semaphore_signal(barrier, inc=1, device_id=device, device_id_type=pl.DeviceIdType.MESH)
    pl.semaphore_wait(barrier, len(devices))


def column_mates(z, c, base):
    mates = [at(lax.rem(z + step, 4), base + core) for step in range(1, 4) for core in range(2)]
    return mates + [at(z, base + 1 - c)]


def remote(src, dst, send_sem, recv_sem, device):
    return pltpu.make_async_remote_copy(
        src_ref=src,
        dst_ref=dst,
        send_sem=send_sem,
        recv_sem=recv_sem,
        device_id=device,
        device_id_type=pl.DeviceIdType.MESH,
    )


class Mover:
    def __init__(self, z, c, base):
        self.z, self.c, self.base, self.sent = z, c, base, []

    def send(self, src, dst, send_sem, recv_sem, to_z, to_c, when=None):
        self_target = jnp.logical_and(to_z == self.z, to_c == self.c)
        other = jnp.logical_not(self_target)
        if when is not None:
            self_target = jnp.logical_and(self_target, when)
            other = jnp.logical_and(other, when)
        out = remote(src, dst, send_sem, recv_sem, at(to_z, self.base + to_c))

        @pl.when(self_target)
        def _():
            pltpu.make_async_copy(src, dst, recv_sem).start()

        @pl.when(other)
        def _():
            out.start()

        self.sent.append((other, out))

    def finish(self):
        for other, out in self.sent:

            @pl.when(other)
            def _(out=out):
                out.wait_send()

        self.sent = []


def landed(dst, sem):
    pltpu.make_async_copy(dst, dst, sem).wait()


def lane_low():
    return lax.broadcasted_iota(jnp.int32, (BLOCK, LANES), 1) < 64


def stack_heads(pair, low):
    zero = jnp.zeros_like(pair)
    return jnp.concatenate([jnp.where(low, pair, zero), jnp.where(low, zero, pair)], axis=0)


def merge_heads(both, low):
    return jnp.where(low, both[:BLOCK], both[BLOCK:])


def moments(resid):
    center = resid - jnp.mean(resid, axis=-1, keepdims=True)
    inverse = lax.rsqrt(jnp.mean(center * center, axis=-1, keepdims=True) + EPS)
    return center * inverse, inverse


def norm_back(upstream, unit, inverse, gain):
    scaled = upstream * gain
    return inverse * (
        scaled
        - jnp.mean(scaled, axis=-1, keepdims=True)
        - unit * jnp.mean(scaled * unit, axis=-1, keepdims=True)
    )


def column_sum(value):
    return jnp.sum(value, axis=0, keepdims=True)


def layer_body(
    tok,
    seg,
    cot,
    w_query_in,
    w_key_in,
    w_value_in,
    w_out_in,
    w_inner_in,
    w_outer_in,
    b_query_in,
    b_value_in,
    b_out_in,
    gain_first_in,
    shift_first_in,
    b_outer_in,
    gain_second_in,
    shift_second_in,
    b_inner_in,
    sums,
    vec_out,
    lay_out,
    grad_parts,
    pool,
    w_outer,
    w_query,
    w_key,
    w_value,
    w_out,
    rows,
    b_inner,
    x,
    segs,
    cotq,
    q,
    k,
    v,
    att,
    low1,
    act,
    slope,
    acc,
    unit1,
    d_out,
    bias,
    lse,
    inv1,
    vec,
    r1,
    r2,
    r3,
    ro,
    rj,
    rxa,
    rxb,
    sv,
    rv,
    w_sem,
    d_send,
    d_recv,
    f_send,
    g_send,
    g_recv,
    c_send,
    c_recv,
    s1,
    t1,
    s2,
    t2,
    s3,
    t3,
    so,
    to,
    tj,
    sf,
    tf,
    lay_s,
    lay_r,
    xs,
    xr,
    gs,
    gr,
    pr,
    vs,
    vr,
):
    z, beta, c, base = place()
    low = lane_low()
    tokens = 3 * BLOCK
    bx, by = lax.rem(beta // 2, 2), lax.rem(beta // 4, 2)
    sibling = at(z, base + 1 - c)
    to_x, to_y = at(z, beta + 2 - 4 * bx), at(z, beta + 4 - 8 * by)
    inner = jnp.logical_and(z > 0, z < 3)
    outer = jnp.logical_not(inner)
    near = at(jnp.where(z < 2, 1 - z, 5 - z), beta)
    across = at(jnp.where(z == 1, 2, 1), beta)
    deep, lowz = z // 2, lax.rem(z, 2)

    loads = []

    def load(src, dst):
        copy = pltpu.make_async_copy(src, dst, w_sem.at[len(loads)])
        copy.start()
        loads.append(copy)
        return copy

    greet(column_mates(z, c, base) + [to_x, to_y])
    move = Mover(z, c, base)
    first, second = c == 0, c == 1
    routes = [(s, 0, s, first) for s in range(3)] + [
        (0, 0, 3, second),
        (1, 1, 0, second),
        (1, 1, 1, second),
        (2, 1, 2, second),
        (2, 1, 3, second),
    ]
    counts = iter(range(16))

    def send_rows(which):
        for slot, ab, chip, when in routes:
            if ab == which:
                for half in range(2):
                    n = next(counts)
                    move.send(
                        tok.at[slot, half], x.at[ab, z, half], d_send.at[n], d_recv.at[ab, z, half], chip, half, when
                    )
                    move.send(seg.at[slot], segs.at[ab, z, 0], g_send.at[n], g_recv.at[ab, z], chip, half, when)

    send_rows(0)
    got_key = load(w_key_in, w_key)
    got_value = load(w_value_in, w_value)
    got_query = load(w_query_in, w_query)
    vectors = [b_query_in, b_value_in, b_out_in, gain_first_in, shift_first_in, b_outer_in, gain_second_in]
    got_rows = [load(ref, rows.at[i]) for i, ref in enumerate(vectors + [shift_second_in])]
    got_rows.append(load(b_inner_in, b_inner.at[0]))
    got_out = load(w_out_in, w_out)
    got_inner = [load(w_inner_in.at[:, :, f * FFT : (f + 1) * FFT], pool.at[EARLY + f]) for f in range(FFN)]
    got_outer = [load(w_outer_in.at[f], w_outer.at[f]) for f in range(FFN)]

    b_query, b_value, b_out, gain_first, shift_first, b_outer, gain_second, shift_second = (
        rows.at[i : i + 1] for i in range(8)
    )
    vec[...] = jnp.zeros_like(vec)
    forwards = []

    def forward_rows(ab, steps=range(4)):
        for step in steps:
            b = (z, z + 1 - 2 * lowz, lax.rem(z + 2, 4), 3 - z)[step]
            landed(x.at[ab, b, c], d_recv.at[ab, b, c])
            copy = remote(x.at[ab, b, c], x.at[ab, b, c], f_send.at[ab, step], d_recv.at[ab, b, c], sibling)
            copy.start()
            forwards.append(copy)

    def send_cotangents():
        for slot in range(3):
            move.send(cot.at[slot], cotq.at[lowz], c_send.at[slot], c_recv.at[lowz], slot, deep, first)
        move.send(cot.at[0], cotq.at[lowz], c_send.at[3], c_recv.at[lowz], 3, deep, second)
        move.send(cot.at[1], cotq.at[2], c_send.at[4], c_recv.at[2], deep, lowz, second)
        move.send(cot.at[2], cotq.at[2], c_send.at[5], c_recv.at[2], 2 + deep, lowz, second)

    forward_rows(0, range(3))
    send_rows(1)
    forward_rows(0, range(3, 4))
    own_blocks = [(0, 2 * c), (0, 2 * c + 1), (1, 2 * lowz + c)]

    def own_tokens(u):
        ab, b = own_blocks[u]
        return x[ab, b].reshape(BLOCK, D)

    def one_hot(row):
        return (lax.broadcasted_iota(jnp.int32, (8, BLOCK), 0) == row).astype(F32)

    got_key.wait()
    got_value.wait()
    got_query.wait()
    for copy in got_rows:
        copy.wait()
    def project(ab):
        for b in range(4):
            landed(x.at[ab, b, 1 - c], d_recv.at[ab, b, 1 - c])
            landed(segs.at[ab, b, 0], g_recv.at[ab, b])
        xk = x[ab].reshape(ROW, D)
        k[ab] = dot(xk, w_key[...]).astype(BF)
        v[ab] = (dot(xk, w_value[...]) + b_value[...]).astype(BF)
        for u, (row, b) in enumerate(own_blocks):
            if row == ab:
                q[u] = ((dot(own_tokens(u), w_query[...]) + b_query[...]).astype(BF) * 0.125).astype(BF)
                own_hot = one_hot(segs[ab, b, 0:1])
                for kb in range(4):
                    same = dot_tn(own_hot, one_hot(segs[ab, kb, 0:1]))
                    bias[u, :, kb * BLOCK : (kb + 1) * BLOCK] = jnp.where(same > 0.5, 0.0, -1e30)

    def lanes(j):
        return pl.ds(pl.multiple_of(j * LANES, LANES), LANES)

    lane = lax.broadcasted_iota(jnp.int32, (BLOCK, LANES), 1)

    def attend(ab, units, start, stop):
        n, base_u = len(units), units[0]

        def pair(j, carry):
            cols = lanes(j)
            both = jnp.concatenate([stack_heads(q[u, :, cols], low) for u in units], axis=0)
            score = dot_nt(both, k[ab, :, cols]).reshape(n, 2, BLOCK, ROW) + bias[base_u : base_u + n][:, None]
            score = score.reshape(n * 2 * BLOCK, ROW)
            top = jnp.max(score, axis=-1, keepdims=True)
            expo = jnp.exp(score - top)
            total = jnp.sum(expo, axis=-1, keepdims=True)
            p = (expo * (1.0 / total)).astype(BF)
            stat = top + jnp.log(total)
            heads = dot(p, v[ab, :, cols])
            for m, u in enumerate(units):
                even, odd = slice(2 * m * BLOCK, (2 * m + 1) * BLOCK), slice((2 * m + 1) * BLOCK, (2 * m + 2) * BLOCK)
                lse[u] = jnp.where(lane == 2 * j, stat[even], jnp.where(lane == 2 * j + 1, stat[odd], lse[u]))
                att[u, :, cols] = jnp.where(low, heads[even], heads[odd]).astype(BF)
            return carry

        lax.fori_loop(start, stop, pair, 0)

    def out_norm(units):
        base_u, n = units[0], len(units)
        acc[base_u : base_u + n] = dot(att[base_u : base_u + n].reshape(n * BLOCK, D), w_out[...]).reshape(n, BLOCK, D)
        for u in units:
            resid = own_tokens(u).astype(F32) + acc[u] + b_out[...]
            unit, inverse = moments(resid)
            unit1[u] = unit
            inv1[u] = jnp.broadcast_to(inverse, (BLOCK, LANES))
            low1[u] = (unit * gain_first[...] + shift_first[...]).astype(BF)

    lse[...] = jnp.zeros_like(lse)
    project(0)
    attend(0, (0, 1), 0, PAIRS)
    forward_rows(1)
    send_cotangents()
    got_out.wait()
    out_norm((0, 1))
    project(1)
    for copy in forwards:
        copy.wait_send()
    attend(1, (2,), 0, PAIRS)
    out_norm((2,))
    acc[...] = jnp.zeros_like(acc)
    for copy in got_inner + got_outer:
        copy.wait()

    def inner_weight(f):
        return pool[EARLY + f].reshape(D, FFT)

    def outer_weight(f):
        return w_outer[f].reshape(FFT, D)

    def feed(f, carry):
        cols = pl.ds(pl.multiple_of(f * FFT, FFT), FFT)
        pre = dot(low1[...].reshape(tokens, D), inner_weight(f)) + b_inner[0:1, cols]
        half = 0.5 * (1.0 + lax.erf(pre * (1.0 / math.sqrt(2.0))))
        slope[f] = (half + pre * jnp.exp(-0.5 * pre * pre) * (1.0 / math.sqrt(2.0 * math.pi))).astype(BF)
        act_low = (pre * half).astype(BF)
        act[f] = act_low
        acc[...] += dot(act_low, outer_weight(f)).reshape(3, BLOCK, D)
        return carry

    lax.fori_loop(0, FFN, feed, 0)

    for slot in range(3):
        landed(cotq.at[slot], c_recv.at[slot])
    for u in range(3):
        resid = unit1[u] * gain_first[...] + shift_first[...] + acc[u] + b_outer[...]
        unit, inverse = moments(resid)
        up = cotq[u].astype(F32)
        cotq[u] = (unit * gain_second[...] + shift_second[...]).astype(BF)
        d_second = norm_back(up, unit, inverse, gain_second[...])
        d_low = d_second.astype(BF)
        acc[u] = d_second
        d_out[u] = d_low
        vec[5:6] += column_sum(d_low.astype(F32))
        vec[6:7] += column_sum(up * unit)
        vec[7:8] += column_sum(up)

    row_core = jnp.where(z == 3, 1, 0)
    row_slot = lax.rem(z, 3)
    def sent_piece(i, e):
        return 2 * (1 - by) + e if i % 2 else 2 * e + 1 - bx

    def kept_piece(i, e):
        return 2 * by + e if i % 2 else 2 * e + bx

    def second_to(i):
        return to_y if i % 2 else to_x

    def third_to(i):
        return to_x if i % 2 else to_y

    def kept_half(i):
        return bx if i % 2 else by

    def place_in(i):
        return i // 2, 8 * (i % 2)

    def first_send(i):
        chunk, row = place_in(i)
        return remote(pool.at[chunk, pl.ds(row + 4 * (1 - c), 4)], r1.at[i], s1.at[i], t1.at[i], sibling)

    def second_send(i, e):
        return remote(r1.at[i, sent_piece(i, e)], r2.at[i, e], s2.at[i, e], t2.at[i, e], second_to(i))

    def third_send(i):
        return remote(r2.at[i, 1 - kept_half(i)], r3.at[i], s3.at[i], t3.at[i], third_to(i))

    def outer_send(i):
        return remote(r3.at[i], ro.at[i], so.at[i], to.at[i], near)

    def cross_send(i):
        return remote(r3.at[i], rj.at[i], so.at[i], tj.at[i], across)

    def final_near(i):
        return remote(sums.at[i], sums.at[i], sf.at[i], tf.at[i], near)

    def wide(value):
        return value.astype(F32)

    def pair_sum(i, p):
        chunk, row = place_in(i)
        return wide(r1[i, p]) + wide(pool[chunk, row + 4 * c + p])

    def stage2(i):
        landed(r1.at[i], t1.at[i])
        for order in range(2):
            e = lax.rem(1 - kept_half(i) + order, 2)
            p = sent_piece(i, e)
            r1[i, p] = pair_sum(i, p).astype(BF)
            second_send(i, e).start()

    def stage3(i):
        e = 1 - kept_half(i)
        landed(r2.at[i, e], t2.at[i, e])
        r2[i, e] = (wide(r2[i, e]) + pair_sum(i, kept_piece(i, e))).astype(BF)
        third_send(i).start()

    def stage4(i):
        e = kept_half(i)
        landed(r2.at[i, e], t2.at[i, e])
        landed(r3.at[i], t3.at[i])
        r3[i] = (wide(r2[i, e]) + pair_sum(i, kept_piece(i, e)) + wide(r3[i])).astype(BF)

        @pl.when(outer)
        def _():
            outer_send(i).start()

    def stage5(i):
        @pl.when(inner)
        def _():
            landed(ro.at[i], to.at[i])
            r3[i] = (wide(r3[i]) + wide(ro[i])).astype(BF)
            cross_send(i).start()

    def stage6(i):
        @pl.when(inner)
        def _():
            landed(rj.at[i], tj.at[i])
            sums[i] = (wide(r3[i]) + wide(rj[i])).astype(BF)
            final_near(i).start()

    def block_outer(i):
        up = d_out[...].reshape(tokens, D)
        for f in range(FFN):
            g_outer = dot_tn(act[f], up).astype(BF)
            for piece in range(2):
                for part in range(4):
                    for half in range(2):
                        row = 384 * piece + 96 * part + 48 * half
                        pool[part, 8 * half + 4 * piece + f] = g_outer[row : row + 48]
        for n in range(8):
            first_send(n).start()

    def keep_rows(i, grad):
        low_grad = grad.astype(BF)
        for p in range(8):
            for half in range(2):
                row = 96 * p + 48 * half
                pool[i, 8 * half + 4 * (p % 2) + p // 2] = low_grad[row : row + 48]
        for half in range(2):
            first_send(2 * i + half).start()

    def block_feed(f):
        up = d_out[...].reshape(tokens, D)
        d_pre = (dot_nt(up, outer_weight(f)) * slope[f].astype(F32)).astype(BF)
        slope[f] = d_pre
        vec[pl.ds(8 + f, 1)] = column_sum(d_pre.astype(F32))
        acc[...] += dot_nt(d_pre, inner_weight(f)).reshape(3, BLOCK, D)

    def block_inner(f):
        keep_rows(4 + f, dot_tn(low1[...].reshape(tokens, D), slope[f]))

    def block_norm(i):
        for u in range(3):
            up = acc[u]
            d_first = norm_back(up, unit1[u], inv1[u][:, 0:1], gain_first[...])
            acc[u] = d_first
            d_low = d_first.astype(BF)
            d_out[u] = d_low
            vec[2:3] += column_sum(d_low.astype(F32))
            vec[3:4] += column_sum(up * unit1[u])
            vec[4:5] += column_sum(up)
        act[0] = dot_nt(d_out[...].reshape(tokens, D), w_out[...]).astype(BF)

    def block_out(i):
        keep_rows(8, dot_tn(att[...].reshape(tokens, D), d_out[...].reshape(tokens, D)))

    def block_attend(j):
        cols = lanes(j)
        for ab in range(2):
            keys, values = k[ab, :, cols], v[ab, :, cols]
            g_key = g_value = None
            for u in (0, 1) if ab == 0 else (2,):
                q_both = stack_heads(q[u, :, cols], low)
                score = dot_nt(q_both, keys)
                score = (score.reshape(2, BLOCK, ROW) + bias[u][None]).reshape(2 * BLOCK, ROW)
                even = jnp.sum(jnp.where(lane == 2 * j, lse[u], 0.0), axis=-1, keepdims=True)
                odd = jnp.sum(jnp.where(lane == 2 * j + 1, lse[u], 0.0), axis=-1, keepdims=True)
                p = jnp.exp(score - jnp.concatenate([even, odd], axis=0))
                d_pair = act[0, u * BLOCK : (u + 1) * BLOCK, cols]
                d_both = stack_heads(d_pair, low)
                product = wide(d_pair) * wide(att[u, :, cols])
                even = jnp.sum(jnp.where(low, product, 0.0), axis=-1, keepdims=True)
                odd = jnp.sum(jnp.where(low, 0.0, product), axis=-1, keepdims=True)
                d_prob = dot_nt(d_both, values)
                d_score = (p * (d_prob - jnp.concatenate([even, odd], axis=0))).astype(BF)
                one_key = dot(q_both.T, d_score)
                one_value = dot(d_both.T, p.astype(BF))
                g_key = one_key if g_key is None else g_key + one_key
                g_value = one_value if g_value is None else g_value + one_value
                q[u, :, cols] = (merge_heads(dot(d_score, keys), low) * 0.125).astype(BF)
            k[ab, :, cols] = g_key.astype(BF).T
            v[ab, :, cols] = g_value.astype(BF).T

    def block_query(i):
        keep_rows(9, sum(dot_tn(own_tokens(u), q[u]) for u in range(3)))

    def block_key(i):
        keep_rows(10, sum(dot_tn(x[ab].reshape(ROW, D), k[ab]) for ab in range(2)))

    def block_value(i):
        keep_rows(11, sum(dot_tn(x[ab].reshape(ROW, D), v[ab]) for ab in range(2)))

    def share(ab, b):
        rows_b = pl.ds(pl.multiple_of(b * BLOCK, BLOCK), BLOCK)
        return dot_nt(k[ab, rows_b, :], w_key[...]) + dot_nt(v[ab, rows_b, :], w_value[...])

    def swap_send(e):
        src = act.at[1 + e // 2, (e % 2) * BLOCK : (e % 2 + 1) * BLOCK]
        return remote(src, rxa.at[e], xs.at[e], xr.at[e], sibling)

    def block_swap(i):
        for e in range(4):
            b = 2 * (1 - c) + e if e < 2 else 1 - c + 2 * (e - 2)
            act[1 + e // 2, (e % 2) * BLOCK : (e % 2 + 1) * BLOCK] = share(e // 2, b).astype(BF)
            swap_send(e).start()

    class Unit:
        def __init__(self, src, dst, send_sem, recv_sem, to_z, to_c):
            self.here = jnp.logical_and(to_z == z, to_c == c)
            self.away = jnp.logical_not(self.here)
            self.local = pltpu.make_async_copy(src, dst, recv_sem)
            self.out = remote(src, dst, send_sem, recv_sem, at(to_z, base + to_c))

        def start(self):
            @pl.when(self.here)
            def _():
                self.local.start()

            @pl.when(self.away)
            def _():
                self.out.start()

        def finish(self):
            @pl.when(self.away)
            def _():
                self.out.wait_send()

    def layer_unit(u):
        shared = u // 2
        slot = (1 - shared) * row_slot + shared * (1 + deep)
        to_z = (1 - shared) * (2 * c + u) + shared * (2 * lowz + c)
        to_c = (1 - shared) * row_core + shared
        return Unit(cotq.at[u], lay_out.at[slot], lay_s.at[u], lay_r.at[slot], to_z, to_c)

    def grad_unit(n):
        shared = n // 2
        slot = (1 - shared) * row_slot + shared * (1 + deep)
        to_z = (1 - shared) * (2 * c + n) + shared * (c + 2 * lowz)
        to_c = (1 - shared) * row_core + shared
        src = rxa.at[(1 - shared) * n + shared * (2 + lowz)]
        return Unit(src, grad_parts.at[slot], gs.at[n], gr.at[slot], to_z, to_c)

    def pair_send():
        return remote(rxa.at[3 - lowz], rxb, gs.at[2], pr.at[0], at(z + 1 - 2 * lowz, beta))

    def block_layer(u):
        layer_unit(u).start()

    def block_total(n):
        shared = n // 2
        e = lax.rem(n + 1 + lowz, 2)
        at_e = (1 - shared) * n + shared * (2 + e)
        landed(rxa.at[at_e], xr.at[at_e])
        unit1[0] = share(shared, (1 - shared) * (2 * c + n) + shared * (c + 2 * e)) + wide(rxa[at_e])

        @pl.when(n != 2)
        def _():
            u = (1 - shared) * n + shared * 2
            unit1[0] += dot_nt(q[u], w_query[...]) + acc[u]

        @pl.when(n == 3)
        def _():
            landed(rxb, pr.at[0])
            unit1[0] += wide(rxb[...])

        rxa[at_e] = unit1[0].astype(BF)

        @pl.when(n == 2)
        def _():
            pair_send().start()

        @pl.when(n != 2)
        def _():
            grad_unit(n).start()

    def vec_send(i):
        hops = [sibling, to_x, to_y, at(z + 1 - 2 * lowz, beta), at(z + 2 - 4 * deep, beta)]
        return remote(sv.at[i], rv.at[i], vs.at[i], vr.at[i], hops[i])

    def block_vector(i):
        if i == 0:
            sv[0] = vec[...]
            sv[0, 0:1] = sum(column_sum(wide(q[u])) for u in range(3))
            sv[0, 1:2] = sum(column_sum(wide(v[ab])) for ab in range(2))
        else:
            landed(rv.at[i - 1], vr.at[i - 1])
            sv[i] = sv[i - 1] + rv[i - 1]
        vec_send(i).start()

    stages = [stage2, stage3, stage4, stage5, stage6]
    blocks = [
        block_outer,
        block_feed,
        block_norm,
        block_attend,
        block_swap,
        block_total,
        block_inner,
        block_out,
        block_query,
        block_key,
        block_value,
        block_layer,
        block_vector,
    ]
    OPS = stages + blocks
    counts = {kind: 0 for kind in KINDS}

    def emit(kinds):
        for kind in kinds:
            OPS[KINDS.index(kind)](counts[kind])
            counts[kind] += 1

    rest = ORDER
    for kind in LOOPED:
        emit(rest[: rest.index(kind)])
        first_turn, last_turn = rest.index(kind), rest.rindex(kind)
        between = rest[first_turn + 1 : last_turn].split(kind)

        def turn(n, carry, kind=kind, between=between):
            OPS[KINDS.index(kind)](n)
            for at_turn, kinds in enumerate(between):

                @pl.when(n == at_turn)
                def _(kinds=kinds):
                    emit(kinds)

            return carry

        lax.fori_loop(0, len(between) + 1, turn, 0)
        rest = rest[last_turn + 1 :]
    emit(rest)

    for i in range(CHUNKS):
        first_send(i).wait_send()
        for e in range(2):
            second_send(i, e).wait_send()
        third_send(i).wait_send()

        @pl.when(outer)
        def _(i=i):
            outer_send(i).wait_send()
            landed(sums.at[i], tf.at[i])

        @pl.when(inner)
        def _(i=i):
            final_near(i).wait_send()
            cross_send(i).wait_send()

    landed(rv.at[4], vr.at[4])
    vec_out[...] = sv[4] + rv[4]
    for i in range(5):
        vec_send(i).wait_send()
    for e in range(4):
        swap_send(e).wait_send()
    pair_send().wait_send()
    for n in (0, 1, 3):
        grad_unit(n).finish()
    for slot in range(3):
        layer_unit(slot).finish()
        landed(lay_out.at[slot], lay_r.at[slot])
        landed(grad_parts.at[slot], gr.at[slot])

    move.finish()


def whole_layer(tokens, segments, cotangent, weights, vectors):
    vmem, anywhere = pl.BlockSpec(memory_space=pltpu.VMEM), pl.BlockSpec(memory_space=pl.ANY)
    dma = pltpu.SemaphoreType.DMA
    args = (tokens, segments, cotangent) + weights + vectors
    n = CHUNKS
    tok = (3, BLOCK, D)
    square = (16, 48, D)
    buffers = [
        ((EARLY + FFN,) + square, BF),
        ((FFN,) + square, BF),
        ((D, D), BF),
        ((D, D), BF),
        ((D, D), BF),
        ((D, D), BF),
        ((8, D), F32),
        ((8, FFN * FFT), F32),
        ((2, 4, 2, 64, D), BF),
        ((2, 4, 8, BLOCK), jnp.int32),
        (tok, BF),
        (tok, BF),
        ((2, ROW, D), BF),
        ((2, ROW, D), BF),
        (tok, BF),
        (tok, BF),
        ((FFN, 3 * BLOCK, FFT), BF),
        ((FFN, 3 * BLOCK, FFT), BF),
        (tok, F32),
        (tok, F32),
        (tok, BF),
        ((3, BLOCK, ROW), F32),
        ((3, BLOCK, LANES), F32),
        ((3, BLOCK, LANES), F32),
        ((16, D), F32),
        ((n, 4, 48, D), BF),
        ((n, 2, 48, D), BF),
        ((n, 48, D), BF),
        ((n, 48, D), BF),
        ((n, 48, D), BF),
        ((4, BLOCK, D), BF),
        ((BLOCK, D), BF),
        ((5, 16, D), F32),
        ((5, 16, D), F32),
    ]
    semaphores = [(21,), (16,), (2, 4, 2), (2, 4), (16,), (2, 4), (6,), (3,)]
    semaphores += [(n,), (n,), (n, 2), (n, 2)] + [(n,)] * 7
    semaphores += [(3,), (3,), (4,), (4,), (4,), (3,), (1,), (5,), (5,)]
    return pl.pallas_call(
        layer_body,
        out_shape=(
            jax.ShapeDtypeStruct((n, 48, D), BF),
            jax.ShapeDtypeStruct((16, D), F32),
            jax.ShapeDtypeStruct(tok, BF),
            jax.ShapeDtypeStruct(tok, BF),
        ),
        in_specs=[anywhere] * len(args),
        out_specs=[vmem] * 4,
        scratch_shapes=[pltpu.VMEM(s, t) for s, t in buffers] + [dma(s) for s in semaphores],
        compiler_params=pltpu.CompilerParams(
            collective_id=0, has_side_effects=True, vmem_limit_bytes=int(63.9 * MIB)
        ),
    )(*args)


def finish_body(sums, vec, lay, parts, *outs):
    p = lax.rem(lax.axis_index("batch"), 8)
    layer_out, input_grad, g_q, g_k, g_v, g_o, g_inner, g_outer, b_inner = outs[:9]
    layer_out[...] = lay[...]
    input_grad[...] = parts[...]

    def piece(i):
        return sums[2 * i : 2 * i + 2].reshape(96, D).astype(F32)

    for part in range(4):
        g_outer[96 * part : 96 * part + 96] = piece(part)
    for f in range(FFN):
        g_inner[:, f * FFT : (f + 1) * FFT] = piece(4 + f)
    g_o[...] = piece(8)
    g_q[...] = piece(9)
    g_k[...] = piece(10)
    g_v[...] = piece(11)
    pick = lax.broadcasted_iota(jnp.int32, (D, LANES), 0) == lax.broadcasted_iota(jnp.int32, (D, LANES), 1) + 96 * p
    vecs = jnp.dot(
        vec[0:8], pick.astype(F32), preferred_element_type=F32, precision=lax.Precision.HIGHEST
    )
    for i in range(8):
        outs[9 + i][...] = vecs[i, 0:96]
    quarter = vec[pl.ds(8 + p // 2, 1), :]
    b_inner[...] = jnp.where(lax.rem(p, 2) == 0, quarter[:, :384], quarter[:, 384:]).reshape(384)


def finish(sums, vec, lay, parts):
    vmem = pl.BlockSpec(memory_space=pltpu.VMEM)
    tok = (3, BLOCK, D)
    shapes = [
        (tok, BF),
        (tok, BF),
        ((96, D), F32),
        ((96, D), F32),
        ((96, D), F32),
        ((96, D), F32),
        ((96, 4 * D), F32),
        ((384, D), F32),
        ((384,), F32),
    ] + [((96,), F32)] * 8
    return pl.pallas_call(
        finish_body,
        out_shape=tuple(jax.ShapeDtypeStruct(s, t) for s, t in shapes),
        in_specs=[vmem] * 4,
        out_specs=[vmem] * len(shapes),
        compiler_params=pltpu.CompilerParams(vmem_limit_bytes=60 * MIB),
    )(sums, vec, lay, parts)


def per_device(
    groups,
    tokens,
    segment_ids,
    w_query,
    b_query,
    w_key,
    w_value,
    b_value,
    w_out,
    b_out,
    gain_first,
    shift_first,
    w_inner,
    b_inner,
    w_outer,
    b_outer,
    gain_second,
    shift_second,
    cotangent,
):
    weights = (w_query, w_key, w_value, w_out, w_inner.reshape(16, 48, FFN * FFT), w_outer.reshape(FFN, 16, 48, D))
    vectors = (b_query, b_value, b_out, gain_first, shift_first, b_outer, gain_second, shift_second, b_inner)
    reduced = whole_layer(tokens.reshape(3, 2, 64, D), segment_ids, cotangent, weights, vectors)
    layer_out, input_grad, g_q, g_k, g_v, g_o, g_inner, g_outer, g_b_inner, *vecs = finish(*reduced)
    g_b_query, g_b_value, g_b_out, g_gain_first, g_shift_first, g_b_outer, g_gain_second, g_shift_second = vecs
    grads = (
        g_q,
        g_b_query,
        g_k,
        g_v,
        g_b_value,
        g_o,
        g_b_out,
        g_gain_first,
        g_shift_first,
        g_inner,
        g_b_inner,
        g_outer,
        g_b_outer,
        g_gain_second,
        g_shift_second,
    )
    if groups > 1:
        place_at = lax.rem(lax.axis_index("batch"), 8)

        def spread(grad):
            whole = jnp.zeros((8 * grad.shape[0],) + grad.shape[1:], grad.dtype)
            whole = lax.dynamic_update_slice_in_dim(whole, grad, place_at * grad.shape[0], 0)
            return lax.psum_scatter(whole, "batch", scatter_dimension=0, tiled=True)

        grads = tuple(spread(grad) for grad in grads)
    return (layer_out, input_grad) + grads


def solution(mesh):
    tokens = P("batch", "blk", None)
    weight, vector = P("batch", None), P("batch")
    return jax.shard_map(
        functools.partial(per_device, mesh.shape["batch"] // 8),
        mesh=mesh,
        in_specs=(tokens, P("batch", "blk")) + (P(),) * 15 + (tokens,),
        out_specs=(tokens, tokens)
        + (
            weight,
            vector,
            weight,
            weight,
            vector,
            weight,
            vector,
            vector,
            vector,
            weight,
            vector,
            weight,
            vector,
            vector,
            vector,
        ),
        check_vma=False,
    )
```

```python
import functools
import math

import jax
import jax.numpy as jnp
from jax import lax
from jax.experimental import pallas as pl
from jax.experimental.pallas import tpu as pltpu
from jax.sharding import PartitionSpec as P

BF = jnp.bfloat16
F32 = jnp.float32
EPS = 1e-05
D = 768
PAIRS = 6
LANES = 128
BLOCK = 128
ROW = 512
FFT = 768
FFN = 4
EARLY = 9
CHUNKS = 24
ORDER = "".join(
    (
        "BYYYF22WF223F23WF23L2343A43A52243A45W4462352A53465A4365A6354",
        "5X6426W4626T2352T23Oq34T5232k5v3644653265243V45356V354622645",
        "6V56T24324V3654635354654656456V66",
    )
)
KINDS = "23456BFLAXTWOqkvYV"
LOOPED = "FAT"
MIB = 1 << 20


def dot(a, b):
    return jnp.dot(a, b, preferred_element_type=F32)


def dot_nt(a, b):
    return lax.dot_general(a, b, (((1,), (1,)), ((), ())), preferred_element_type=F32)


def dot_tn(a, b):
    return lax.dot_general(a, b, (((0,), (0,)), ((), ())), preferred_element_type=F32)


def place():
    z = lax.axis_index("blk")
    beta = lax.axis_index("batch")
    c = lax.rem(beta, 2)
    return z, beta, c, beta - c


def at(z, beta):
    return {"blk": z, "batch": beta}


def greet(devices):
    barrier = pltpu.get_barrier_semaphore()
    for device in devices:
        pl.semaphore_signal(barrier, inc=1, device_id=device, device_id_type=pl.DeviceIdType.MESH)
    pl.semaphore_wait(barrier, len(devices))


def column_mates(z, c, base):
    mates = [at(lax.rem(z + step, 4), base + core) for step in range(1, 4) for core in range(2)]
    return mates + [at(z, base + 1 - c)]


def remote(src, dst, send_sem, recv_sem, device):
    return pltpu.make_async_remote_copy(
        src_ref=src,
        dst_ref=dst,
        send_sem=send_sem,
        recv_sem=recv_sem,
        device_id=device,
        device_id_type=pl.DeviceIdType.MESH,
    )


class Mover:
    def __init__(self, z, c, base):
        self.z, self.c, self.base, self.sent = z, c, base, []

    def send(self, src, dst, send_sem, recv_sem, to_z, to_c, when=None):
        self_target = jnp.logical_and(to_z == self.z, to_c == self.c)
        other = jnp.logical_not(self_target)
        if when is not None:
            self_target = jnp.logical_and(self_target, when)
            other = jnp.logical_and(other, when)
        out = remote(src, dst, send_sem, recv_sem, at(to_z, self.base + to_c))

        @pl.when(self_target)
        def _():
            pltpu.make_async_copy(src, dst, recv_sem).start()

        @pl.when(other)
        def _():
            out.start()

        self.sent.append((other, out))

    def finish(self):
        for other, out in self.sent:

            @pl.when(other)
            def _(out=out):
                out.wait_send()

        self.sent = []


def landed(dst, sem):
    pltpu.make_async_copy(dst, dst, sem).wait()


def lane_low():
    return lax.broadcasted_iota(jnp.int32, (BLOCK, LANES), 1) < 64


def stack_heads(pair, low):
    zero = jnp.zeros_like(pair)
    return jnp.concatenate([jnp.where(low, pair, zero), jnp.where(low, zero, pair)], axis=0)


def merge_heads(both, low):
    return jnp.where(low, both[:BLOCK], both[BLOCK:])


def moments(resid):
    center = resid - jnp.mean(resid, axis=-1, keepdims=True)
    inverse = lax.rsqrt(jnp.mean(center * center, axis=-1, keepdims=True) + EPS)
    return center * inverse, inverse


def norm_back(upstream, unit, inverse, gain):
    scaled = upstream * gain
    return inverse * (
        scaled
        - jnp.mean(scaled, axis=-1, keepdims=True)
        - unit * jnp.mean(scaled * unit, axis=-1, keepdims=True)
    )


def column_sum(value):
    return jnp.sum(value, axis=0, keepdims=True)


def layer_body(
    tok,
    seg,
    cot,
    w_query_in,
    w_key_in,
    w_value_in,
    w_out_in,
    w_inner_in,
    w_outer_in,
    b_query_in,
    b_value_in,
    b_out_in,
    gain_first_in,
    shift_first_in,
    b_outer_in,
    gain_second_in,
    shift_second_in,
    b_inner_in,
    sums_hbm,
    vec_hbm,
    lay_hbm,
    grad_hbm,
    sums,
    lay_out,
    grad_parts,
    pool,
    w_outer,
    w_query,
    w_key,
    w_value,
    w_out,
    rows,
    b_inner,
    x,
    segs,
    cotq,
    q,
    k,
    v,
    att,
    low1,
    act,
    slope,
    acc,
    unit1,
    d_out,
    bias,
    lse,
    inv1,
    vec,
    r1,
    r2,
    r3,
    ro,
    rj,
    rxa,
    rxb,
    sv,
    rv,
    w_sem,
    d_send,
    d_recv,
    f_send,
    g_send,
    g_recv,
    c_send,
    c_recv,
    s1,
    t1,
    s2,
    t2,
    s3,
    t3,
    so,
    to,
    tj,
    sf,
    tf,
    lay_s,
    lay_r,
    xs,
    xr,
    gs,
    gr,
    pr,
    vs,
    vr,
    out_sem,
):
    z, beta, c, base = place()
    low = lane_low()
    tokens = 3 * BLOCK
    bx, by = lax.rem(beta // 2, 2), lax.rem(beta // 4, 2)
    sibling = at(z, base + 1 - c)
    to_x, to_y = at(z, beta + 2 - 4 * bx), at(z, beta + 4 - 8 * by)
    inner = jnp.logical_and(z > 0, z < 3)
    outer = jnp.logical_not(inner)
    near = at(jnp.where(z < 2, 1 - z, 5 - z), beta)
    across = at(jnp.where(z == 1, 2, 1), beta)
    deep, lowz = z // 2, lax.rem(z, 2)

    loads = []

    def load(src, dst):
        copy = pltpu.make_async_copy(src, dst, w_sem.at[len(loads)])
        copy.start()
        loads.append(copy)
        return copy

    greet(column_mates(z, c, base) + [to_x, to_y])
    move = Mover(z, c, base)
    first, second = c == 0, c == 1
    routes = [(s, 0, s, first) for s in range(3)] + [
        (0, 0, 3, second),
        (1, 1, 0, second),
        (1, 1, 1, second),
        (2, 1, 2, second),
        (2, 1, 3, second),
    ]
    counts = iter(range(16))

    def send_rows(which):
        for slot, ab, chip, when in routes:
            if ab == which:
                for half in range(2):
                    n = next(counts)
                    move.send(
                        tok.at[slot, half], x.at[ab, z, half], d_send.at[n], d_recv.at[ab, z, half], chip, half, when
                    )
                    move.send(seg.at[slot], segs.at[ab, z, 0], g_send.at[n], g_recv.at[ab, z], chip, half, when)

    send_rows(0)
    got_key = load(w_key_in, w_key)
    got_value = load(w_value_in, w_value)
    got_query = load(w_query_in, w_query)
    vectors = [b_query_in, b_value_in, b_out_in, gain_first_in, shift_first_in, b_outer_in, gain_second_in]
    got_rows = [load(ref, rows.at[i]) for i, ref in enumerate(vectors + [shift_second_in])]
    got_rows.append(load(b_inner_in, b_inner.at[0]))
    got_out = load(w_out_in, w_out)
    got_inner = [load(w_inner_in.at[:, :, f * FFT : (f + 1) * FFT], pool.at[EARLY + f]) for f in range(FFN)]
    got_outer = [load(w_outer_in.at[f], w_outer.at[f]) for f in range(FFN)]

    b_query, b_value, b_out, gain_first, shift_first, b_outer, gain_second, shift_second = (
        rows.at[i : i + 1] for i in range(8)
    )
    vec[...] = jnp.zeros_like(vec)
    forwards = []

    def forward_rows(ab, steps=range(4)):
        for step in steps:
            b = (z, z + 1 - 2 * lowz, lax.rem(z + 2, 4), 3 - z)[step]
            landed(x.at[ab, b, c], d_recv.at[ab, b, c])
            copy = remote(x.at[ab, b, c], x.at[ab, b, c], f_send.at[ab, step], d_recv.at[ab, b, c], sibling)
            copy.start()
            forwards.append(copy)

    def send_cotangents():
        for slot in range(3):
            move.send(cot.at[slot], cotq.at[lowz], c_send.at[slot], c_recv.at[lowz], slot, deep, first)
        move.send(cot.at[0], cotq.at[lowz], c_send.at[3], c_recv.at[lowz], 3, deep, second)
        move.send(cot.at[1], cotq.at[2], c_send.at[4], c_recv.at[2], deep, lowz, second)
        move.send(cot.at[2], cotq.at[2], c_send.at[5], c_recv.at[2], 2 + deep, lowz, second)

    forward_rows(0, range(3))
    send_rows(1)
    forward_rows(0, range(3, 4))
    own_blocks = [(0, 2 * c), (0, 2 * c + 1), (1, 2 * lowz + c)]

    def own_tokens(u):
        ab, b = own_blocks[u]
        return x[ab, b].reshape(BLOCK, D)

    def one_hot(row):
        return (lax.broadcasted_iota(jnp.int32, (8, BLOCK), 0) == row).astype(F32)

    got_key.wait()
    got_value.wait()
    got_query.wait()
    for copy in got_rows:
        copy.wait()
    def project(ab):
        for b in range(4):
            landed(x.at[ab, b, 1 - c], d_recv.at[ab, b, 1 - c])
            landed(segs.at[ab, b, 0], g_recv.at[ab, b])
        xk = x[ab].reshape(ROW, D)
        k[ab] = dot(xk, w_key[...]).astype(BF)
        v[ab] = (dot(xk, w_value[...]) + b_value[...]).astype(BF)
        for u, (row, b) in enumerate(own_blocks):
            if row == ab:
                q[u] = ((dot(own_tokens(u), w_query[...]) + b_query[...]).astype(BF) * 0.125).astype(BF)
                own_hot = one_hot(segs[ab, b, 0:1])
                for kb in range(4):
                    same = dot_tn(own_hot, one_hot(segs[ab, kb, 0:1]))
                    bias[u, :, kb * BLOCK : (kb + 1) * BLOCK] = jnp.where(same > 0.5, 0.0, -1e30)

    def lanes(j):
        return pl.ds(pl.multiple_of(j * LANES, LANES), LANES)

    lane = lax.broadcasted_iota(jnp.int32, (BLOCK, LANES), 1)

    def attend(ab, units, start, stop):
        n, base_u = len(units), units[0]

        def pair(j, carry):
            cols = lanes(j)
            both = jnp.concatenate([stack_heads(q[u, :, cols], low) for u in units], axis=0)
            score = dot_nt(both, k[ab, :, cols]).reshape(n, 2, BLOCK, ROW) + bias[base_u : base_u + n][:, None]
            score = score.reshape(n * 2 * BLOCK, ROW)
            top = jnp.max(score, axis=-1, keepdims=True)
            expo = jnp.exp(score - top)
            total = jnp.sum(expo, axis=-1, keepdims=True)
            p = (expo * (1.0 / total)).astype(BF)
            stat = top + jnp.log(total)
            heads = dot(p, v[ab, :, cols])
            for m, u in enumerate(units):
                even, odd = slice(2 * m * BLOCK, (2 * m + 1) * BLOCK), slice((2 * m + 1) * BLOCK, (2 * m + 2) * BLOCK)
                lse[u] = jnp.where(lane == 2 * j, stat[even], jnp.where(lane == 2 * j + 1, stat[odd], lse[u]))
                att[u, :, cols] = jnp.where(low, heads[even], heads[odd]).astype(BF)
            return carry

        lax.fori_loop(start, stop, pair, 0)

    def out_norm(units):
        base_u, n = units[0], len(units)
        acc[base_u : base_u + n] = dot(att[base_u : base_u + n].reshape(n * BLOCK, D), w_out[...]).reshape(n, BLOCK, D)
        for u in units:
            resid = own_tokens(u).astype(F32) + acc[u] + b_out[...]
            unit, inverse = moments(resid)
            unit1[u] = unit
            inv1[u] = jnp.broadcast_to(inverse, (BLOCK, LANES))
            low1[u] = (unit * gain_first[...] + shift_first[...]).astype(BF)

    lse[...] = jnp.zeros_like(lse)
    project(0)
    attend(0, (0, 1), 0, PAIRS)
    forward_rows(1)
    send_cotangents()
    got_out.wait()
    out_norm((0, 1))
    project(1)
    for copy in forwards:
        copy.wait_send()
    attend(1, (2,), 0, PAIRS)
    out_norm((2,))
    acc[...] = jnp.zeros_like(acc)
    for copy in got_inner + got_outer:
        copy.wait()

    def inner_weight(f):
        return pool[EARLY + f].reshape(D, FFT)

    def outer_weight(f):
        return w_outer[f].reshape(FFT, D)

    def feed(f, carry):
        cols = pl.ds(pl.multiple_of(f * FFT, FFT), FFT)
        pre = dot(low1[...].reshape(tokens, D), inner_weight(f)) + b_inner[0:1, cols]
        half = 0.5 * (1.0 + lax.erf(pre * (1.0 / math.sqrt(2.0))))
        slope[f] = (half + pre * jnp.exp(-0.5 * pre * pre) * (1.0 / math.sqrt(2.0 * math.pi))).astype(BF)
        act_low = (pre * half).astype(BF)
        act[f] = act_low
        acc[...] += dot(act_low, outer_weight(f)).reshape(3, BLOCK, D)
        return carry

    lax.fori_loop(0, FFN, feed, 0)

    for slot in range(3):
        landed(cotq.at[slot], c_recv.at[slot])
    for u in range(3):
        resid = unit1[u] * gain_first[...] + shift_first[...] + acc[u] + b_outer[...]
        unit, inverse = moments(resid)
        up = cotq[u].astype(F32)
        cotq[u] = (unit * gain_second[...] + shift_second[...]).astype(BF)
        d_second = norm_back(up, unit, inverse, gain_second[...])
        d_low = d_second.astype(BF)
        acc[u] = d_second
        d_out[u] = d_low
        vec[5:6] += column_sum(d_low.astype(F32))
        vec[6:7] += column_sum(up * unit)
        vec[7:8] += column_sum(up)

    row_core = jnp.where(z == 3, 1, 0)
    row_slot = lax.rem(z, 3)
    def sent_piece(i, e):
        return 2 * (1 - by) + e if i % 2 else 2 * e + 1 - bx

    def kept_piece(i, e):
        return 2 * by + e if i % 2 else 2 * e + bx

    def second_to(i):
        return to_y if i % 2 else to_x

    def third_to(i):
        return to_x if i % 2 else to_y

    def kept_half(i):
        return bx if i % 2 else by

    def place_in(i):
        return i // 2, 8 * (i % 2)

    def first_send(i):
        chunk, row = place_in(i)
        return remote(pool.at[chunk, pl.ds(row + 4 * (1 - c), 4)], r1.at[i], s1.at[i], t1.at[i], sibling)

    def second_send(i, e):
        return remote(r1.at[i, sent_piece(i, e)], r2.at[i, e], s2.at[i, e], t2.at[i, e], second_to(i))

    def third_send(i):
        return remote(r2.at[i, 1 - kept_half(i)], r3.at[i], s3.at[i], t3.at[i], third_to(i))

    def outer_send(i):
        return remote(r3.at[i], ro.at[i], so.at[i], to.at[i], near)

    def cross_send(i):
        return remote(r3.at[i], rj.at[i], so.at[i], tj.at[i], across)

    def final_near(i):
        return remote(sums.at[i], sums.at[i], sf.at[i], tf.at[i], near)

    def wide(value):
        return value.astype(F32)

    def pair_sum(i, p):
        chunk, row = place_in(i)
        return wide(r1[i, p]) + wide(pool[chunk, row + 4 * c + p])

    def stage2(i):
        landed(r1.at[i], t1.at[i])
        for order in range(2):
            e = lax.rem(1 - kept_half(i) + order, 2)
            p = sent_piece(i, e)
            r1[i, p] = pair_sum(i, p).astype(BF)
            second_send(i, e).start()

    def stage3(i):
        e = 1 - kept_half(i)
        landed(r2.at[i, e], t2.at[i, e])
        r2[i, e] = (wide(r2[i, e]) + pair_sum(i, kept_piece(i, e))).astype(BF)
        third_send(i).start()

    def stage4(i):
        e = kept_half(i)
        landed(r2.at[i, e], t2.at[i, e])
        landed(r3.at[i], t3.at[i])
        r3[i] = (wide(r2[i, e]) + pair_sum(i, kept_piece(i, e)) + wide(r3[i])).astype(BF)

        @pl.when(outer)
        def _():
            outer_send(i).start()

    def stage5(i):
        @pl.when(inner)
        def _():
            landed(ro.at[i], to.at[i])
            r3[i] = (wide(r3[i]) + wide(ro[i])).astype(BF)
            cross_send(i).start()

    def stage6(i):
        @pl.when(inner)
        def _():
            landed(rj.at[i], tj.at[i])
            sums[i] = (wide(r3[i]) + wide(rj[i])).astype(BF)
            final_near(i).start()

    def block_outer(i):
        up = d_out[...].reshape(tokens, D)
        for f in range(FFN):
            g_outer = dot_tn(act[f], up).astype(BF)
            for piece in range(2):
                for part in range(4):
                    for half in range(2):
                        row = 384 * piece + 96 * part + 48 * half
                        pool[part, 8 * half + 4 * piece + f] = g_outer[row : row + 48]
        for n in range(8):
            first_send(n).start()

    def keep_rows(i, grad):
        low_grad = grad.astype(BF)
        for p in range(8):
            for half in range(2):
                row = 96 * p + 48 * half
                pool[i, 8 * half + 4 * (p % 2) + p // 2] = low_grad[row : row + 48]
        for half in range(2):
            first_send(2 * i + half).start()

    def block_feed(f):
        up = d_out[...].reshape(tokens, D)
        d_pre = (dot_nt(up, outer_weight(f)) * slope[f].astype(F32)).astype(BF)
        slope[f] = d_pre
        vec[pl.ds(8 + f, 1)] = column_sum(d_pre.astype(F32))
        acc[...] += dot_nt(d_pre, inner_weight(f)).reshape(3, BLOCK, D)

    def block_inner(f):
        keep_rows(4 + f, dot_tn(low1[...].reshape(tokens, D), slope[f]))

    def block_norm(i):
        for u in range(3):
            up = acc[u]
            d_first = norm_back(up, unit1[u], inv1[u][:, 0:1], gain_first[...])
            acc[u] = d_first
            d_low = d_first.astype(BF)
            d_out[u] = d_low
            vec[2:3] += column_sum(d_low.astype(F32))
            vec[3:4] += column_sum(up * unit1[u])
            vec[4:5] += column_sum(up)
        act[0] = dot_nt(d_out[...].reshape(tokens, D), w_out[...]).astype(BF)

    def block_out(i):
        keep_rows(8, dot_tn(att[...].reshape(tokens, D), d_out[...].reshape(tokens, D)))

    def block_attend(j):
        cols = lanes(j)
        for ab in range(2):
            keys, values = k[ab, :, cols], v[ab, :, cols]
            g_key = g_value = None
            for u in (0, 1) if ab == 0 else (2,):
                q_both = stack_heads(q[u, :, cols], low)
                score = dot_nt(q_both, keys)
                score = (score.reshape(2, BLOCK, ROW) + bias[u][None]).reshape(2 * BLOCK, ROW)
                even = jnp.sum(jnp.where(lane == 2 * j, lse[u], 0.0), axis=-1, keepdims=True)
                odd = jnp.sum(jnp.where(lane == 2 * j + 1, lse[u], 0.0), axis=-1, keepdims=True)
                p = jnp.exp(score - jnp.concatenate([even, odd], axis=0))
                d_pair = act[0, u * BLOCK : (u + 1) * BLOCK, cols]
                d_both = stack_heads(d_pair, low)
                product = wide(d_pair) * wide(att[u, :, cols])
                even = jnp.sum(jnp.where(low, product, 0.0), axis=-1, keepdims=True)
                odd = jnp.sum(jnp.where(low, 0.0, product), axis=-1, keepdims=True)
                d_prob = dot_nt(d_both, values)
                d_score = (p * (d_prob - jnp.concatenate([even, odd], axis=0))).astype(BF)
                one_key = dot(q_both.T, d_score)
                one_value = dot(d_both.T, p.astype(BF))
                g_key = one_key if g_key is None else g_key + one_key
                g_value = one_value if g_value is None else g_value + one_value
                q[u, :, cols] = (merge_heads(dot(d_score, keys), low) * 0.125).astype(BF)
            k[ab, :, cols] = g_key.astype(BF).T
            v[ab, :, cols] = g_value.astype(BF).T

    def block_query(i):
        keep_rows(9, sum(dot_tn(own_tokens(u), q[u]) for u in range(3)))

    def block_key(i):
        keep_rows(10, sum(dot_tn(x[ab].reshape(ROW, D), k[ab]) for ab in range(2)))

    def block_value(i):
        keep_rows(11, sum(dot_tn(x[ab].reshape(ROW, D), v[ab]) for ab in range(2)))

    def share(ab, b):
        rows_b = pl.ds(pl.multiple_of(b * BLOCK, BLOCK), BLOCK)
        return dot_nt(k[ab, rows_b, :], w_key[...]) + dot_nt(v[ab, rows_b, :], w_value[...])

    def swap_send(e):
        src = act.at[1 + e // 2, (e % 2) * BLOCK : (e % 2 + 1) * BLOCK]
        return remote(src, rxa.at[e], xs.at[e], xr.at[e], sibling)

    def block_swap(i):
        for e in range(4):
            b = 2 * (1 - c) + e if e < 2 else 1 - c + 2 * (e - 2)
            act[1 + e // 2, (e % 2) * BLOCK : (e % 2 + 1) * BLOCK] = share(e // 2, b).astype(BF)
            swap_send(e).start()

    class Unit:
        def __init__(self, src, dst, send_sem, recv_sem, to_z, to_c):
            self.here = jnp.logical_and(to_z == z, to_c == c)
            self.away = jnp.logical_not(self.here)
            self.local = pltpu.make_async_copy(src, dst, recv_sem)
            self.out = remote(src, dst, send_sem, recv_sem, at(to_z, base + to_c))

        def start(self):
            @pl.when(self.here)
            def _():
                self.local.start()

            @pl.when(self.away)
            def _():
                self.out.start()

        def finish(self):
            @pl.when(self.away)
            def _():
                self.out.wait_send()

    def layer_unit(u):
        shared = u // 2
        slot = (1 - shared) * row_slot + shared * (1 + deep)
        to_z = (1 - shared) * (2 * c + u) + shared * (2 * lowz + c)
        to_c = (1 - shared) * row_core + shared
        return Unit(cotq.at[u], lay_out.at[slot], lay_s.at[u], lay_r.at[slot], to_z, to_c)

    def grad_unit(n):
        shared = n // 2
        slot = (1 - shared) * row_slot + shared * (1 + deep)
        to_z = (1 - shared) * (2 * c + n) + shared * (c + 2 * lowz)
        to_c = (1 - shared) * row_core + shared
        src = rxa.at[(1 - shared) * n + shared * (2 + lowz)]
        return Unit(src, grad_parts.at[slot], gs.at[n], gr.at[slot], to_z, to_c)

    def pair_send():
        return remote(rxa.at[3 - lowz], rxb, gs.at[2], pr.at[0], at(z + 1 - 2 * lowz, beta))

    def block_layer(u):
        layer_unit(u).start()

    def block_total(n):
        shared = n // 2
        e = lax.rem(n + 1 + lowz, 2)
        at_e = (1 - shared) * n + shared * (2 + e)
        landed(rxa.at[at_e], xr.at[at_e])
        unit1[0] = share(shared, (1 - shared) * (2 * c + n) + shared * (c + 2 * e)) + wide(rxa[at_e])

        @pl.when(n != 2)
        def _():
            u = (1 - shared) * n + shared * 2
            unit1[0] += dot_nt(q[u], w_query[...]) + acc[u]

        @pl.when(n == 3)
        def _():
            landed(rxb, pr.at[0])
            unit1[0] += wide(rxb[...])

        rxa[at_e] = unit1[0].astype(BF)

        @pl.when(n == 2)
        def _():
            pair_send().start()

        @pl.when(n != 2)
        def _():
            grad_unit(n).start()

    def vec_send(i):
        hops = [sibling, to_x, to_y, at(z + 1 - 2 * lowz, beta), at(z + 2 - 4 * deep, beta)]
        return remote(sv.at[i], rv.at[i], vs.at[i], vr.at[i], hops[i])

    def block_vector(i):
        if i == 0:
            sv[0] = vec[...]
            sv[0, 0:1] = sum(column_sum(wide(q[u])) for u in range(3))
            sv[0, 1:2] = sum(column_sum(wide(v[ab])) for ab in range(2))
        else:
            landed(rv.at[i - 1], vr.at[i - 1])
            sv[i] = sv[i - 1] + rv[i - 1]
        vec_send(i).start()

    stages = [stage2, stage3, stage4, stage5, stage6]
    blocks = [
        block_outer,
        block_feed,
        block_norm,
        block_attend,
        block_swap,
        block_total,
        block_inner,
        block_out,
        block_query,
        block_key,
        block_value,
        block_layer,
        block_vector,
    ]
    OPS = stages + blocks
    counts = {kind: 0 for kind in KINDS}

    def emit(kinds):
        for kind in kinds:
            OPS[KINDS.index(kind)](counts[kind])
            counts[kind] += 1

    rest = ORDER
    for kind in LOOPED:
        emit(rest[: rest.index(kind)])
        first_turn, last_turn = rest.index(kind), rest.rindex(kind)
        between = rest[first_turn + 1 : last_turn].split(kind)

        def turn(n, carry, kind=kind, between=between):
            OPS[KINDS.index(kind)](n)
            for at_turn, kinds in enumerate(between):

                @pl.when(n == at_turn)
                def _(kinds=kinds):
                    emit(kinds)

            return carry

        lax.fori_loop(0, len(between) + 1, turn, 0)
        rest = rest[last_turn + 1 :]
    emit(rest)

    writes = []

    def write(src, dst):
        writes.append(pltpu.make_async_copy(src, dst, out_sem.at[len(writes)]))
        writes[-1].start()

    for slot in range(3):
        layer_unit(slot).finish()
        landed(lay_out.at[slot], lay_r.at[slot])
    write(lay_out, lay_hbm)
    for i in range(CHUNKS):
        first_send(i).wait_send()
        for e in range(2):
            second_send(i, e).wait_send()
        third_send(i).wait_send()

        @pl.when(outer)
        def _(i=i):
            outer_send(i).wait_send()
            landed(sums.at[i], tf.at[i])

        @pl.when(inner)
        def _(i=i):
            final_near(i).wait_send()
            cross_send(i).wait_send()

        write(sums.at[i], sums_hbm.at[i])

    landed(rv.at[4], vr.at[4])
    vec[...] = sv[4] + rv[4]
    write(vec, vec_hbm)
    for i in range(5):
        vec_send(i).wait_send()
    for e in range(4):
        swap_send(e).wait_send()
    pair_send().wait_send()
    for n in (0, 1, 3):
        grad_unit(n).finish()
    for slot in range(3):
        landed(grad_parts.at[slot], gr.at[slot])
    write(grad_parts, grad_hbm)
    for copy in writes:
        copy.wait()

    move.finish()


def whole_layer(tokens, segments, cotangent, weights, vectors):
    anywhere = pl.BlockSpec(memory_space=pl.ANY)
    dma = pltpu.SemaphoreType.DMA
    args = (tokens, segments, cotangent) + weights + vectors
    n = CHUNKS
    tok = (3, BLOCK, D)
    square = (16, 48, D)
    buffers = [
        ((n, 48, D), BF),
        (tok, BF),
        (tok, BF),
        ((EARLY + FFN,) + square, BF),
        ((FFN,) + square, BF),
        ((D, D), BF),
        ((D, D), BF),
        ((D, D), BF),
        ((D, D), BF),
        ((8, D), F32),
        ((8, FFN * FFT), F32),
        ((2, 4, 2, 64, D), BF),
        ((2, 4, 8, BLOCK), jnp.int32),
        (tok, BF),
        (tok, BF),
        ((2, ROW, D), BF),
        ((2, ROW, D), BF),
        (tok, BF),
        (tok, BF),
        ((FFN, 3 * BLOCK, FFT), BF),
        ((FFN, 3 * BLOCK, FFT), BF),
        (tok, F32),
        (tok, F32),
        (tok, BF),
        ((3, BLOCK, ROW), F32),
        ((3, BLOCK, LANES), F32),
        ((3, BLOCK, LANES), F32),
        ((16, D), F32),
        ((n, 4, 48, D), BF),
        ((n, 2, 48, D), BF),
        ((n, 48, D), BF),
        ((n, 48, D), BF),
        ((n, 48, D), BF),
        ((4, BLOCK, D), BF),
        ((BLOCK, D), BF),
        ((5, 16, D), F32),
        ((5, 16, D), F32),
    ]
    semaphores = [(21,), (16,), (2, 4, 2), (2, 4), (16,), (2, 4), (6,), (3,)]
    semaphores += [(n,), (n,), (n, 2), (n, 2)] + [(n,)] * 7
    semaphores += [(3,), (3,), (4,), (4,), (4,), (3,), (1,), (5,), (5,), (n + 3,)]
    return pl.pallas_call(
        layer_body,
        out_shape=(
            jax.ShapeDtypeStruct((n, 48, D), BF),
            jax.ShapeDtypeStruct((16, D), F32),
            jax.ShapeDtypeStruct(tok, BF),
            jax.ShapeDtypeStruct(tok, BF),
        ),
        in_specs=[anywhere] * len(args),
        out_specs=[anywhere] * 4,
        scratch_shapes=[pltpu.VMEM(s, t) for s, t in buffers] + [dma(s) for s in semaphores],
        compiler_params=pltpu.CompilerParams(
            collective_id=0, has_side_effects=True, vmem_limit_bytes=int(63.9 * MIB)
        ),
    )(*args)


def finish_body(sums, vec, lay, parts, *outs):
    p = lax.rem(lax.axis_index("batch"), 8)
    layer_out, input_grad, g_q, g_k, g_v, g_o, g_inner, g_outer, b_inner = outs[:9]
    layer_out[...] = lay[...]
    input_grad[...] = parts[...]

    def piece(i):
        return sums[2 * i : 2 * i + 2].reshape(96, D).astype(F32)

    for part in range(4):
        g_outer[96 * part : 96 * part + 96] = piece(part)
    for f in range(FFN):
        g_inner[:, f * FFT : (f + 1) * FFT] = piece(4 + f)
    g_o[...] = piece(8)
    g_q[...] = piece(9)
    g_k[...] = piece(10)
    g_v[...] = piece(11)
    pick = lax.broadcasted_iota(jnp.int32, (D, LANES), 0) == lax.broadcasted_iota(jnp.int32, (D, LANES), 1) + 96 * p
    vecs = jnp.dot(
        vec[0:8], pick.astype(F32), preferred_element_type=F32, precision=lax.Precision.HIGHEST
    )
    for i in range(8):
        outs[9 + i][...] = vecs[i, 0:96]
    quarter = vec[pl.ds(8 + p // 2, 1), :]
    b_inner[...] = jnp.where(lax.rem(p, 2) == 0, quarter[:, :384], quarter[:, 384:]).reshape(384)


def finish(sums, vec, lay, parts):
    vmem = pl.BlockSpec(memory_space=pltpu.VMEM)
    tok = (3, BLOCK, D)
    shapes = [
        (tok, BF),
        (tok, BF),
        ((96, D), F32),
        ((96, D), F32),
        ((96, D), F32),
        ((96, D), F32),
        ((96, 4 * D), F32),
        ((384, D), F32),
        ((384,), F32),
    ] + [((96,), F32)] * 8
    return pl.pallas_call(
        finish_body,
        out_shape=tuple(jax.ShapeDtypeStruct(s, t) for s, t in shapes),
        in_specs=[vmem] * 4,
        out_specs=[vmem] * len(shapes),
        compiler_params=pltpu.CompilerParams(vmem_limit_bytes=60 * MIB),
    )(sums, vec, lay, parts)


def per_device(
    groups,
    tokens,
    segment_ids,
    w_query,
    b_query,
    w_key,
    w_value,
    b_value,
    w_out,
    b_out,
    gain_first,
    shift_first,
    w_inner,
    b_inner,
    w_outer,
    b_outer,
    gain_second,
    shift_second,
    cotangent,
):
    weights = (w_query, w_key, w_value, w_out, w_inner.reshape(16, 48, FFN * FFT), w_outer.reshape(FFN, 16, 48, D))
    vectors = (b_query, b_value, b_out, gain_first, shift_first, b_outer, gain_second, shift_second, b_inner)
    reduced = whole_layer(tokens.reshape(3, 2, 64, D), segment_ids, cotangent, weights, vectors)
    layer_out, input_grad, g_q, g_k, g_v, g_o, g_inner, g_outer, g_b_inner, *vecs = finish(*reduced)
    g_b_query, g_b_value, g_b_out, g_gain_first, g_shift_first, g_b_outer, g_gain_second, g_shift_second = vecs
    grads = (
        g_q,
        g_b_query,
        g_k,
        g_v,
        g_b_value,
        g_o,
        g_b_out,
        g_gain_first,
        g_shift_first,
        g_inner,
        g_b_inner,
        g_outer,
        g_b_outer,
        g_gain_second,
        g_shift_second,
    )
    if groups > 1:
        place_at = lax.rem(lax.axis_index("batch"), 8)

        def spread(grad):
            whole = jnp.zeros((8 * grad.shape[0],) + grad.shape[1:], grad.dtype)
            whole = lax.dynamic_update_slice_in_dim(whole, grad, place_at * grad.shape[0], 0)
            return lax.psum_scatter(whole, "batch", scatter_dimension=0, tiled=True)

        grads = tuple(spread(grad) for grad in grads)
    return (layer_out, input_grad) + grads


def solution(mesh):
    tokens = P("batch", "blk", None)
    weight, vector = P("batch", None), P("batch")
    return jax.shard_map(
        functools.partial(per_device, mesh.shape["batch"] // 8),
        mesh=mesh,
        in_specs=(tokens, P("batch", "blk")) + (P(),) * 15 + (tokens,),
        out_specs=(tokens, tokens)
        + (
            weight,
            vector,
            weight,
            weight,
            vector,
            weight,
            vector,
            vector,
            vector,
            weight,
            vector,
            weight,
            vector,
            vector,
            vector,
        ),
        check_vma=False,
    )
```

```python
import functools
import math

import jax
import jax.numpy as jnp
from jax import lax
from jax.experimental import pallas as pl
from jax.experimental.pallas import tpu as pltpu
from jax.sharding import PartitionSpec as P

BF = jnp.bfloat16
F32 = jnp.float32
EPS = 1e-05
D = 768
PAIRS = 6
LANES = 128
BLOCK = 128
ROW = 512
FFT = 768
FFN = 4
EARLY = 9
CHUNKS = 24
ORDER = "".join(
    (
        "BFYY2Y2F22F3W2F23W33L3242A4A54342A3542W5346A524635A3645A5364",
        "2625X546W4626T36232T5O34q323254T25k263v26534424T6535534V6343",
        "456V2652465463V5654356646545V66V6",
    )
)
KINDS = "23456BFLAXTWOqkvYV"
LOOPED = "FAT"
MIB = 1 << 20


def dot(a, b):
    return jnp.dot(a, b, preferred_element_type=F32)


def dot_nt(a, b):
    return lax.dot_general(a, b, (((1,), (1,)), ((), ())), preferred_element_type=F32)


def dot_tn(a, b):
    return lax.dot_general(a, b, (((0,), (0,)), ((), ())), preferred_element_type=F32)


def place():
    z = lax.axis_index("blk")
    beta = lax.axis_index("batch")
    c = lax.rem(beta, 2)
    return z, beta, c, beta - c


def at(z, beta):
    return {"blk": z, "batch": beta}


def greet(devices):
    barrier = pltpu.get_barrier_semaphore()
    for device in devices:
        pl.semaphore_signal(barrier, inc=1, device_id=device, device_id_type=pl.DeviceIdType.MESH)
    pl.semaphore_wait(barrier, len(devices))


def column_mates(z, c, base):
    mates = [at(lax.rem(z + step, 4), base + core) for step in range(1, 4) for core in range(2)]
    return mates + [at(z, base + 1 - c)]


def remote(src, dst, send_sem, recv_sem, device):
    return pltpu.make_async_remote_copy(
        src_ref=src,
        dst_ref=dst,
        send_sem=send_sem,
        recv_sem=recv_sem,
        device_id=device,
        device_id_type=pl.DeviceIdType.MESH,
    )


class Mover:
    def __init__(self, z, c, base):
        self.z, self.c, self.base, self.sent = z, c, base, []

    def send(self, src, dst, send_sem, recv_sem, to_z, to_c, when=None):
        self_target = jnp.logical_and(to_z == self.z, to_c == self.c)
        other = jnp.logical_not(self_target)
        if when is not None:
            self_target = jnp.logical_and(self_target, when)
            other = jnp.logical_and(other, when)
        out = remote(src, dst, send_sem, recv_sem, at(to_z, self.base + to_c))

        @pl.when(self_target)
        def _():
            pltpu.make_async_copy(src, dst, recv_sem).start()

        @pl.when(other)
        def _():
            out.start()

        self.sent.append((other, out))

    def finish(self):
        for other, out in self.sent:

            @pl.when(other)
            def _(out=out):
                out.wait_send()

        self.sent = []


def landed(dst, sem):
    pltpu.make_async_copy(dst, dst, sem).wait()


def lane_low():
    return lax.broadcasted_iota(jnp.int32, (BLOCK, LANES), 1) < 64


def stack_heads(pair, low):
    zero = jnp.zeros_like(pair)
    return jnp.concatenate([jnp.where(low, pair, zero), jnp.where(low, zero, pair)], axis=0)


def merge_heads(both, low):
    return jnp.where(low, both[:BLOCK], both[BLOCK:])


def moments(resid):
    center = resid - jnp.mean(resid, axis=-1, keepdims=True)
    inverse = lax.rsqrt(jnp.mean(center * center, axis=-1, keepdims=True) + EPS)
    return center * inverse, inverse


def norm_back(upstream, unit, inverse, gain):
    scaled = upstream * gain
    return inverse * (
        scaled
        - jnp.mean(scaled, axis=-1, keepdims=True)
        - unit * jnp.mean(scaled * unit, axis=-1, keepdims=True)
    )


def column_sum(value):
    return jnp.sum(value, axis=0, keepdims=True)


def layer_body(
    tok,
    seg,
    cot,
    w_query_in,
    w_key_in,
    w_value_in,
    w_out_in,
    w_inner_in,
    w_outer_in,
    b_query_in,
    b_value_in,
    b_out_in,
    gain_first_in,
    shift_first_in,
    b_outer_in,
    gain_second_in,
    shift_second_in,
    b_inner_in,
    sums_hbm,
    vec_hbm,
    lay_hbm,
    grad_hbm,
    sums,
    lay_out,
    grad_parts,
    pool,
    w_outer,
    w_query,
    w_key,
    w_value,
    w_out,
    rows,
    b_inner,
    x,
    segs,
    cotq,
    q,
    k,
    v,
    att,
    low1,
    act,
    slope,
    acc,
    unit1,
    d_out,
    bias,
    lse,
    inv1,
    vec,
    r1,
    r2,
    r3,
    ro,
    rj,
    rxa,
    rxb,
    sv,
    rv,
    w_sem,
    d_send,
    d_recv,
    f_send,
    g_send,
    g_recv,
    c_send,
    c_recv,
    s1,
    t1,
    s2,
    t2,
    s3,
    t3,
    so,
    to,
    tj,
    sf,
    tf,
    lay_s,
    lay_r,
    xs,
    xr,
    gs,
    gr,
    pr,
    vs,
    vr,
    out_sem,
):
    z, beta, c, base = place()
    low = lane_low()
    tokens = 3 * BLOCK
    bx, by = lax.rem(beta // 2, 2), lax.rem(beta // 4, 2)
    sibling = at(z, base + 1 - c)
    to_x, to_y = at(z, beta + 2 - 4 * bx), at(z, beta + 4 - 8 * by)
    inner = jnp.logical_and(z > 0, z < 3)
    outer = jnp.logical_not(inner)
    near = at(jnp.where(z < 2, 1 - z, 5 - z), beta)
    across = at(jnp.where(z == 1, 2, 1), beta)
    deep, lowz = z // 2, lax.rem(z, 2)

    loads = []

    def load(src, dst):
        copy = pltpu.make_async_copy(src, dst, w_sem.at[len(loads)])
        copy.start()
        loads.append(copy)
        return copy

    greet(column_mates(z, c, base) + [to_x, to_y])
    move = Mover(z, c, base)
    first, second = c == 0, c == 1
    routes = [(s, 0, s, first) for s in range(3)] + [
        (0, 0, 3, second),
        (1, 1, 0, second),
        (1, 1, 1, second),
        (2, 1, 2, second),
        (2, 1, 3, second),
    ]
    counts = iter(range(16))

    def send_rows(which):
        for slot, ab, chip, when in routes:
            if ab == which:
                for half in range(2):
                    n = next(counts)
                    move.send(
                        tok.at[slot, half], x.at[ab, z, half], d_send.at[n], d_recv.at[ab, z, half], chip, half, when
                    )
                    move.send(seg.at[slot], segs.at[ab, z, 0], g_send.at[n], g_recv.at[ab, z], chip, half, when)

    send_rows(0)
    got_key = load(w_key_in, w_key)
    got_value = load(w_value_in, w_value)
    got_query = load(w_query_in, w_query)
    vectors = [b_query_in, b_value_in, b_out_in, gain_first_in, shift_first_in, b_outer_in, gain_second_in]
    got_rows = [load(ref, rows.at[i]) for i, ref in enumerate(vectors + [shift_second_in])]
    got_rows.append(load(b_inner_in, b_inner.at[0]))
    got_out = load(w_out_in, w_out)
    got_inner = [load(w_inner_in.at[:, :, f * FFT : (f + 1) * FFT], pool.at[EARLY + f]) for f in range(FFN)]
    got_outer = [load(w_outer_in.at[f], w_outer.at[f]) for f in range(FFN)]

    b_query, b_value, b_out, gain_first, shift_first, b_outer, gain_second, shift_second = (
        rows.at[i : i + 1] for i in range(8)
    )
    vec[...] = jnp.zeros_like(vec)
    forwards = []

    def forward_rows(ab, steps=range(4)):
        for step in steps:
            b = (z, z + 1 - 2 * lowz, lax.rem(z + 2, 4), 3 - z)[step]
            landed(x.at[ab, b, c], d_recv.at[ab, b, c])
            copy = remote(x.at[ab, b, c], x.at[ab, b, c], f_send.at[ab, step], d_recv.at[ab, b, c], sibling)
            copy.start()
            forwards.append(copy)

    def send_cotangents():
        for slot in range(3):
            move.send(cot.at[slot], cotq.at[lowz], c_send.at[slot], c_recv.at[lowz], slot, deep, first)
        move.send(cot.at[0], cotq.at[lowz], c_send.at[3], c_recv.at[lowz], 3, deep, second)
        move.send(cot.at[1], cotq.at[2], c_send.at[4], c_recv.at[2], deep, lowz, second)
        move.send(cot.at[2], cotq.at[2], c_send.at[5], c_recv.at[2], 2 + deep, lowz, second)

    forward_rows(0, range(3))
    send_rows(1)
    forward_rows(0, range(3, 4))
    own_blocks = [(0, 2 * c), (0, 2 * c + 1), (1, 2 * lowz + c)]

    def own_tokens(u):
        ab, b = own_blocks[u]
        return x[ab, b].reshape(BLOCK, D)

    def one_hot(row):
        return (lax.broadcasted_iota(jnp.int32, (8, BLOCK), 0) == row).astype(F32)

    got_key.wait()
    got_value.wait()
    got_query.wait()
    for copy in got_rows:
        copy.wait()
    def project(ab):
        for b in range(4):
            landed(x.at[ab, b, 1 - c], d_recv.at[ab, b, 1 - c])
            landed(segs.at[ab, b, 0], g_recv.at[ab, b])
        xk = x[ab].reshape(ROW, D)
        k[ab] = dot(xk, w_key[...]).astype(BF)
        v[ab] = (dot(xk, w_value[...]) + b_value[...]).astype(BF)
        for u, (row, b) in enumerate(own_blocks):
            if row == ab:
                q[u] = ((dot(own_tokens(u), w_query[...]) + b_query[...]).astype(BF) * 0.125).astype(BF)
                own_hot = one_hot(segs[ab, b, 0:1])
                for kb in range(4):
                    same = dot_tn(own_hot, one_hot(segs[ab, kb, 0:1]))
                    bias[u, :, kb * BLOCK : (kb + 1) * BLOCK] = jnp.where(same > 0.5, 0.0, -1e30)

    def lanes(j):
        return pl.ds(pl.multiple_of(j * LANES, LANES), LANES)

    lane = lax.broadcasted_iota(jnp.int32, (BLOCK, LANES), 1)

    def attend(ab, units, start, stop):
        n, base_u = len(units), units[0]

        def pair(j, carry):
            cols = lanes(j)
            both = jnp.concatenate([stack_heads(q[u, :, cols], low) for u in units], axis=0)
            score = dot_nt(both, k[ab, :, cols]).reshape(n, 2, BLOCK, ROW) + bias[base_u : base_u + n][:, None]
            score = score.reshape(n * 2 * BLOCK, ROW)
            top = jnp.max(score, axis=-1, keepdims=True)
            expo = jnp.exp(score - top)
            total = jnp.sum(expo, axis=-1, keepdims=True)
            p = (expo * (1.0 / total)).astype(BF)
            stat = top + jnp.log(total)
            heads = dot(p, v[ab, :, cols])
            for m, u in enumerate(units):
                even, odd = slice(2 * m * BLOCK, (2 * m + 1) * BLOCK), slice((2 * m + 1) * BLOCK, (2 * m + 2) * BLOCK)
                lse[u] = jnp.where(lane == 2 * j, stat[even], jnp.where(lane == 2 * j + 1, stat[odd], lse[u]))
                att[u, :, cols] = jnp.where(low, heads[even], heads[odd]).astype(BF)
            return carry

        lax.fori_loop(start, stop, pair, 0)

    def out_norm(units):
        base_u, n = units[0], len(units)
        acc[base_u : base_u + n] = dot(att[base_u : base_u + n].reshape(n * BLOCK, D), w_out[...]).reshape(n, BLOCK, D)
        for u in units:
            resid = own_tokens(u).astype(F32) + acc[u] + b_out[...]
            unit, inverse = moments(resid)
            unit1[u] = unit
            inv1[u] = jnp.broadcast_to(inverse, (BLOCK, LANES))
            low1[u] = (unit * gain_first[...] + shift_first[...]).astype(BF)

    lse[...] = jnp.zeros_like(lse)
    project(0)
    attend(0, (0, 1), 0, PAIRS)
    forward_rows(1, range(3))
    send_cotangents()
    forward_rows(1, range(3, 4))
    got_out.wait()
    out_norm((0, 1))
    project(1)
    for copy in forwards:
        copy.wait_send()
    attend(1, (2,), 0, PAIRS)
    out_norm((2,))
    acc[...] = jnp.zeros_like(acc)
    for copy in got_inner + got_outer:
        copy.wait()

    def inner_weight(f):
        return pool[EARLY + f].reshape(D, FFT)

    def outer_weight(f):
        return w_outer[f].reshape(FFT, D)

    def feed(f, carry):
        cols = pl.ds(pl.multiple_of(f * FFT, FFT), FFT)
        pre = dot(low1[...].reshape(tokens, D), inner_weight(f)) + b_inner[0:1, cols]
        half = 0.5 * (1.0 + lax.erf(pre * (1.0 / math.sqrt(2.0))))
        slope[f] = (half + pre * jnp.exp(-0.5 * pre * pre) * (1.0 / math.sqrt(2.0 * math.pi))).astype(BF)
        act_low = (pre * half).astype(BF)
        act[f] = act_low
        acc[...] += dot(act_low, outer_weight(f)).reshape(3, BLOCK, D)
        return carry

    lax.fori_loop(0, FFN, feed, 0)

    for slot in range(3):
        landed(cotq.at[slot], c_recv.at[slot])
    for u in range(3):
        resid = unit1[u] * gain_first[...] + shift_first[...] + acc[u] + b_outer[...]
        unit, inverse = moments(resid)
        up = cotq[u].astype(F32)
        cotq[u] = (unit * gain_second[...] + shift_second[...]).astype(BF)
        d_second = norm_back(up, unit, inverse, gain_second[...])
        d_low = d_second.astype(BF)
        acc[u] = d_second
        d_out[u] = d_low
        vec[5:6] += column_sum(d_low.astype(F32))
        vec[6:7] += column_sum(up * unit)
        vec[7:8] += column_sum(up)

    row_core = jnp.where(z == 3, 1, 0)
    row_slot = lax.rem(z, 3)
    def sent_piece(i, e):
        return 2 * (1 - by) + e if i % 2 else 2 * e + 1 - bx

    def kept_piece(i, e):
        return 2 * by + e if i % 2 else 2 * e + bx

    def second_to(i):
        return to_y if i % 2 else to_x

    def third_to(i):
        return to_x if i % 2 else to_y

    def kept_half(i):
        return bx if i % 2 else by

    def place_in(i):
        return i // 2, 8 * (i % 2)

    def first_send(i):
        chunk, row = place_in(i)
        return remote(pool.at[chunk, pl.ds(row + 4 * (1 - c), 4)], r1.at[i], s1.at[i], t1.at[i], sibling)

    def second_send(i, e):
        return remote(r1.at[i, sent_piece(i, e)], r2.at[i, e], s2.at[i, e], t2.at[i, e], second_to(i))

    def third_send(i):
        return remote(r2.at[i, 1 - kept_half(i)], r3.at[i], s3.at[i], t3.at[i], third_to(i))

    def outer_send(i):
        return remote(r3.at[i], ro.at[i], so.at[i], to.at[i], near)

    def cross_send(i):
        return remote(r3.at[i], rj.at[i], so.at[i], tj.at[i], across)

    def final_near(i):
        return remote(sums.at[i], sums.at[i], sf.at[i], tf.at[i], near)

    def wide(value):
        return value.astype(F32)

    def pair_sum(i, p):
        chunk, row = place_in(i)
        return wide(r1[i, p]) + wide(pool[chunk, row + 4 * c + p])

    def stage2(i):
        landed(r1.at[i], t1.at[i])
        for order in range(2):
            e = lax.rem(1 - kept_half(i) + order, 2)
            p = sent_piece(i, e)
            r1[i, p] = pair_sum(i, p).astype(BF)
            second_send(i, e).start()

    def stage3(i):
        e = 1 - kept_half(i)
        landed(r2.at[i, e], t2.at[i, e])
        r2[i, e] = (wide(r2[i, e]) + pair_sum(i, kept_piece(i, e))).astype(BF)
        third_send(i).start()

    def stage4(i):
        e = kept_half(i)
        landed(r2.at[i, e], t2.at[i, e])
        landed(r3.at[i], t3.at[i])
        r3[i] = (wide(r2[i, e]) + pair_sum(i, kept_piece(i, e)) + wide(r3[i])).astype(BF)

        @pl.when(outer)
        def _():
            outer_send(i).start()

    def stage5(i):
        @pl.when(inner)
        def _():
            landed(ro.at[i], to.at[i])
            r3[i] = (wide(r3[i]) + wide(ro[i])).astype(BF)
            cross_send(i).start()

    def stage6(i):
        @pl.when(inner)
        def _():
            landed(rj.at[i], tj.at[i])
            sums[i] = (wide(r3[i]) + wide(rj[i])).astype(BF)
            final_near(i).start()

    def block_outer(i):
        up = d_out[...].reshape(tokens, D)
        for f in range(FFN):
            g_outer = dot_tn(act[f], up).astype(BF)
            for piece in range(2):
                for part in range(4):
                    for half in range(2):
                        row = 384 * piece + 96 * part + 48 * half
                        pool[part, 8 * half + 4 * piece + f] = g_outer[row : row + 48]
        for n in range(8):
            first_send(n).start()

    def keep_rows(i, grad):
        low_grad = grad.astype(BF)
        for p in range(8):
            for half in range(2):
                row = 96 * p + 48 * half
                pool[i, 8 * half + 4 * (p % 2) + p // 2] = low_grad[row : row + 48]
        for half in range(2):
            first_send(2 * i + half).start()

    def block_feed(f):
        up = d_out[...].reshape(tokens, D)
        d_pre = (dot_nt(up, outer_weight(f)) * slope[f].astype(F32)).astype(BF)
        slope[f] = d_pre
        vec[pl.ds(8 + f, 1)] = column_sum(d_pre.astype(F32))
        acc[...] += dot_nt(d_pre, inner_weight(f)).reshape(3, BLOCK, D)

    def block_inner(f):
        keep_rows(4 + f, dot_tn(low1[...].reshape(tokens, D), slope[f]))

    def block_norm(i):
        for u in range(3):
            up = acc[u]
            d_first = norm_back(up, unit1[u], inv1[u][:, 0:1], gain_first[...])
            acc[u] = d_first
            d_low = d_first.astype(BF)
            d_out[u] = d_low
            vec[2:3] += column_sum(d_low.astype(F32))
            vec[3:4] += column_sum(up * unit1[u])
            vec[4:5] += column_sum(up)
        act[0] = dot_nt(d_out[...].reshape(tokens, D), w_out[...]).astype(BF)

    def block_out(i):
        keep_rows(8, dot_tn(att[...].reshape(tokens, D), d_out[...].reshape(tokens, D)))

    def block_attend(j):
        cols = lanes(j)
        for ab in range(2):
            keys, values = k[ab, :, cols], v[ab, :, cols]
            g_key = g_value = None
            for u in (0, 1) if ab == 0 else (2,):
                q_both = stack_heads(q[u, :, cols], low)
                score = dot_nt(q_both, keys)
                score = (score.reshape(2, BLOCK, ROW) + bias[u][None]).reshape(2 * BLOCK, ROW)
                even = jnp.sum(jnp.where(lane == 2 * j, lse[u], 0.0), axis=-1, keepdims=True)
                odd = jnp.sum(jnp.where(lane == 2 * j + 1, lse[u], 0.0), axis=-1, keepdims=True)
                p = jnp.exp(score - jnp.concatenate([even, odd], axis=0))
                d_pair = act[0, u * BLOCK : (u + 1) * BLOCK, cols]
                d_both = stack_heads(d_pair, low)
                product = wide(d_pair) * wide(att[u, :, cols])
                even = jnp.sum(jnp.where(low, product, 0.0), axis=-1, keepdims=True)
                odd = jnp.sum(jnp.where(low, 0.0, product), axis=-1, keepdims=True)
                d_prob = dot_nt(d_both, values)
                d_score = (p * (d_prob - jnp.concatenate([even, odd], axis=0))).astype(BF)
                one_key = dot(q_both.T, d_score)
                one_value = dot(d_both.T, p.astype(BF))
                g_key = one_key if g_key is None else g_key + one_key
                g_value = one_value if g_value is None else g_value + one_value
                q[u, :, cols] = (merge_heads(dot(d_score, keys), low) * 0.125).astype(BF)
            k[ab, :, cols] = g_key.astype(BF).T
            v[ab, :, cols] = g_value.astype(BF).T

    def block_query(i):
        keep_rows(9, sum(dot_tn(own_tokens(u), q[u]) for u in range(3)))

    def block_key(i):
        keep_rows(10, sum(dot_tn(x[ab].reshape(ROW, D), k[ab]) for ab in range(2)))

    def block_value(i):
        keep_rows(11, sum(dot_tn(x[ab].reshape(ROW, D), v[ab]) for ab in range(2)))

    def share(ab, b):
        rows_b = pl.ds(pl.multiple_of(b * BLOCK, BLOCK), BLOCK)
        return dot_nt(k[ab, rows_b, :], w_key[...]) + dot_nt(v[ab, rows_b, :], w_value[...])

    def swap_send(e):
        src = act.at[1 + e // 2, (e % 2) * BLOCK : (e % 2 + 1) * BLOCK]
        return remote(src, rxa.at[e], xs.at[e], xr.at[e], sibling)

    def block_swap(i):
        for e in range(4):
            b = 2 * (1 - c) + e if e < 2 else 1 - c + 2 * (e - 2)
            act[1 + e // 2, (e % 2) * BLOCK : (e % 2 + 1) * BLOCK] = share(e // 2, b).astype(BF)
            swap_send(e).start()

    class Unit:
        def __init__(self, src, dst, send_sem, recv_sem, to_z, to_c):
            self.here = jnp.logical_and(to_z == z, to_c == c)
            self.away = jnp.logical_not(self.here)
            self.local = pltpu.make_async_copy(src, dst, recv_sem)
            self.out = remote(src, dst, send_sem, recv_sem, at(to_z, base + to_c))

        def start(self):
            @pl.when(self.here)
            def _():
                self.local.start()

            @pl.when(self.away)
            def _():
                self.out.start()

        def finish(self):
            @pl.when(self.away)
            def _():
                self.out.wait_send()

    def layer_unit(u):
        shared = u // 2
        slot = (1 - shared) * row_slot + shared * (1 + deep)
        to_z = (1 - shared) * (2 * c + u) + shared * (2 * lowz + c)
        to_c = (1 - shared) * row_core + shared
        return Unit(cotq.at[u], lay_out.at[slot], lay_s.at[u], lay_r.at[slot], to_z, to_c)

    def grad_unit(n):
        shared = n // 2
        slot = (1 - shared) * row_slot + shared * (1 + deep)
        to_z = (1 - shared) * (2 * c + n) + shared * (c + 2 * lowz)
        to_c = (1 - shared) * row_core + shared
        src = rxa.at[(1 - shared) * n + shared * (2 + lowz)]
        return Unit(src, grad_parts.at[slot], gs.at[n], gr.at[slot], to_z, to_c)

    def pair_send():
        return remote(rxa.at[3 - lowz], rxb, gs.at[2], pr.at[0], at(z + 1 - 2 * lowz, beta))

    def block_layer(u):
        layer_unit(u).start()

    def block_total(n):
        shared = n // 2
        e = lax.rem(n + 1 + lowz, 2)
        at_e = (1 - shared) * n + shared * (2 + e)
        landed(rxa.at[at_e], xr.at[at_e])
        unit1[0] = share(shared, (1 - shared) * (2 * c + n) + shared * (c + 2 * e)) + wide(rxa[at_e])

        @pl.when(n != 2)
        def _():
            u = (1 - shared) * n + shared * 2
            unit1[0] += dot_nt(q[u], w_query[...]) + acc[u]

        @pl.when(n == 3)
        def _():
            landed(rxb, pr.at[0])
            unit1[0] += wide(rxb[...])

        rxa[at_e] = unit1[0].astype(BF)

        @pl.when(n == 2)
        def _():
            pair_send().start()

        @pl.when(n != 2)
        def _():
            grad_unit(n).start()

    def vec_send(i):
        hops = [sibling, to_x, to_y, at(z + 1 - 2 * lowz, beta), at(z + 2 - 4 * deep, beta)]
        return remote(sv.at[i], rv.at[i], vs.at[i], vr.at[i], hops[i])

    def block_vector(i):
        if i == 0:
            sv[0] = vec[...]
            sv[0, 0:1] = sum(column_sum(wide(q[u])) for u in range(3))
            sv[0, 1:2] = sum(column_sum(wide(v[ab])) for ab in range(2))
        else:
            landed(rv.at[i - 1], vr.at[i - 1])
            sv[i] = sv[i - 1] + rv[i - 1]
        vec_send(i).start()

    stages = [stage2, stage3, stage4, stage5, stage6]
    blocks = [
        block_outer,
        block_feed,
        block_norm,
        block_attend,
        block_swap,
        block_total,
        block_inner,
        block_out,
        block_query,
        block_key,
        block_value,
        block_layer,
        block_vector,
    ]
    OPS = stages + blocks
    counts = {kind: 0 for kind in KINDS}

    def emit(kinds):
        for kind in kinds:
            OPS[KINDS.index(kind)](counts[kind])
            counts[kind] += 1

    rest = ORDER
    for kind in LOOPED:
        emit(rest[: rest.index(kind)])
        first_turn, last_turn = rest.index(kind), rest.rindex(kind)
        between = rest[first_turn + 1 : last_turn].split(kind)

        def turn(n, carry, kind=kind, between=between):
            OPS[KINDS.index(kind)](n)
            for at_turn, kinds in enumerate(between):

                @pl.when(n == at_turn)
                def _(kinds=kinds):
                    emit(kinds)

            return carry

        lax.fori_loop(0, len(between) + 1, turn, 0)
        rest = rest[last_turn + 1 :]
    emit(rest)

    writes = []

    def write(src, dst):
        writes.append(pltpu.make_async_copy(src, dst, out_sem.at[len(writes)]))
        writes[-1].start()

    for slot in range(3):
        layer_unit(slot).finish()
        landed(lay_out.at[slot], lay_r.at[slot])
    write(lay_out, lay_hbm)
    for i in range(CHUNKS):
        first_send(i).wait_send()
        for e in range(2):
            second_send(i, e).wait_send()
        third_send(i).wait_send()

        @pl.when(outer)
        def _(i=i):
            outer_send(i).wait_send()
            landed(sums.at[i], tf.at[i])

        @pl.when(inner)
        def _(i=i):
            final_near(i).wait_send()
            cross_send(i).wait_send()

        write(sums.at[i], sums_hbm.at[i])

    landed(rv.at[4], vr.at[4])
    vec[...] = sv[4] + rv[4]
    write(vec, vec_hbm)
    for i in range(5):
        vec_send(i).wait_send()
    for e in range(4):
        swap_send(e).wait_send()
    pair_send().wait_send()
    for n in (0, 1, 3):
        grad_unit(n).finish()
    for slot in range(3):
        landed(grad_parts.at[slot], gr.at[slot])
    write(grad_parts, grad_hbm)
    for copy in writes:
        copy.wait()

    move.finish()


def whole_layer(tokens, segments, cotangent, weights, vectors):
    anywhere = pl.BlockSpec(memory_space=pl.ANY)
    dma = pltpu.SemaphoreType.DMA
    args = (tokens, segments, cotangent) + weights + vectors
    n = CHUNKS
    tok = (3, BLOCK, D)
    square = (16, 48, D)
    buffers = [
        ((n, 48, D), BF),
        (tok, BF),
        (tok, BF),
        ((EARLY + FFN,) + square, BF),
        ((FFN,) + square, BF),
        ((D, D), BF),
        ((D, D), BF),
        ((D, D), BF),
        ((D, D), BF),
        ((8, D), F32),
        ((8, FFN * FFT), F32),
        ((2, 4, 2, 64, D), BF),
        ((2, 4, 8, BLOCK), jnp.int32),
        (tok, BF),
        (tok, BF),
        ((2, ROW, D), BF),
        ((2, ROW, D), BF),
        (tok, BF),
        (tok, BF),
        ((FFN, 3 * BLOCK, FFT), BF),
        ((FFN, 3 * BLOCK, FFT), BF),
        (tok, F32),
        (tok, F32),
        (tok, BF),
        ((3, BLOCK, ROW), F32),
        ((3, BLOCK, LANES), F32),
        ((3, BLOCK, LANES), F32),
        ((16, D), F32),
        ((n, 4, 48, D), BF),
        ((n, 2, 48, D), BF),
        ((n, 48, D), BF),
        ((n, 48, D), BF),
        ((n, 48, D), BF),
        ((4, BLOCK, D), BF),
        ((BLOCK, D), BF),
        ((5, 16, D), F32),
        ((5, 16, D), F32),
    ]
    semaphores = [(21,), (16,), (2, 4, 2), (2, 4), (16,), (2, 4), (6,), (3,)]
    semaphores += [(n,), (n,), (n, 2), (n, 2)] + [(n,)] * 7
    semaphores += [(3,), (3,), (4,), (4,), (4,), (3,), (1,), (5,), (5,), (n + 3,)]
    return pl.pallas_call(
        layer_body,
        out_shape=(
            jax.ShapeDtypeStruct((n, 48, D), BF),
            jax.ShapeDtypeStruct((16, D), F32),
            jax.ShapeDtypeStruct(tok, BF),
            jax.ShapeDtypeStruct(tok, BF),
        ),
        in_specs=[anywhere] * len(args),
        out_specs=[anywhere] * 4,
        scratch_shapes=[pltpu.VMEM(s, t) for s, t in buffers] + [dma(s) for s in semaphores],
        compiler_params=pltpu.CompilerParams(
            collective_id=0, has_side_effects=True, vmem_limit_bytes=int(63.9 * MIB)
        ),
    )(*args)


def finish_body(sums, vec, lay, parts, *outs):
    p = lax.rem(lax.axis_index("batch"), 8)
    layer_out, input_grad, g_q, g_k, g_v, g_o, g_inner, g_outer, b_inner = outs[:9]
    layer_out[...] = lay[...]
    input_grad[...] = parts[...]

    def piece(i):
        return sums[2 * i : 2 * i + 2].reshape(96, D).astype(F32)

    for part in range(4):
        g_outer[96 * part : 96 * part + 96] = piece(part)
    for f in range(FFN):
        g_inner[:, f * FFT : (f + 1) * FFT] = piece(4 + f)
    g_o[...] = piece(8)
    g_q[...] = piece(9)
    g_k[...] = piece(10)
    g_v[...] = piece(11)
    pick = lax.broadcasted_iota(jnp.int32, (D, LANES), 0) == lax.broadcasted_iota(jnp.int32, (D, LANES), 1) + 96 * p
    vecs = jnp.dot(
        vec[0:8], pick.astype(F32), preferred_element_type=F32, precision=lax.Precision.HIGHEST
    )
    for i in range(8):
        outs[9 + i][...] = vecs[i, 0:96]
    quarter = vec[pl.ds(8 + p // 2, 1), :]
    b_inner[...] = jnp.where(lax.rem(p, 2) == 0, quarter[:, :384], quarter[:, 384:]).reshape(384)


def finish(sums, vec, lay, parts):
    vmem = pl.BlockSpec(memory_space=pltpu.VMEM)
    tok = (3, BLOCK, D)
    shapes = [
        (tok, BF),
        (tok, BF),
        ((96, D), F32),
        ((96, D), F32),
        ((96, D), F32),
        ((96, D), F32),
        ((96, 4 * D), F32),
        ((384, D), F32),
        ((384,), F32),
    ] + [((96,), F32)] * 8
    return pl.pallas_call(
        finish_body,
        out_shape=tuple(jax.ShapeDtypeStruct(s, t) for s, t in shapes),
        in_specs=[vmem] * 4,
        out_specs=[vmem] * len(shapes),
        compiler_params=pltpu.CompilerParams(vmem_limit_bytes=60 * MIB),
    )(sums, vec, lay, parts)


def per_device(
    groups,
    tokens,
    segment_ids,
    w_query,
    b_query,
    w_key,
    w_value,
    b_value,
    w_out,
    b_out,
    gain_first,
    shift_first,
    w_inner,
    b_inner,
    w_outer,
    b_outer,
    gain_second,
    shift_second,
    cotangent,
):
    weights = (w_query, w_key, w_value, w_out, w_inner.reshape(16, 48, FFN * FFT), w_outer.reshape(FFN, 16, 48, D))
    vectors = (b_query, b_value, b_out, gain_first, shift_first, b_outer, gain_second, shift_second, b_inner)
    reduced = whole_layer(tokens.reshape(3, 2, 64, D), segment_ids, cotangent, weights, vectors)
    layer_out, input_grad, g_q, g_k, g_v, g_o, g_inner, g_outer, g_b_inner, *vecs = finish(*reduced)
    g_b_query, g_b_value, g_b_out, g_gain_first, g_shift_first, g_b_outer, g_gain_second, g_shift_second = vecs
    grads = (
        g_q,
        g_b_query,
        g_k,
        g_v,
        g_b_value,
        g_o,
        g_b_out,
        g_gain_first,
        g_shift_first,
        g_inner,
        g_b_inner,
        g_outer,
        g_b_outer,
        g_gain_second,
        g_shift_second,
    )
    if groups > 1:
        place_at = lax.rem(lax.axis_index("batch"), 8)

        def spread(grad):
            whole = jnp.zeros((8 * grad.shape[0],) + grad.shape[1:], grad.dtype)
            whole = lax.dynamic_update_slice_in_dim(whole, grad, place_at * grad.shape[0], 0)
            return lax.psum_scatter(whole, "batch", scatter_dimension=0, tiled=True)

        grads = tuple(spread(grad) for grad in grads)
    return (layer_out, input_grad) + grads


def solution(mesh):
    tokens = P("batch", "blk", None)
    weight, vector = P("batch", None), P("batch")
    return jax.shard_map(
        functools.partial(per_device, mesh.shape["batch"] // 8),
        mesh=mesh,
        in_specs=(tokens, P("batch", "blk")) + (P(),) * 15 + (tokens,),
        out_specs=(tokens, tokens)
        + (
            weight,
            vector,
            weight,
            weight,
            vector,
            weight,
            vector,
            vector,
            vector,
            weight,
            vector,
            weight,
            vector,
            vector,
            vector,
        ),
        check_vma=False,
    )
```
